256 devices in a mesh: morton: 32 (over y, x, core), sub: 8 (over z).
Axes of the slice: x: 4, y: 4, z: 8, core: 2. Of those that a mesh axis runs over, the one named last changes fastest.
Arguments:
- flow_state: float32 [5, 125, 32768], P(None, None, ('morton', 'sub')), may hold values from -0.65 to 3.75, as said below
- element_level: int32 [32768], P(('morton', 'sub')), may hold values from 0 to 2
- neighbour: int32 [6, 32768], P(None, ('morton', 'sub')), may hold values from -1 to 895, as said below
- send_next: int32 [256, 32], P(('morton', 'sub')), may hold values from 0 to 767
- send_prev: int32 [256, 32], P(('morton', 'sub')), may hold values from 0 to 767
- coarse_face: int32 [256, 8, 2], P(('morton', 'sub')), may hold values from 0 to 767, as said below
- fine_face: int32 [256, 8, 2, 4], P(('morton', 'sub')), may hold values from 0 to 767
- send_count: int32 [256, 8], P(('morton', 'sub')), may hold values from 1 to 2, as said below
Outputs:
- state_out: float32 [5, 125, 32768], P(None, None, ('morton', 'sub'))
- register: float32 [5, 125, 32768], P(None, None, ('morton', 'sub'))
The draws below stay inside these ranges and needn't reach their ends.
Inputs may be any that keep to these rules, and one draw needn't show every extreme that they name: `flow_state`: density lies in 0.7 to 1.3 and the pressure 0.4 (energy - |momentum|^2 / (2 density)) in 0.7 to 1.3 at every node. `neighbour`: an entry is -1 exactly at the slots coarse_face[k, p, j] with j < send_count[k, p]; it equals 6 * 128 + 2 * 32 + 4 (2 p + j) + q exactly at the slots fine_face[k, p, j, q] with j below the count that peer p of the sub group sends to device k; the slots of neighbours 6 * 128 to 831 are each used once; other entries are local slots. Within a device the entries of coarse_face and fine_face are distinct slots, none of them among the slots that read ghost traces. `send_count`: in every group along sub some device receives 2 used slots from every peer.
All inputs are finite; a program needn't handle non-finite values.
Results may differ from the reference program's by a relative error of at most 0.0003.
Values sent between devices are 32-bit elements; how exact they have to be, the bound alone decides.
A program may use at most 64 MiB of HBM per device.

```python
import jax
import jax.numpy as jnp
import numpy as np
from jax import lax

E_DEV = 128
GHOST = 32
CAP = 2
NE = 32768
N_MORTON = 32
N_SUB = 8


def mesh_tables(base_key):
    devices = N_MORTON * N_SUB
    face_slots = 6 * E_DEV
    mortar_slots = N_SUB * CAP
    counts = jax.random.randint(jax.random.fold_in(base_key, 11), (devices, N_SUB), max(1, CAP // 2), CAP + 1)
    busiest = jax.random.randint(jax.random.fold_in(base_key, 12), (N_MORTON,), 0, N_SUB)
    target = jnp.arange(N_SUB)[None, :]
    morton_group = jnp.arange(devices) // N_SUB
    counts = jnp.where(target == busiest[morton_group][:, None], CAP, counts).astype(jnp.int32)
    incoming = counts.reshape(N_MORTON, N_SUB, N_SUB).transpose(0, 2, 1).reshape(devices, N_SUB)

    def per_device(device_key, received_count, sent_count):
        shuffled = jax.random.permutation(jax.random.fold_in(device_key, 1), face_slots).astype(jnp.int32)
        neighbour = jax.random.randint(jax.random.fold_in(device_key, 2), (face_slots,), 0, face_slots)
        neighbour = neighbour.at[shuffled[:GHOST]].set(face_slots + jnp.arange(GHOST))
        neighbour = neighbour.at[shuffled[GHOST:2 * GHOST]].set(face_slots + GHOST + jnp.arange(GHOST))
        fine_slots = shuffled[2 * GHOST:2 * GHOST + 4 * mortar_slots].reshape(N_SUB, CAP, 4)
        slot_rank = jnp.arange(CAP)[None, :]
        fine_used = (slot_rank < received_count[:, None])[:, :, None]
        panel_entry = face_slots + 2 * GHOST + jnp.arange(4 * mortar_slots).reshape(N_SUB, CAP, 4)
        neighbour = neighbour.at[fine_slots].set(jnp.where(fine_used, panel_entry, neighbour[fine_slots]))
        coarse = shuffled[2 * GHOST + 4 * mortar_slots:2 * GHOST + 5 * mortar_slots].reshape(N_SUB, CAP)
        coarse_used = slot_rank < sent_count[:, None]
        neighbour = neighbour.at[coarse].set(jnp.where(coarse_used, -1, neighbour[coarse]))
        next_list = jax.random.randint(jax.random.fold_in(device_key, 3), (GHOST,), 0, face_slots)
        prev_list = jax.random.randint(jax.random.fold_in(device_key, 4), (GHOST,), 0, face_slots)
        return (neighbour.astype(jnp.int32), next_list, prev_list, coarse, fine_slots)
    device_keys = jax.vmap(lambda k: jax.random.fold_in(base_key, 100 + k))(jnp.arange(devices))
    neighbour, next_list, prev_list, coarse, fine_slots = jax.vmap(per_device)(device_keys, incoming, counts)
    return (neighbour, next_list, prev_list, coarse, fine_slots, counts)


def draw_flow_state(key, part):
    uniform_noise = jax.random.uniform(key, (5, 125, E_DEV * N_MORTON * N_SUB), jnp.float32, -1.0, 1.0)
    density = 1.0 + 0.3 * uniform_noise[0]
    velocity = 0.5 * uniform_noise[1:4]
    pressure = 1.0 + 0.3 * uniform_noise[4]
    momenta = density * velocity
    energy = pressure / 0.4 + 0.5 * density * jnp.sum(velocity * velocity, axis=0)
    return jnp.concatenate([density[None], momenta, energy[None]], axis=0).astype(jnp.float32)


def draw_neighbour(key, part):
    devices = N_MORTON * N_SUB
    neighbour = mesh_tables(key)[0]
    return neighbour.reshape(devices, 6, E_DEV).transpose(1, 0, 2).reshape(6, devices * E_DEV)


def draw_send_next(key, part):
    return mesh_tables(key)[1]


def draw_send_prev(key, part):
    return mesh_tables(key)[2]


def draw_coarse_face(key, part):
    return mesh_tables(key)[3]


def draw_fine_face(key, part):
    return mesh_tables(key)[4]


def draw_send_count(key, part):
    return mesh_tables(key)[5]


def touch_ends(entries, rng, low, high):
    shape = entries.shape
    index_at = [jax.random.randint(jax.random.fold_in(rng, axis), (), 0, shape[axis]) for axis in range(len(shape))]
    entries = entries.at[tuple(index_at)].set(low)
    longest = shape.index(max(shape))
    index_at[longest] = (index_at[longest] + 1) % shape[longest]
    return entries.at[tuple(index_at)].set(high)


def setup_inputs(seed: int = 0) -> dict:
    keys = jax.random.split(jax.random.key(seed), 9)
    flow_state = draw_flow_state(jax.random.fold_in(keys[8], 71), 0)
    element_level = touch_ends(jax.random.randint(keys[1], (NE,), 0, 3), jax.random.fold_in(keys[1], 1), 0, 2).astype(jnp.int32)
    neighbour = draw_neighbour(jax.random.fold_in(keys[8], 71), 0)
    send_next = draw_send_next(jax.random.fold_in(keys[8], 71), 0)
    send_prev = draw_send_prev(jax.random.fold_in(keys[8], 71), 0)
    coarse_face = draw_coarse_face(jax.random.fold_in(keys[8], 71), 0)
    fine_face = draw_fine_face(jax.random.fold_in(keys[8], 71), 0)
    send_count = draw_send_count(jax.random.fold_in(keys[8], 71), 0)
    return {"flow_state": flow_state, "element_level": element_level, "neighbour": neighbour, "send_next": send_next, "send_prev": send_prev, "coarse_face": coarse_face, "fine_face": fine_face, "send_count": send_count}


gamma_gas = 1.4
viscosity = 0.01
penalty = 0.1
lift_gain = 10.0
step_size = 0.05
section_a2 = -0.4178904745
section_b1 = 0.1496590219993
section_b2 = 0.3792103129999
highest = lax.Precision.HIGHEST

def basis_tables():
    points = np.array([-1.0, -np.sqrt(3.0 / 7.0), 0.0, np.sqrt(3.0 / 7.0), 1.0])
    weights = np.array([0.1, 49.0 / 90.0, 32.0 / 45.0, 49.0 / 90.0, 0.1])
    products = np.array([np.prod([points[i] - points[m] for m in range(5) if m != i]) for i in range(5)])
    derivative = np.zeros((5, 5))
    for i in range(5):
        for j in range(5):
            if i != j:
                derivative[i, j] = products[i] / (products[j] * (points[i] - points[j]))
        derivative[i, i] = -np.sum(derivative[i])
    halves = []
    projections = []
    for h in range(2):
        shifted = (points + 2.0 * h - 1.0) / 2.0
        interp = np.zeros((5, 5))
        for i in range(5):
            for j in range(5):
                interp[i, j] = np.prod([(shifted[i] - points[m]) / (points[j] - points[m]) for m in range(5) if m != j])
        halves.append(interp)
        projections.append(weights[None, :] * interp.T / (2.0 * weights[:, None]))
    interpolation = np.stack([np.kron(halves[q // 2], halves[q % 2]) for q in range(4)])
    projection = np.stack([np.kron(projections[q // 2], projections[q % 2]) for q in range(4)])
    ident_five = np.eye(5)
    ident_quad = np.eye(25)
    gradients = np.stack([np.kron(derivative, ident_quad), np.kron(ident_five, np.kron(derivative, ident_five)), np.kron(ident_quad, derivative)])
    laplace = gradients[0] @ gradients[0] + gradients[1] @ gradients[1] + gradients[2] @ gradients[2]
    select = np.zeros((6, 25, 125))
    for f in range(6):
        level = 4 * (f % 2)
        for t1 in range(5):
            for t2 in range(5):
                if f // 2 == 0:
                    node = 25 * level + 5 * t1 + t2
                elif f // 2 == 1:
                    node = 25 * t1 + 5 * level + t2
                else:
                    node = 25 * t1 + 5 * t2 + level
                select[f, 5 * t1 + t2, node] = 1.0
    return (jnp.asarray(derivative, jnp.float32), jnp.asarray(interpolation, jnp.float32), jnp.asarray(projection, jnp.float32), jnp.asarray(gradients, jnp.float32), jnp.asarray(laplace, jnp.float32), jnp.asarray(select, jnp.float32))

def euler_flux(fields, d):
    density = fields[0]
    velocity = fields[1 + d] / density
    pressure = (gamma_gas - 1.0) * (fields[4] - 0.5 * (fields[1] * fields[1] + fields[2] * fields[2] + fields[3] * fields[3]) / density)
    components = [fields[1 + d], fields[1] * velocity, fields[2] * velocity, fields[3] * velocity, (fields[4] + pressure) * velocity]
    components[1 + d] = components[1 + d] + pressure
    wave_speed = jnp.abs(velocity) + jnp.sqrt(gamma_gas * pressure / density)
    return (jnp.stack(components), wave_speed)

def apply_nodes(matrix, values):
    batched = jnp.broadcast_to(matrix, (values.shape[0],) + matrix.shape)
    return jnp.einsum('fxn,fne->fxe', batched, values, precision=highest)

def volume_rate(fields, metric, gradients, laplace):
    advect = jnp.zeros_like(fields)
    for d in range(3):
        flux_d, unused = euler_flux(fields, d)
        advect = advect + apply_nodes(gradients[d], flux_d)
    diffuse = apply_nodes(laplace, fields)
    return metric * (viscosity * metric * diffuse - advect)

def face_traces(fields, select):
    return jnp.concatenate([apply_nodes(select[f], fields) for f in range(6)], axis=2)

def face_terms(traces, lookup, neighbour, metric):
    elements = metric.shape[0]
    outside_all = jnp.take(lookup, jnp.maximum(neighbour, 0), axis=2)
    normals = []
    numerics = []
    surfaces = []
    for f in range(6):
        orient = 1.0 if f % 2 else -1.0
        inside = traces[:, :, f * elements:(f + 1) * elements]
        outside = outside_all[:, :, f * elements:(f + 1) * elements]
        flux_in, speed_in = euler_flux(inside, f // 2)
        flux_out, speed_out = euler_flux(outside, f // 2)
        damping = 0.5 * jnp.maximum(speed_in, speed_out) + penalty * metric
        numeric = 0.5 * orient * (flux_in + flux_out) + damping * (inside - outside)
        coupled = neighbour[f * elements:(f + 1) * elements] >= 0
        normals.append(orient * flux_in)
        numerics.append(numeric)
        surfaces.append(jnp.where(coupled, orient * flux_in - numeric, 0.0))
    return (jnp.concatenate(normals, axis=2), jnp.concatenate(numerics, axis=2), jnp.concatenate(surfaces, axis=2))

def lift_faces(rate_nodes, surfaces, metric, select):
    elements = metric.shape[0]
    for f in range(6):
        face_block = lift_gain * metric * surfaces[:, :, f * elements:(f + 1) * elements]
        rate_nodes = rate_nodes + apply_nodes(jnp.transpose(select[f]), face_block)
    return rate_nodes

def interpolate_panels(received, interpolation):
    panels = jnp.einsum('qus,fspj->fupjq', interpolation, received, precision=highest)
    return panels.reshape(5, 25, -1)

def project_panels(fine_fluxes, projection):
    return -jnp.einsum('qsu,fupjq->fspj', projection, fine_fluxes, precision=highest)

def coarse_terms(own_flux, returned, send_count):
    usable = jnp.arange(own_flux.shape[3])[None, :] < send_count[:, None]
    return jnp.where(usable, own_flux - returned, 0.0)

def swap_groups(pieces):
    layout = pieces.shape
    grouped = pieces.reshape((N_MORTON, N_SUB) + layout[1:])
    return jnp.swapaxes(grouped, 1, 4).reshape(layout)

def evaluate(states, metric, connection, tables):
    neighbour, send_next, send_prev, coarse_face, fine_face, send_count = connection
    derivative, interpolation, projection, gradients, laplace, select = tables
    elements = states.shape[-1]

    def outbound(inputs):
        fields, next_list, prev_list, coarse = inputs
        traces = face_traces(fields, select)
        return (jnp.take(traces, next_list, axis=2), jnp.take(traces, prev_list, axis=2), jnp.take(traces, coarse, axis=2))
    to_next, to_prev, outgoing = lax.map(outbound, (states, send_next, send_prev, coarse_face))
    from_prev = jnp.roll(to_next, 1, axis=0)
    from_next = jnp.roll(to_prev, -1, axis=0)
    received = swap_groups(outgoing)

    def interior(inputs):
        fields, scale_row, neighbours, prev_in, next_in, incoming, coarse, fine_list = inputs
        traces = face_traces(fields, select)
        lookup = jnp.concatenate([traces, prev_in, next_in, interpolate_panels(incoming, interpolation)], axis=2)
        normals, numerics, surfaces = face_terms(traces, lookup, neighbours, scale_row)
        rate_part = lift_faces(volume_rate(fields, scale_row, gradients, laplace), surfaces, scale_row, select)
        projected = project_panels(jnp.take(numerics, fine_list, axis=2), projection)
        return (rate_part, projected, jnp.take(normals, coarse, axis=2))
    rate_part, projected, own_flux = lax.map(interior, (states, metric, neighbour, from_prev, from_next, received, coarse_face, fine_face))
    returned = swap_groups(projected)

    def finish(inputs):
        rate_row, scale_row, own_row, back_row, coarse, counts = inputs
        coarse_part = coarse_terms(own_row, back_row, counts)
        surfaces = jnp.zeros((5, 25, 6 * elements), jnp.float32).at[:, :, coarse.reshape(-1)].add(coarse_part.reshape(5, 25, -1))
        lifted = lift_faces(jnp.zeros((5, 125, elements), jnp.float32), surfaces, scale_row, select)
        return rate_row + lifted
    return lax.map(finish, (rate_part, metric, own_flux, returned, coarse_face, send_count))

def reference(flow_state, element_level, neighbour, send_next, send_prev, coarse_face, fine_face, send_count):
    devices = N_MORTON * N_SUB
    tables = basis_tables()
    states = flow_state.reshape(5, 125, devices, E_DEV).transpose(2, 0, 1, 3)
    metric = (0.25 * jnp.left_shift(jnp.ones_like(element_level), element_level).astype(jnp.float32)).reshape(devices, E_DEV)
    neighbours = neighbour.reshape(6, devices, E_DEV).transpose(1, 0, 2).reshape(devices, 6 * E_DEV)
    connection = (neighbours, send_next, send_prev, coarse_face, fine_face, send_count)
    first_section = step_size * evaluate(states, metric, connection, tables)
    middle = states + section_b1 * first_section
    register = section_a2 * first_section + step_size * evaluate(middle, metric, connection, tables)
    state_out = middle + section_b2 * register
    state_out = state_out.transpose(1, 2, 0, 3).reshape(5, 125, devices * E_DEV)
    register = register.transpose(1, 2, 0, 3).reshape(5, 125, devices * E_DEV)
    return (state_out, register)
```

```python
import functools

import jax
import jax.numpy as jnp
import numpy as np
from jax import lax
from jax.experimental import pallas as pl
from jax.experimental.pallas import tpu as pltpu
from jax.sharding import PartitionSpec as P

gamma_gas = 1.4
viscosity = 0.01
penalty = 0.1
lift_gain = 10.0
step_size = 0.05
section_a2 = -0.4178904745
section_b1 = 0.1496590219993
section_b2 = 0.3792103129999
MESH = pl.DeviceIdType.MESH
f32 = jnp.float32
bf16 = jnp.bfloat16


def basis_tables():
    points = np.array([-1.0, -np.sqrt(3.0 / 7.0), 0.0, np.sqrt(3.0 / 7.0), 1.0])
    weights = np.array([0.1, 49.0 / 90.0, 32.0 / 45.0, 49.0 / 90.0, 0.1])
    products = np.array(
        [np.prod([points[i] - points[m] for m in range(5) if m != i]) for i in range(5)]
    )
    derivative = np.zeros((5, 5))
    for i in range(5):
        for j in range(5):
            if i != j:
                derivative[i, j] = products[i] / (products[j] * (points[i] - points[j]))
        derivative[i, i] = -np.sum(derivative[i])
    halves = []
    projections = []
    for h in range(2):
        shifted = (points + 2.0 * h - 1.0) / 2.0
        interp = np.zeros((5, 5))
        for i in range(5):
            for j in range(5):
                interp[i, j] = np.prod(
                    [(shifted[i] - points[m]) / (points[j] - points[m]) for m in range(5) if m != j]
                )
        halves.append(interp)
        projections.append(weights[None, :] * interp.T / (2.0 * weights[:, None]))
    interpolation = np.stack([np.kron(halves[q // 2], halves[q % 2]) for q in range(4)])
    projection = np.stack([np.kron(projections[q // 2], projections[q % 2]) for q in range(4)])
    ident_five = np.eye(5)
    ident_quad = np.eye(25)
    gradients = np.stack(
        [
            np.kron(derivative, ident_quad),
            np.kron(ident_five, np.kron(derivative, ident_five)),
            np.kron(ident_quad, derivative),
        ]
    )
    laplace = (
        gradients[0] @ gradients[0] + gradients[1] @ gradients[1] + gradients[2] @ gradients[2]
    )
    return interpolation, projection, gradients, laplace


def two_parts(table):
    table = table.astype(np.float32)
    high = table.astype(jnp.bfloat16)
    low = (table - high.astype(np.float32)).astype(jnp.bfloat16)
    return np.stack([high, low])


def operator_tables():
    interpolation, projection, gradients, laplace = basis_tables()
    volume = np.zeros((128, 512))
    for d in range(3):
        volume[:125, 128 * d : 128 * d + 125] = -gradients[d]
    volume[:125, 384:509] = laplace
    panel = np.zeros((128, 512))
    gather = np.zeros((512, 128))
    for q in range(4):
        for f in range(5):
            rows = slice(25 * f, 25 * f + 25)
            columns = slice(128 * q + 25 * f, 128 * q + 25 * f + 25)
            panel[rows, columns] = interpolation[q].T
            gather[columns, rows] = projection[q].T
    return two_parts(volume).reshape(256, 512), two_parts(panel), two_parts(gather)


def split(x):
    high = x.astype(bf16)
    low = (x - high.astype(f32)).astype(bf16)
    return high, low


def dot(a, b):
    return jnp.dot(a, b, preferred_element_type=f32)


def gas_state(fields):
    inverse = 1.0 / fields[0]
    kinetic = fields[1] * fields[1] + fields[2] * fields[2] + fields[3] * fields[3]
    pressure = (gamma_gas - 1.0) * (fields[4] - 0.5 * kinetic * inverse)
    return inverse, pressure


def flux_along(fields, d, inverse, pressure):
    velocity = fields[1 + d] * inverse
    components = [
        fields[1 + d],
        fields[1] * velocity,
        fields[2] * velocity,
        fields[3] * velocity,
        (fields[4] + pressure) * velocity,
    ]
    components[1 + d] = components[1 + d] + pressure
    return components, velocity


def sound_speed(inverse, pressure):
    return jnp.sqrt(gamma_gas * pressure * inverse)


def kernel(
    n_morton,
    n_sub,
    state_ref,
    level_ref,
    near_ref,
    next_ref,
    prev_ref,
    coarse_ref,
    fine_ref,
    count_ref,
    volume_ref,
    panel_ref,
    gather_ref,
    out_ref,
    register_ref,
    x_ref,
    rate_ref,
    first_ref,
    face_ref,
    face_bf_ref,
    rows_ref,
    pick_ref,
    spread_ref,
    outside_ref,
    added_ref,
    flux_high_ref,
    flux_low_ref,
    mortar_ref,
    numeric_ref,
    ring_send,
    ring_recv,
    message_send,
    message_recv,
    send_sem,
    recv_sem,
):
    m = lax.axis_index("morton")
    s = lax.axis_index("sub")
    devices = n_morton * n_sub
    place = m * n_sub + s
    after = lax.rem(place + 1, devices)
    before = lax.rem(place + devices - 1, devices)
    after_id = (after // n_sub, lax.rem(after, n_sub))
    before_id = (before // n_sub, lax.rem(before, n_sub))
    peers = [lax.rem(s + o, n_sub) for o in range(n_sub)]

    barrier = pltpu.get_barrier_semaphore()
    for o in range(1, n_sub):
        pl.semaphore_signal(barrier, inc=1, device_id=(m, peers[o]), device_id_type=MESH)
    for target in (after_id, before_id):
        pl.semaphore_signal(barrier, inc=1, device_id=target, device_id_type=MESH)

    level = level_ref[...]
    metric = 0.25 * jnp.left_shift(jnp.ones_like(level), level).astype(f32)
    near = near_ref[...]
    extra = near - 832
    panel_lane = 832 + (extra & 3) * 16 + ((extra >> 2) & 1) * 8 + (extra >> 3)
    entry = jnp.where(near >= 832, panel_lane, near)

    for f in range(5):
        x_ref[f, 0:125, :] = state_ref[f]
        x_ref[f, 125:128, :] = jnp.ones((3, 128), f32)
    row_ids = lax.broadcasted_iota(jnp.int32, (128, 128), 0)
    for face in range(6):
        face_ref[face, 125:126, :] = jnp.full((1, 128), float(face // 2), f32)
        face_ref[face, 126:127, :] = metric
        face_ref[face, 127:128, :] = jnp.full((1, 128), 1.0 if face % 2 else -1.0, f32)
    numeric_ref[125:128, :] = jnp.zeros((3, 128), f32)

    def section(step):
        for face in range(6):
            level_at = 4 * (face % 2)
            for f in range(5):
                base = 25 * f
                if face < 2:
                    face_ref[face, base : base + 25, :] = x_ref[f, 25 * level_at : 25 * level_at + 25, :]
                elif face < 4:
                    for a in range(5):
                        start = 25 * a + 5 * level_at
                        face_ref[face, base + 5 * a : base + 5 * a + 5, :] = x_ref[f, start : start + 5, :]
                else:
                    face_ref[face, base : base + 25, :] = x_ref[f, pl.ds(level_at, 25, stride=5), :]
        for face in range(6):
            rows_ref[128 * face : 128 * face + 128, :] = face_ref[face].T

        if step == 0:
            pl.semaphore_wait(barrier, n_sub + 1)
        copies = []
        for p in range(n_sub):
            for j in range(2):
                for q in range(4):
                    message_send[step, p, 4 * j + q : 4 * j + q + 1, :] = rows_ref[
                        pl.ds(fine_ref[0, p, j, q], 1), :
                    ]
                message_send[step, p, 8 + j : 9 + j, :] = rows_ref[pl.ds(coarse_ref[0, p, j], 1), :]
        for o in (4, 3, 5, 2, 6, 1, 7):
            copy = pltpu.make_async_remote_copy(
                src_ref=message_send.at[step, peers[o]],
                dst_ref=message_recv.at[step, s],
                send_sem=send_sem.at[step, o],
                recv_sem=recv_sem.at[step, o],
                device_id=(m, peers[o]),
                device_id_type=MESH,
            )
            copy.start()
            copies.append(copy)
        for side, (list_ref, target) in enumerate(((next_ref, after_id), (prev_ref, before_id))):
            for i in range(32):
                ring_send[step, side, i : i + 1, :] = rows_ref[pl.ds(list_ref[0, i], 1), :]
            copy = pltpu.make_async_remote_copy(
                src_ref=ring_send.at[step, side],
                dst_ref=ring_recv.at[step, side],
                send_sem=send_sem.at[step, n_sub + side],
                recv_sem=recv_sem.at[step, n_sub + side],
                device_id=target,
                device_id_type=MESH,
            )
            copy.start()
            copies.append(copy)
        message_recv[step, s] = message_send[step, s]

        fields = [x_ref[f] for f in range(5)]
        inverse, pressure = gas_state(fields)
        for d in range(3):
            components, unused = flux_along(fields, d, inverse, pressure)
            for f in range(5):
                high, low = split(components[f])
                flux_high_ref[128 * d : 128 * d + 128, 128 * f : 128 * f + 128] = high
                flux_low_ref[128 * d : 128 * d + 128, 128 * f : 128 * f + 128] = low
        for f in range(5):
            high, low = split(viscosity * metric * fields[f])
            flux_high_ref[384:512, 128 * f : 128 * f + 128] = high
            flux_low_ref[384:512, 128 * f : 128 * f + 128] = low
        both = dot(volume_ref[...], flux_high_ref[...])
        total = both[0:128] + both[128:256] + dot(volume_ref[0:128, :], flux_low_ref[...])
        for f in range(5):
            rate_ref[f] = metric * total[:, 128 * f : 128 * f + 128]

        if step == 0:
            for face in range(6):
                wanted = entry[face : face + 1, :]
                for block in range(7):
                    hit = (row_ids + 128 * block) == wanted
                    pick_ref[128 * block : 128 * block + 128, 128 * face : 128 * face + 128] = jnp.where(
                        hit, 1.0, 0.0
                    ).astype(bf16)
            small_rows = lax.broadcasted_iota(jnp.int32, (16, 128), 0)
            small_lanes = lax.broadcasted_iota(jnp.int32, (16, 128), 1)
            owner = jnp.full((16, 128), -1, jnp.int32)
            for j in range(2):
                for p in range(n_sub):
                    slot = jnp.where(j < count_ref[0, p], coarse_ref[0, p, j], -1)
                    owner = jnp.where(small_rows == 8 * j + p, slot, owner)
            for face in range(6):
                spread_ref[:, 128 * face : 128 * face + 128] = jnp.where(
                    owner == small_lanes + 128 * face, 1.0, 0.0
                ).astype(bf16)
            owners.append(owner)
        for face in range(6):
            high, low = split(face_ref[face])
            face_bf_ref[0:128, 128 * face : 128 * face + 128] = high
            face_bf_ref[128:256, 128 * face : 128 * face + 128] = low
        local = dot(face_bf_ref[...], pick_ref[0:768, :])
        local = local[0:128] + local[128:256]
        for face in range(6):
            outside_ref[face] = local[:, 128 * face : 128 * face + 128]

        def panels_of(source):
            coarse_rows = jnp.concatenate(
                [source[step, :, 8 + j, :] for j in range(2)], axis=0
            )
            high, low = split(coarse_rows)
            wide = dot(high, panel_ref[0]) + dot(low, panel_ref[0]) + dot(high, panel_ref[1])
            return [wide[:, 128 * q : 128 * q + 128] for q in range(4)]

        own_panels = panels_of(message_send)

        for copy in copies:
            copy.wait_recv()

        arrived = jnp.concatenate(
            [ring_recv[step, 0], ring_recv[step, 1]] + panels_of(message_recv), axis=0
        ).T
        high, low = split(arrived)
        remote = dot(jnp.concatenate([high, low], axis=0), pick_ref[768:896, :])
        remote = remote[0:128] + remote[128:256]
        for face in range(6):
            outside_ref[face] = outside_ref[face] + remote[:, 128 * face : 128 * face + 128]

        fine_rows = [
            message_recv[step, :, 4 * j + q, :] for q in range(4) for j in range(2)
        ]
        mortar_ref[...] = jnp.concatenate(fine_rows + own_panels, axis=0).T
        left = lax.broadcasted_iota(jnp.int32, (1, 128), 1) < 64

        def across(x):
            return pltpu.roll(x, 64, 1)

        facts = [mortar_ref[125 + i : 126 + i, :] for i in range(3)]
        facts = [jnp.where(left, x, across(x)) for x in facts]
        along, mortar_metric, orient = facts
        sides = [mortar_ref[25 * f : 25 * f + 25, :] for f in range(5)]
        inverse, pressure = gas_state(sides)
        normal = jnp.where(along < 0.5, sides[1], jnp.where(along < 1.5, sides[2], sides[3]))
        velocity = normal * inverse
        speed = jnp.abs(velocity) + sound_speed(inverse, pressure)
        components = [
            normal,
            sides[1] * velocity + jnp.where(along < 0.5, pressure, 0.0),
            sides[2] * velocity + jnp.where((along > 0.5) & (along < 1.5), pressure, 0.0),
            sides[3] * velocity + jnp.where(along > 1.5, pressure, 0.0),
            (sides[4] + pressure) * velocity,
        ]
        damping = 0.5 * jnp.maximum(speed, across(speed)) + penalty * mortar_metric
        for f in range(5):
            numeric_ref[25 * f : 25 * f + 25, :] = 0.5 * orient * (
                components[f] + across(components[f])
            ) + damping * (sides[f] - across(sides[f]))
        numeric = numeric_ref[...].T
        wide = jnp.concatenate([numeric[16 * q : 16 * q + 16, :] for q in range(4)], axis=1)
        high, low = split(wide)
        projected = dot(high, gather_ref[0]) + dot(low, gather_ref[0]) + dot(high, gather_ref[1])
        projected = jnp.where(owners[0] >= 0, projected, 0.0).T
        high, low = split(projected)
        added = dot(jnp.concatenate([high, low], axis=0), spread_ref[...])
        added = added[0:128] + added[128:256]
        for face in range(6):
            added_ref[face] = added[:, 128 * face : 128 * face + 128]

        gain = lift_gain * metric
        for face in range(6):
            d = face // 2
            orient_here = 1.0 if face % 2 else -1.0
            inside = [face_ref[face, 25 * f : 25 * f + 25, :] for f in range(5)]
            beyond = [outside_ref[face, 25 * f : 25 * f + 25, :] for f in range(5)]
            coupled = near[face : face + 1, :] >= 0
            beyond = [jnp.where(coupled, b, i) for b, i in zip(beyond, inside)]
            inverse, pressure = gas_state(inside)
            flux_in, velocity = flux_along(inside, d, inverse, pressure)
            speed_in = jnp.abs(velocity) + sound_speed(inverse, pressure)
            inverse, pressure = gas_state(beyond)
            flux_out, velocity = flux_along(beyond, d, inverse, pressure)
            speed_out = jnp.abs(velocity) + sound_speed(inverse, pressure)
            damping = 0.5 * jnp.maximum(speed_in, speed_out) + penalty * metric
            level_at = 4 * (face % 2)
            for f in range(5):
                numeric_here = 0.5 * orient_here * (flux_in[f] + flux_out[f]) + damping * (
                    inside[f] - beyond[f]
                )
                surface = orient_here * flux_in[f] - jnp.where(coupled, numeric_here, 0.0)
                lifted = gain * (surface + added_ref[face, 25 * f : 25 * f + 25, :])
                if face < 2:
                    rows = slice(25 * level_at, 25 * level_at + 25)
                    rate_ref[f, rows, :] = rate_ref[f, rows, :] + lifted
                elif face < 4:
                    for a in range(5):
                        start = 25 * a + 5 * level_at
                        rows = slice(start, start + 5)
                        rate_ref[f, rows, :] = rate_ref[f, rows, :] + lifted[5 * a : 5 * a + 5, :]
                else:
                    rows = pl.ds(level_at, 25, stride=5)
                    rate_ref[f, rows, :] = rate_ref[f, rows, :] + lifted
        return copies

    owners = []
    copies = section(0)
    for f in range(5):
        first = step_size * rate_ref[f]
        first_ref[f] = section_a2 * first
        x_ref[f] = x_ref[f] + section_b1 * first
    copies = copies + section(1)
    for f in range(5):
        register = first_ref[f] + step_size * rate_ref[f]
        out = x_ref[f] + section_b2 * register
        register_ref[f] = register[0:125]
        out_ref[f] = out[0:125]
    for copy in copies:
        copy.wait_send()


def per_device(mesh_shape, flow_state, element_level, neighbour, send_next, send_prev, coarse_face, fine_face, send_count):
    n_morton, n_sub = mesh_shape
    volume, panel, gather = (jnp.asarray(t) for t in operator_tables())
    vmem = pl.BlockSpec(memory_space=pltpu.VMEM)
    smem = pl.BlockSpec(memory_space=pltpu.SMEM)
    shape = jax.ShapeDtypeStruct(flow_state.shape, f32)
    return pl.pallas_call(
        functools.partial(kernel, n_morton, n_sub),
        out_shape=(shape, shape),
        in_specs=[vmem, vmem, vmem, smem, smem, smem, smem, smem, vmem, vmem, vmem],
        out_specs=(vmem, vmem),
        scratch_shapes=[
            pltpu.VMEM((5, 128, 128), f32),
            pltpu.VMEM((5, 128, 128), f32),
            pltpu.VMEM((5, 128, 128), f32),
            pltpu.VMEM((6, 128, 128), f32),
            pltpu.VMEM((256, 768), bf16),
            pltpu.VMEM((768, 128), f32),
            pltpu.VMEM((896, 768), bf16),
            pltpu.VMEM((16, 768), bf16),
            pltpu.VMEM((6, 128, 128), f32),
            pltpu.VMEM((6, 128, 128), f32),
            pltpu.VMEM((512, 640), bf16),
            pltpu.VMEM((512, 640), bf16),
            pltpu.VMEM((128, 128), f32),
            pltpu.VMEM((128, 128), f32),
            pltpu.VMEM((2, 2, 32, 128), f32),
            pltpu.VMEM((2, 2, 32, 128), f32),
            pltpu.VMEM((2, n_sub, 10, 128), f32),
            pltpu.VMEM((2, n_sub, 10, 128), f32),
            pltpu.SemaphoreType.DMA((2, n_sub + 2)),
            pltpu.SemaphoreType.DMA((2, n_sub + 2)),
        ],
        compiler_params=pltpu.CompilerParams(
            collective_id=0, has_side_effects=True, vmem_limit_bytes=48 * 1024 * 1024
        ),
    )(
        flow_state,
        element_level.reshape(1, -1),
        neighbour,
        send_next,
        send_prev,
        coarse_face,
        fine_face,
        send_count,
        volume,
        panel,
        gather,
    )


def solution(mesh):
    whole = ("morton", "sub")
    placed = (
        P(None, None, whole),
        P(whole),
        P(None, whole),
        P(whole, None),
        P(whole, None),
        P(whole, None, None),
        P(whole, None, None, None),
        P(whole, None),
    )
    mesh_shape = (mesh.shape["morton"], mesh.shape["sub"])
    return jax.shard_map(
        functools.partial(per_device, mesh_shape),
        mesh=mesh,
        in_specs=placed,
        out_specs=(P(None, None, whole), P(None, None, whole)),
        check_vma=False,
    )
```

```python
import functools

import jax
import jax.numpy as jnp
import numpy as np
from jax import lax
from jax.experimental import pallas as pl
from jax.experimental.pallas import tpu as pltpu
from jax.sharding import PartitionSpec as P

gamma_gas = 1.4
viscosity = 0.01
penalty = 0.1
lift_gain = 10.0
step_size = 0.05
section_a2 = -0.4178904745
section_b1 = 0.1496590219993
section_b2 = 0.3792103129999
MESH = pl.DeviceIdType.MESH
f32 = jnp.float32
bf16 = jnp.bfloat16


def basis_tables():
    points = np.array([-1.0, -np.sqrt(3.0 / 7.0), 0.0, np.sqrt(3.0 / 7.0), 1.0])
    weights = np.array([0.1, 49.0 / 90.0, 32.0 / 45.0, 49.0 / 90.0, 0.1])
    products = np.array(
        [np.prod([points[i] - points[m] for m in range(5) if m != i]) for i in range(5)]
    )
    derivative = np.zeros((5, 5))
    for i in range(5):
        for j in range(5):
            if i != j:
                derivative[i, j] = products[i] / (products[j] * (points[i] - points[j]))
        derivative[i, i] = -np.sum(derivative[i])
    halves = []
    projections = []
    for h in range(2):
        shifted = (points + 2.0 * h - 1.0) / 2.0
        interp = np.zeros((5, 5))
        for i in range(5):
            for j in range(5):
                interp[i, j] = np.prod(
                    [(shifted[i] - points[m]) / (points[j] - points[m]) for m in range(5) if m != j]
                )
        halves.append(interp)
        projections.append(weights[None, :] * interp.T / (2.0 * weights[:, None]))
    interpolation = np.stack([np.kron(halves[q // 2], halves[q % 2]) for q in range(4)])
    projection = np.stack([np.kron(projections[q // 2], projections[q % 2]) for q in range(4)])
    ident_five = np.eye(5)
    ident_quad = np.eye(25)
    gradients = np.stack(
        [
            np.kron(derivative, ident_quad),
            np.kron(ident_five, np.kron(derivative, ident_five)),
            np.kron(ident_quad, derivative),
        ]
    )
    laplace = (
        gradients[0] @ gradients[0] + gradients[1] @ gradients[1] + gradients[2] @ gradients[2]
    )
    return interpolation, projection, gradients, laplace


def two_parts(table):
    table = table.astype(np.float32)
    high = table.astype(jnp.bfloat16)
    low = (table - high.astype(np.float32)).astype(jnp.bfloat16)
    return np.stack([high, low])


def operator_tables():
    interpolation, projection, gradients, laplace = basis_tables()
    volume = np.zeros((128, 512))
    for d in range(3):
        volume[:125, 128 * d : 128 * d + 125] = -gradients[d]
    volume[:125, 384:509] = laplace
    panel = np.zeros((128, 512))
    gather = np.zeros((512, 128))
    for q in range(4):
        for f in range(5):
            rows = slice(25 * f, 25 * f + 25)
            columns = slice(128 * q + 25 * f, 128 * q + 25 * f + 25)
            panel[rows, columns] = interpolation[q].T
            gather[columns, rows] = projection[q].T
    return two_parts(volume).reshape(256, 512), two_parts(panel), two_parts(gather)


def split(x):
    high = x.astype(bf16)
    low = (x - high.astype(f32)).astype(bf16)
    return high, low


def dot(a, b):
    return jnp.dot(a, b, preferred_element_type=f32)


def gas_state(fields):
    inverse = 1.0 / fields[0]
    kinetic = fields[1] * fields[1] + fields[2] * fields[2] + fields[3] * fields[3]
    pressure = (gamma_gas - 1.0) * (fields[4] - 0.5 * kinetic * inverse)
    return inverse, pressure


def flux_along(fields, d, inverse, pressure):
    velocity = fields[1 + d] * inverse
    components = [
        fields[1 + d],
        fields[1] * velocity,
        fields[2] * velocity,
        fields[3] * velocity,
        (fields[4] + pressure) * velocity,
    ]
    components[1 + d] = components[1 + d] + pressure
    return components, velocity


def sound_speed(inverse, pressure):
    return jnp.sqrt(gamma_gas * pressure * inverse)


def kernel(
    n_morton,
    n_sub,
    state_hbm,
    level_hbm,
    near_hbm,
    next_hbm,
    prev_hbm,
    coarse_hbm,
    fine_hbm,
    count_hbm,
    volume_hbm,
    panel_hbm,
    gather_hbm,
    x_ref,
    first_ref,
    rate_ref,
    state_ref,
    level_ref,
    near_ref,
    next_ref,
    prev_ref,
    coarse_ref,
    fine_ref,
    count_ref,
    volume_ref,
    panel_ref,
    gather_ref,
    load_sem,
    face_ref,
    face_bf_ref,
    rows_ref,
    pick_ref,
    spread_ref,
    outside_ref,
    added_ref,
    flux_high_ref,
    flux_low_ref,
    mortar_ref,
    numeric_ref,
    ring_send,
    ring_recv,
    message_send,
    message_recv,
    send_sem,
    recv_sem,
):
    m = lax.axis_index("morton")
    s = lax.axis_index("sub")
    devices = n_morton * n_sub
    place = m * n_sub + s
    after = lax.rem(place + 1, devices)
    before = lax.rem(place + devices - 1, devices)
    after_id = (after // n_sub, lax.rem(after, n_sub))
    before_id = (before // n_sub, lax.rem(before, n_sub))
    peers = [lax.rem(s + o, n_sub) for o in range(n_sub)]

    barrier = pltpu.get_barrier_semaphore()
    for o in range(1, n_sub):
        pl.semaphore_signal(barrier, inc=1, device_id=(m, peers[o]), device_id_type=MESH)
    for target in (after_id, before_id):
        pl.semaphore_signal(barrier, inc=1, device_id=target, device_id_type=MESH)

    loads = [
        pltpu.make_async_copy(source, target, load_sem.at[i])
        for i, (source, target) in enumerate(
            (
                (state_hbm, state_ref),
                (level_hbm, level_ref),
                (fine_hbm, fine_ref),
                (coarse_hbm, coarse_ref),
                (next_hbm, next_ref),
                (prev_hbm, prev_ref),
                (near_hbm, near_ref),
                (count_hbm, count_ref),
                (volume_hbm, volume_ref),
                (panel_hbm, panel_ref),
                (gather_hbm, gather_ref),
            )
        )
    ]
    for load in loads:
        load.start()
    for load in loads[0:8]:
        load.wait()

    level = level_ref[...]
    metric = 0.25 * jnp.left_shift(jnp.ones_like(level), level).astype(f32)
    near = near_ref[...]
    extra = near - 832
    panel_lane = 832 + (extra & 3) * 16 + ((extra >> 2) & 1) * 8 + (extra >> 3)
    entry = jnp.where(near >= 832, panel_lane, near)

    for f in range(5):
        x_ref[f, 0:125, :] = state_ref[f]
        x_ref[f, 125:128, :] = jnp.ones((3, 128), f32)
    row_ids = lax.broadcasted_iota(jnp.int32, (128, 128), 0)
    for face in range(6):
        face_ref[face, 125:126, :] = jnp.full((1, 128), float(face // 2), f32)
        face_ref[face, 126:127, :] = metric
        face_ref[face, 127:128, :] = jnp.full((1, 128), 1.0 if face % 2 else -1.0, f32)
    numeric_ref[125:128, :] = jnp.zeros((3, 128), f32)

    def section(step):
        for face in range(6):
            level_at = 4 * (face % 2)
            for f in range(5):
                base = 25 * f
                if face < 2:
                    face_ref[face, base : base + 25, :] = x_ref[f, 25 * level_at : 25 * level_at + 25, :]
                elif face < 4:
                    for a in range(5):
                        start = 25 * a + 5 * level_at
                        face_ref[face, base + 5 * a : base + 5 * a + 5, :] = x_ref[f, start : start + 5, :]
                else:
                    face_ref[face, base : base + 25, :] = x_ref[f, pl.ds(level_at, 25, stride=5), :]
        for face in range(6):
            rows_ref[128 * face : 128 * face + 128, :] = face_ref[face].T

        if step == 0:
            pl.semaphore_wait(barrier, n_sub + 1)
        copies = []
        for p in range(n_sub):
            for j in range(2):
                for q in range(4):
                    message_send[step, p, 4 * j + q : 4 * j + q + 1, :] = rows_ref[
                        pl.ds(fine_ref[0, j, q, p], 1), :
                    ]
                message_send[step, p, 8 + j : 9 + j, :] = rows_ref[pl.ds(coarse_ref[0, j, p], 1), :]
        for o in (4, 3, 5, 2, 6, 1, 7):
            copy = pltpu.make_async_remote_copy(
                src_ref=message_send.at[step, peers[o]],
                dst_ref=message_recv.at[step, s],
                send_sem=send_sem.at[step, o],
                recv_sem=recv_sem.at[step, o],
                device_id=(m, peers[o]),
                device_id_type=MESH,
            )
            copy.start()
            copies.append(copy)
        for side, (list_ref, target) in enumerate(((next_ref, after_id), (prev_ref, before_id))):
            for i in range(32):
                ring_send[step, side, i : i + 1, :] = rows_ref[pl.ds(list_ref[0, i], 1), :]
            copy = pltpu.make_async_remote_copy(
                src_ref=ring_send.at[step, side],
                dst_ref=ring_recv.at[step, side],
                send_sem=send_sem.at[step, n_sub + side],
                recv_sem=recv_sem.at[step, n_sub + side],
                device_id=target,
                device_id_type=MESH,
            )
            copy.start()
            copies.append(copy)
        message_recv[step, s] = message_send[step, s]

        if step == 0:
            for load in loads[8:11]:
                load.wait()
        fields = [x_ref[f] for f in range(5)]
        inverse, pressure = gas_state(fields)
        for d in range(3):
            components, unused = flux_along(fields, d, inverse, pressure)
            for f in range(5):
                high, low = split(components[f])
                flux_high_ref[128 * d : 128 * d + 128, 128 * f : 128 * f + 128] = high
                flux_low_ref[128 * d : 128 * d + 128, 128 * f : 128 * f + 128] = low
        for f in range(5):
            high, low = split(viscosity * metric * fields[f])
            flux_high_ref[384:512, 128 * f : 128 * f + 128] = high
            flux_low_ref[384:512, 128 * f : 128 * f + 128] = low
        both = dot(volume_ref[...], flux_high_ref[...])
        total = both[0:128] + both[128:256] + dot(volume_ref[0:128, :], flux_low_ref[...])
        for f in range(5):
            rate_ref[f] = metric * total[:, 128 * f : 128 * f + 128]

        if step == 0:
            for face in range(6):
                wanted = entry[face : face + 1, :]
                for block in range(7):
                    hit = (row_ids + 128 * block) == wanted
                    pick_ref[128 * block : 128 * block + 128, 128 * face : 128 * face + 128] = jnp.where(
                        hit, 1.0, 0.0
                    ).astype(bf16)
            small_rows = lax.broadcasted_iota(jnp.int32, (16, 128), 0)
            small_lanes = lax.broadcasted_iota(jnp.int32, (16, 128), 1)
            owner = jnp.full((16, 128), -1, jnp.int32)
            for j in range(2):
                for p in range(n_sub):
                    slot = jnp.where(j < count_ref[0, p], coarse_ref[0, j, p], -1)
                    owner = jnp.where(small_rows == 8 * j + p, slot, owner)
            for face in range(6):
                spread_ref[:, 128 * face : 128 * face + 128] = jnp.where(
                    owner == small_lanes + 128 * face, 1.0, 0.0
                ).astype(bf16)
            owners.append(owner)
        for face in range(6):
            high, low = split(face_ref[face])
            face_bf_ref[0:128, 128 * face : 128 * face + 128] = high
            face_bf_ref[128:256, 128 * face : 128 * face + 128] = low
        local = dot(face_bf_ref[...], pick_ref[0:768, :])
        local = local[0:128] + local[128:256]
        for face in range(6):
            outside_ref[face] = local[:, 128 * face : 128 * face + 128]

        def panels_of(source):
            coarse_rows = jnp.concatenate(
                [source[step, :, 8 + j, :] for j in range(2)], axis=0
            )
            high, low = split(coarse_rows)
            wide = dot(high, panel_ref[0]) + dot(low, panel_ref[0]) + dot(high, panel_ref[1])
            return [wide[:, 128 * q : 128 * q + 128] for q in range(4)]

        own_panels = panels_of(message_send)

        for copy in copies:
            copy.wait_recv()

        arrived = jnp.concatenate(
            [ring_recv[step, 0], ring_recv[step, 1]] + panels_of(message_recv), axis=0
        ).T
        high, low = split(arrived)
        remote = dot(jnp.concatenate([high, low], axis=0), pick_ref[768:896, :])
        remote = remote[0:128] + remote[128:256]
        for face in range(6):
            outside_ref[face] = outside_ref[face] + remote[:, 128 * face : 128 * face + 128]

        fine_rows = [
            message_recv[step, :, 4 * j + q, :] for q in range(4) for j in range(2)
        ]
        mortar_ref[...] = jnp.concatenate(fine_rows + own_panels, axis=0).T
        left = lax.broadcasted_iota(jnp.int32, (1, 128), 1) < 64

        def across(x):
            return pltpu.roll(x, 64, 1)

        facts = [mortar_ref[125 + i : 126 + i, :] for i in range(3)]
        facts = [jnp.where(left, x, across(x)) for x in facts]
        along, mortar_metric, orient = facts
        sides = [mortar_ref[25 * f : 25 * f + 25, :] for f in range(5)]
        inverse, pressure = gas_state(sides)
        normal = jnp.where(along < 0.5, sides[1], jnp.where(along < 1.5, sides[2], sides[3]))
        velocity = normal * inverse
        speed = jnp.abs(velocity) + sound_speed(inverse, pressure)
        components = [
            normal,
            sides[1] * velocity + jnp.where(along < 0.5, pressure, 0.0),
            sides[2] * velocity + jnp.where((along > 0.5) & (along < 1.5), pressure, 0.0),
            sides[3] * velocity + jnp.where(along > 1.5, pressure, 0.0),
            (sides[4] + pressure) * velocity,
        ]
        damping = 0.5 * jnp.maximum(speed, across(speed)) + penalty * mortar_metric
        for f in range(5):
            numeric_ref[25 * f : 25 * f + 25, :] = 0.5 * orient * (
                components[f] + across(components[f])
            ) + damping * (sides[f] - across(sides[f]))
        numeric = numeric_ref[...].T
        wide = jnp.concatenate([numeric[16 * q : 16 * q + 16, :] for q in range(4)], axis=1)
        high, low = split(wide)
        projected = dot(high, gather_ref[0]) + dot(low, gather_ref[0]) + dot(high, gather_ref[1])
        projected = jnp.where(owners[0] >= 0, projected, 0.0).T
        high, low = split(projected)
        added = dot(jnp.concatenate([high, low], axis=0), spread_ref[...])
        added = added[0:128] + added[128:256]
        for face in range(6):
            added_ref[face] = added[:, 128 * face : 128 * face + 128]

        gain = lift_gain * metric
        for face in range(6):
            d = face // 2
            orient_here = 1.0 if face % 2 else -1.0
            inside = [face_ref[face, 25 * f : 25 * f + 25, :] for f in range(5)]
            beyond = [outside_ref[face, 25 * f : 25 * f + 25, :] for f in range(5)]
            coupled = near[face : face + 1, :] >= 0
            beyond = [jnp.where(coupled, b, i) for b, i in zip(beyond, inside)]
            inverse, pressure = gas_state(inside)
            flux_in, velocity = flux_along(inside, d, inverse, pressure)
            speed_in = jnp.abs(velocity) + sound_speed(inverse, pressure)
            inverse, pressure = gas_state(beyond)
            flux_out, velocity = flux_along(beyond, d, inverse, pressure)
            speed_out = jnp.abs(velocity) + sound_speed(inverse, pressure)
            damping = 0.5 * jnp.maximum(speed_in, speed_out) + penalty * metric
            level_at = 4 * (face % 2)
            for f in range(5):
                numeric_here = 0.5 * orient_here * (flux_in[f] + flux_out[f]) + damping * (
                    inside[f] - beyond[f]
                )
                surface = orient_here * flux_in[f] - jnp.where(coupled, numeric_here, 0.0)
                lifted = gain * (surface + added_ref[face, 25 * f : 25 * f + 25, :])
                if face < 2:
                    rows = slice(25 * level_at, 25 * level_at + 25)
                    rate_ref[f, rows, :] = rate_ref[f, rows, :] + lifted
                elif face < 4:
                    for a in range(5):
                        start = 25 * a + 5 * level_at
                        rows = slice(start, start + 5)
                        rate_ref[f, rows, :] = rate_ref[f, rows, :] + lifted[5 * a : 5 * a + 5, :]
                else:
                    rows = pl.ds(level_at, 25, stride=5)
                    rate_ref[f, rows, :] = rate_ref[f, rows, :] + lifted
        return copies

    owners = []
    copies = section(0)
    for f in range(5):
        first = step_size * rate_ref[f]
        first_ref[f] = section_a2 * first
        x_ref[f] = x_ref[f] + section_b1 * first
    copies = copies + section(1)
    for copy in copies:
        copy.wait_send()


def finish(x_ref, first_ref, rate_ref, out_hbm, register_hbm, out_ref, register_ref, sem):
    copies = []
    for f in range(5):
        register = first_ref[f, 0:125, :] + step_size * rate_ref[f, 0:125, :]
        register_ref[f] = register
        out_ref[f] = x_ref[f, 0:125, :] + section_b2 * register
        copies.append(pltpu.make_async_copy(register_ref.at[f], register_hbm.at[f], sem.at[0, f]))
        copies.append(pltpu.make_async_copy(out_ref.at[f], out_hbm.at[f], sem.at[1, f]))
        for copy in copies[-2:]:
            copy.start()
    for copy in copies:
        copy.wait()


def per_device(mesh_shape, flow_state, element_level, neighbour, send_next, send_prev, coarse_face, fine_face, send_count):
    n_morton, n_sub = mesh_shape
    volume, panel, gather = (jnp.asarray(t) for t in operator_tables())
    vmem = pl.BlockSpec(memory_space=pltpu.VMEM)
    hbm = pl.BlockSpec(memory_space=pltpu.HBM)
    shape = jax.ShapeDtypeStruct(flow_state.shape, f32)
    block = jax.ShapeDtypeStruct((5, 128, 128), f32)
    operands = (
        flow_state,
        element_level.reshape(1, -1),
        neighbour,
        send_next,
        send_prev,
        jnp.transpose(coarse_face, (0, 2, 1)),
        jnp.transpose(fine_face, (0, 2, 3, 1)),
        send_count,
        volume,
        panel,
        gather,
    )
    spaces = [pltpu.VMEM] * 3 + [pltpu.SMEM] * 5 + [pltpu.VMEM] * 3
    pieces = pl.pallas_call(
        functools.partial(kernel, n_morton, n_sub),
        out_shape=(block, block, block),
        in_specs=[hbm] * len(operands),
        out_specs=(vmem, vmem, vmem),
        scratch_shapes=[space(x.shape, x.dtype) for space, x in zip(spaces, operands)]
        + [
            pltpu.SemaphoreType.DMA((len(operands),)),
            pltpu.VMEM((6, 128, 128), f32),
            pltpu.VMEM((256, 768), bf16),
            pltpu.VMEM((768, 128), f32),
            pltpu.VMEM((896, 768), bf16),
            pltpu.VMEM((16, 768), bf16),
            pltpu.VMEM((6, 128, 128), f32),
            pltpu.VMEM((6, 128, 128), f32),
            pltpu.VMEM((512, 640), bf16),
            pltpu.VMEM((512, 640), bf16),
            pltpu.VMEM((128, 128), f32),
            pltpu.VMEM((128, 128), f32),
            pltpu.VMEM((2, 2, 32, 128), f32),
            pltpu.VMEM((2, 2, 32, 128), f32),
            pltpu.VMEM((2, n_sub, 10, 128), f32),
            pltpu.VMEM((2, n_sub, 10, 128), f32),
            pltpu.SemaphoreType.DMA((2, n_sub + 2)),
            pltpu.SemaphoreType.DMA((2, n_sub + 2)),
        ],
        compiler_params=pltpu.CompilerParams(
            collective_id=0, has_side_effects=True, vmem_limit_bytes=40 * 1024 * 1024
        ),
    )(*[pltpu.with_memory_space_constraint(x, pltpu.HBM) for x in operands])
    return pl.pallas_call(
        finish,
        out_shape=(shape, shape),
        in_specs=[vmem, vmem, vmem],
        out_specs=(hbm, hbm),
        scratch_shapes=[
            pltpu.VMEM(flow_state.shape, f32),
            pltpu.VMEM(flow_state.shape, f32),
            pltpu.SemaphoreType.DMA((2, 5)),
        ],
        compiler_params=pltpu.CompilerParams(vmem_limit_bytes=16 * 1024 * 1024),
    )(*pieces)


def solution(mesh):
    whole = ("morton", "sub")
    placed = (
        P(None, None, whole),
        P(whole),
        P(None, whole),
        P(whole, None),
        P(whole, None),
        P(whole, None, None),
        P(whole, None, None, None),
        P(whole, None),
    )
    mesh_shape = (mesh.shape["morton"], mesh.shape["sub"])
    return jax.shard_map(
        functools.partial(per_device, mesh_shape),
        mesh=mesh,
        in_specs=placed,
        out_specs=(P(None, None, whole), P(None, None, whole)),
        check_vma=False,
    )
```

```python
import functools

import jax
import jax.numpy as jnp
import numpy as np
from jax import lax
from jax.experimental import pallas as pl
from jax.experimental.pallas import tpu as pltpu
from jax.sharding import PartitionSpec as P

gamma_gas = 1.4
viscosity = 0.01
penalty = 0.1
lift_gain = 10.0
step_size = 0.05
section_a2 = -0.4178904745
section_b1 = 0.1496590219993
section_b2 = 0.3792103129999
MESH = pl.DeviceIdType.MESH
f32 = jnp.float32
bf16 = jnp.bfloat16


def basis_tables():
    points = np.array([-1.0, -np.sqrt(3.0 / 7.0), 0.0, np.sqrt(3.0 / 7.0), 1.0])
    weights = np.array([0.1, 49.0 / 90.0, 32.0 / 45.0, 49.0 / 90.0, 0.1])
    products = np.array(
        [np.prod([points[i] - points[m] for m in range(5) if m != i]) for i in range(5)]
    )
    derivative = np.zeros((5, 5))
    for i in range(5):
        for j in range(5):
            if i != j:
                derivative[i, j] = products[i] / (products[j] * (points[i] - points[j]))
        derivative[i, i] = -np.sum(derivative[i])
    halves = []
    projections = []
    for h in range(2):
        shifted = (points + 2.0 * h - 1.0) / 2.0
        interp = np.zeros((5, 5))
        for i in range(5):
            for j in range(5):
                interp[i, j] = np.prod(
                    [(shifted[i] - points[m]) / (points[j] - points[m]) for m in range(5) if m != j]
                )
        halves.append(interp)
        projections.append(weights[None, :] * interp.T / (2.0 * weights[:, None]))
    interpolation = np.stack([np.kron(halves[q // 2], halves[q % 2]) for q in range(4)])
    projection = np.stack([np.kron(projections[q // 2], projections[q % 2]) for q in range(4)])
    ident_five = np.eye(5)
    ident_quad = np.eye(25)
    gradients = np.stack(
        [
            np.kron(derivative, ident_quad),
            np.kron(ident_five, np.kron(derivative, ident_five)),
            np.kron(ident_quad, derivative),
        ]
    )
    laplace = (
        gradients[0] @ gradients[0] + gradients[1] @ gradients[1] + gradients[2] @ gradients[2]
    )
    return interpolation, projection, gradients, laplace


def two_parts(table):
    table = table.astype(np.float32)
    high = table.astype(jnp.bfloat16)
    low = (table - high.astype(np.float32)).astype(jnp.bfloat16)
    return np.stack([high, low])


def operator_tables():
    interpolation, projection, gradients, laplace = basis_tables()
    volume = np.zeros((128, 512))
    for d in range(3):
        volume[:125, 128 * d : 128 * d + 125] = -gradients[d]
    volume[:125, 384:509] = laplace
    panel = np.zeros((128, 512))
    gather = np.zeros((512, 128))
    for q in range(4):
        for f in range(5):
            rows = slice(25 * f, 25 * f + 25)
            columns = slice(128 * q + 25 * f, 128 * q + 25 * f + 25)
            panel[rows, columns] = interpolation[q].T
            gather[columns, rows] = projection[q]
    return two_parts(volume).reshape(256, 512), two_parts(panel), two_parts(gather)


def split(x):
    high = x.astype(bf16)
    low = (x - high.astype(f32)).astype(bf16)
    return high, low


def dot(a, b):
    return jnp.dot(a, b, preferred_element_type=f32)


def gas_state(fields):
    inverse = 1.0 / fields[0]
    kinetic = fields[1] * fields[1] + fields[2] * fields[2] + fields[3] * fields[3]
    pressure = (gamma_gas - 1.0) * (fields[4] - 0.5 * kinetic * inverse)
    return inverse, pressure


def flux_along(fields, d, inverse, pressure):
    velocity = fields[1 + d] * inverse
    components = [
        fields[1 + d],
        fields[1] * velocity,
        fields[2] * velocity,
        fields[3] * velocity,
        (fields[4] + pressure) * velocity,
    ]
    components[1 + d] = components[1 + d] + pressure
    return components, velocity


def sound_speed(inverse, pressure):
    return jnp.sqrt(gamma_gas * pressure * inverse)


def mortar_part(fields):
    inverse, pressure = gas_state(fields)
    return inverse, pressure, sound_speed(inverse, pressure)


def flux_by_lane(fields, parts, along):
    inverse, pressure, sound = parts
    normal = jnp.where(along < 0.5, fields[1], jnp.where(along < 1.5, fields[2], fields[3]))
    velocity = normal * inverse
    components = [
        normal,
        fields[1] * velocity + jnp.where(along < 0.5, pressure, 0.0),
        fields[2] * velocity + jnp.where((along > 0.5) & (along < 1.5), pressure, 0.0),
        fields[3] * velocity + jnp.where(along > 1.5, pressure, 0.0),
        (fields[4] + pressure) * velocity,
    ]
    return components, jnp.abs(velocity) + sound


def face_fields(ref):
    return [ref[25 * f : 25 * f + 25, :] for f in range(5)]


def both_halves(x):
    return x[0:128] + x[128:256]


def kernel(
    n_morton,
    n_sub,
    state_hbm,
    level_hbm,
    near_hbm,
    next_hbm,
    prev_hbm,
    coarse_hbm,
    fine_hbm,
    count_hbm,
    volume_hbm,
    panel_hbm,
    gather_hbm,
    x_ref,
    first_ref,
    rate_ref,
    state_ref,
    level_ref,
    near_ref,
    next_ref,
    prev_ref,
    coarse_ref,
    fine_ref,
    count_ref,
    volume_ref,
    panel_ref,
    gather_ref,
    load_sem,
    face_ref,
    face_bf_ref,
    pick_ref,
    spread_ref,
    send_pick_ref,
    outside_ref,
    added_ref,
    flux_high_ref,
    flux_low_ref,
    inner_ref,
    ring_ref,
    known_ref,
    arrived_ref,
    numeric_ref,
    ring_send,
    ring_recv,
    message_send,
    message_recv,
    send_sem,
    recv_sem,
):
    m = lax.axis_index("morton")
    s = lax.axis_index("sub")
    devices = n_morton * n_sub
    place = m * n_sub + s
    after = lax.rem(place + 1, devices)
    before = lax.rem(place + devices - 1, devices)
    after_id = (after // n_sub, lax.rem(after, n_sub))
    before_id = (before // n_sub, lax.rem(before, n_sub))
    peers = [lax.rem(s + o, n_sub) for o in range(n_sub)]

    barrier = pltpu.get_barrier_semaphore()
    for o in (4, 3, 5, 2, 6, 1, 7):
        pl.semaphore_signal(barrier, inc=1, device_id=(m, peers[o]), device_id_type=MESH)
    for target in (after_id, before_id):
        pl.semaphore_signal(barrier, inc=1, device_id=target, device_id_type=MESH)

    loads = [
        pltpu.make_async_copy(source, target, load_sem.at[i])
        for i, (source, target) in enumerate(
            (
                (state_hbm, state_ref),
                (level_hbm, level_ref),
                (fine_hbm, fine_ref),
                (coarse_hbm, coarse_ref),
                (next_hbm, next_ref),
                (prev_hbm, prev_ref),
                (near_hbm, near_ref),
                (count_hbm, count_ref),
                (volume_hbm, volume_ref),
                (panel_hbm, panel_ref),
                (gather_hbm, gather_ref),
            )
        )
    ]
    for load in loads:
        load.start()
    for load in loads[0:8]:
        load.wait()

    level = level_ref[...]
    metric = 0.25 * jnp.left_shift(jnp.ones_like(level), level).astype(f32)
    near = near_ref[...]
    extra = near - 832
    panel_lane = 768 + (extra & 3) * 16 + ((extra >> 2) & 1) * 8 + (extra >> 3)
    entry = jnp.where(near >= 832, panel_lane, jnp.where(near >= 768, near + 64, near))
    lane = lax.broadcasted_iota(jnp.int32, (1, 128), 1)
    low_lanes = lane < 64
    counts = jnp.zeros((1, 128), jnp.int32)
    for p in range(n_sub):
        counts = jnp.where((lane & 7) == p, count_ref[0, p], counts)
    used = ((lane >> 3) & 1) < counts

    for f in range(5):
        x_ref[f, 0:125, :] = state_ref[f]
        x_ref[f, 125:128, :] = jnp.ones((3, 128), f32)
    for face in range(6):
        face_ref[face, 125:126, :] = jnp.full((1, 128), float(face // 2), f32)
        face_ref[face, 126:127, :] = metric
        face_ref[face, 127:128, :] = jnp.full((1, 128), 1.0 if face % 2 else -1.0, f32)
    numeric_ref[125:128, :] = jnp.zeros((3, 128), f32)

    rows = lax.broadcasted_iota(jnp.int32, (16, 128), 0)
    lanes = lax.broadcasted_iota(jnp.int32, (16, 128), 1)

    def marks(slots, target_ref, at):
        column = jnp.full((16, 128), -1, jnp.int32)
        for r, slot in enumerate(slots):
            column = jnp.where(rows == r, slot, column)
        for face in range(6):
            hit = jnp.where(column == lanes + 128 * face, 1.0, 0.0).astype(bf16)
            for row in at:
                target_ref[row : row + 16, 128 * face : 128 * face + 128] = hit

    for b in range(4):
        list_ref = (next_ref, prev_ref)[b // 2]
        marks([list_ref[0, 16 * (b % 2) + i] for i in range(16)], send_pick_ref, [16 * b])
    for p in range(n_sub):
        marks(
            [fine_ref[0, r // 4, r % 4, p] for r in range(8)] + [coarse_ref[0, j, p] for j in range(2)],
            send_pick_ref,
            [64 + 16 * p],
        )

    def onto_planes(target_ref, face, f, value):
        level_at = 4 * (face % 2)
        if face < 2:
            plane = slice(25 * level_at, 25 * level_at + 25)
            target_ref[f, plane, :] = target_ref[f, plane, :] + value
        elif face < 4:
            for a in range(5):
                start = 25 * a + 5 * level_at
                plane = slice(start, start + 5)
                target_ref[f, plane, :] = target_ref[f, plane, :] + value[5 * a : 5 * a + 5, :]
        else:
            plane = pl.ds(level_at, 25, stride=5)
            target_ref[f, plane, :] = target_ref[f, plane, :] + value

    def store_added(product):
        added = both_halves(product)
        for face in range(6):
            added_ref[face] = added[:, 128 * face : 128 * face + 128]

    def panels_of(source):
        coarse_rows = jnp.concatenate([source[:, 8 + j, :] for j in range(2)], axis=0)
        high, low = split(coarse_rows)
        wide = dot(high, panel_ref[0]) + dot(low, panel_ref[0]) + dot(high, panel_ref[1])
        return [wide[:, 128 * q : 128 * q + 128] for q in range(4)]

    gain = lift_gain * metric

    def section(step):
        for face in range(6):
            level_at = 4 * (face % 2)
            for f in range(5):
                base = 25 * f
                if face < 2:
                    face_ref[face, base : base + 25, :] = x_ref[f, 25 * level_at : 25 * level_at + 25, :]
                elif face < 4:
                    for a in range(5):
                        start = 25 * a + 5 * level_at
                        face_ref[face, base + 5 * a : base + 5 * a + 5, :] = x_ref[f, start : start + 5, :]
                else:
                    face_ref[face, base : base + 25, :] = x_ref[f, pl.ds(level_at, 25, stride=5), :]
        for face in range(6):
            high, low = split(face_ref[face])
            face_bf_ref[0:128, 128 * face : 128 * face + 128] = high
            face_bf_ref[128:256, 128 * face : 128 * face + 128] = low
        across = (((1,), (1,)), ((), ()))
        packed = lax.dot_general(
            send_pick_ref[...], face_bf_ref[...], across, preferred_element_type=f32
        )
        packed = packed[:, 0:128] + packed[:, 128:256]
        for p in range(n_sub):
            message_send[step, p] = packed[64 + 16 * p : 74 + 16 * p, :]
        for side in range(2):
            ring_send[step, side] = packed[32 * side : 32 * side + 32, :]
        if step == 0:
            pl.semaphore_wait(barrier, n_sub + 1)
        messages = []
        for o in (4, 3, 5, 2, 6, 1, 7):
            copy = pltpu.make_async_remote_copy(
                src_ref=message_send.at[step, peers[o]],
                dst_ref=message_recv.at[step, s],
                send_sem=send_sem.at[step, o],
                recv_sem=recv_sem.at[step, o],
                device_id=(m, peers[o]),
                device_id_type=MESH,
            )
            copy.start()
            messages.append(copy)
        rings = []
        for side, target in enumerate((after_id, before_id)):
            copy = pltpu.make_async_remote_copy(
                src_ref=ring_send.at[step, side],
                dst_ref=ring_recv.at[step, side],
                send_sem=send_sem.at[step, n_sub + side],
                recv_sem=recv_sem.at[step, n_sub + side],
                device_id=target,
                device_id_type=MESH,
            )
            copy.start()
            rings.append(copy)
        message_recv[step, s] = message_send[step, s]

        if step == 0:
            for load in loads[8:11]:
                load.wait()
        else:
            for face in range(6):
                for f in range(5):
                    onto_planes(rate_ref, face, f, gain * added_ref[face, 25 * f : 25 * f + 25, :])
            for f in range(5):
                first_ref[f] = (section_a2 * step_size) * rate_ref[f]
        fields = [x_ref[f] for f in range(5)]
        inverse, pressure = gas_state(fields)
        for d in range(3):
            components, unused = flux_along(fields, d, inverse, pressure)
            for f in range(5):
                high, low = split(components[f])
                flux_high_ref[128 * d : 128 * d + 128, 128 * f : 128 * f + 128] = high
                flux_low_ref[128 * d : 128 * d + 128, 128 * f : 128 * f + 128] = low
        for f in range(5):
            high, low = split(viscosity * metric * fields[f])
            flux_high_ref[384:512, 128 * f : 128 * f + 128] = high
            flux_low_ref[384:512, 128 * f : 128 * f + 128] = low
        total = both_halves(dot(volume_ref[...], flux_high_ref[...]))
        total = total + dot(volume_ref[0:128, :], flux_low_ref[...])
        for f in range(5):
            rate_ref[f] = metric * total[:, 128 * f : 128 * f + 128]

        if step == 0:
            for face in range(6):
                wanted = entry[face : face + 1, :]
                for block in range(56):
                    pick_ref[16 * block : 16 * block + 16, 128 * face : 128 * face + 128] = jnp.where(
                        rows + 16 * block == wanted, 1.0, 0.0
                    ).astype(bf16)
            spread_ref[0:64, :] = pick_ref[768:832, :]
            owned = [
                jnp.where(j < count_ref[0, p], coarse_ref[0, j, p], -1) for j in range(2) for p in range(n_sub)
            ]
            marks(owned, spread_ref, [64, 80, 96, 112])
        local = both_halves(dot(face_bf_ref[...], pick_ref[0:768, :]))
        for face in range(6):
            outside_ref[face] = local[:, 128 * face : 128 * face + 128]
        inner_ref[...] = both_halves(
            lax.dot_general(face_bf_ref[...], pick_ref[768:896, :], across, preferred_element_type=f32)
        )
        own = jnp.concatenate([jnp.zeros((64, 128), f32)] + panels_of(message_send.at[step]), axis=0).T
        known_ref[...] = jnp.where(low_lanes, inner_ref[...], own)
        inner_facts = [inner_ref[125 + i : 126 + i, :] for i in range(3)]

        for copy in rings:
            copy.wait_recv()
        ring_ref[...] = jnp.concatenate(
            [jnp.zeros((64, 128), f32), ring_recv[step, 0], ring_recv[step, 1]], axis=0
        ).T
        along, scale, orient = inner_facts
        inside = face_fields(inner_ref)
        beyond = face_fields(ring_ref)
        flux_in, speed_in = flux_by_lane(inside, mortar_part(inside), along)
        flux_out, speed_out = flux_by_lane(beyond, mortar_part(beyond), along)
        damping = 0.5 * jnp.maximum(speed_in, speed_out) + penalty * scale
        for f in range(5):
            value = 0.5 * orient * (flux_in[f] + flux_out[f]) + damping * (inside[f] - beyond[f])
            numeric_ref[25 * f : 25 * f + 25, :] = jnp.where(low_lanes, 0.0, -value)
        high, low = split(numeric_ref[...])
        store_added(dot(jnp.concatenate([high, low], axis=0), pick_ref[768:896, :]))

        for face in range(6):
            d = face // 2
            orient_here = 1.0 if face % 2 else -1.0
            inside = face_fields(face_ref.at[face])
            beyond = face_fields(outside_ref.at[face])
            coupled = (near[face : face + 1, :] >= 0) & (near[face : face + 1, :] < 768)
            inverse, pressure = gas_state(inside)
            flux_in, velocity = flux_along(inside, d, inverse, pressure)
            speed_in = jnp.abs(velocity) + sound_speed(inverse, pressure)
            inverse, pressure = gas_state(beyond)
            flux_out, velocity = flux_along(beyond, d, inverse, pressure)
            speed_out = jnp.abs(velocity) + sound_speed(inverse, pressure)
            damping = 0.5 * jnp.maximum(speed_in, speed_out) + penalty * metric
            for f in range(5):
                value = 0.5 * orient_here * (flux_in[f] + flux_out[f]) + damping * (inside[f] - beyond[f])
                surface = orient_here * flux_in[f] - jnp.where(coupled, value, 0.0)
                surface = surface + added_ref[face, 25 * f : 25 * f + 25, :]
                onto_planes(rate_ref, face, f, gain * surface)
        if step == 0:
            for f in range(5):
                x_ref[f] = x_ref[f] + (section_b1 * step_size) * rate_ref[f]

        known = face_fields(known_ref)
        known_parts = mortar_part(known)
        for copy in messages:
            copy.wait_recv()
        fine_rows = [message_recv[step, :, 4 * j + q, :] for q in range(4) for j in range(2)]
        arrived_ref[...] = jnp.concatenate(panels_of(message_recv.at[step]) + fine_rows, axis=0).T
        facts = [
            jnp.where(low_lanes, x, arrived_ref[125 + i : 126 + i, :]) for i, x in enumerate(inner_facts)
        ]
        along, scale, orient = facts
        valid = jnp.where(low_lanes, orient, jnp.where(used, 1.0, 0.0)) != 0.0
        arrived = face_fields(arrived_ref)
        flux_new, speed_new = flux_by_lane(arrived, mortar_part(arrived), along)
        flux_old, speed_old = flux_by_lane(known, known_parts, along)
        damping = 0.5 * jnp.maximum(speed_new, speed_old) + penalty * scale
        damping = jnp.where(low_lanes, -damping, damping)
        for f in range(5):
            value = 0.5 * orient * (flux_new[f] + flux_old[f]) + damping * (arrived[f] - known[f])
            numeric_ref[25 * f : 25 * f + 25, :] = value
        numeric = numeric_ref[...]
        high, low = split(numeric)
        wide = dot(gather_ref[0], high) + dot(gather_ref[0], low) + dot(gather_ref[1], high)
        ready = -numeric
        for q in range(4):
            block = (lane >= 64 + 16 * q) & (lane < 80 + 16 * q)
            ready = jnp.where(block, wide[128 * q : 128 * q + 128, :], ready)
        ready = jnp.where(valid, ready, 0.0)
        high, low = split(ready)
        store_added(dot(jnp.concatenate([high, low], axis=0), spread_ref[...]))
        if step == 0:
            gain_now = (section_b1 * step_size * lift_gain) * metric
            for face in range(6):
                for f in range(5):
                    onto_planes(x_ref, face, f, gain_now * added_ref[face, 25 * f : 25 * f + 25, :])
        else:
            for face in range(6):
                for f in range(5):
                    onto_planes(rate_ref, face, f, gain * added_ref[face, 25 * f : 25 * f + 25, :])
        return rings + messages

    copies = section(0)
    copies = copies + section(1)
    for copy in copies:
        copy.wait_send()


def finish(x_ref, first_ref, rate_ref, out_hbm, register_hbm, out_ref, register_ref, sem):
    copies = []
    for f in range(5):
        register = first_ref[f, 0:125, :] + step_size * rate_ref[f, 0:125, :]
        register_ref[f] = register
        out_ref[f] = x_ref[f, 0:125, :] + section_b2 * register
        copies.append(pltpu.make_async_copy(register_ref.at[f], register_hbm.at[f], sem.at[0, f]))
        copies.append(pltpu.make_async_copy(out_ref.at[f], out_hbm.at[f], sem.at[1, f]))
        for copy in copies[-2:]:
            copy.start()
    for copy in copies:
        copy.wait()


def per_device(mesh_shape, flow_state, element_level, neighbour, send_next, send_prev, coarse_face, fine_face, send_count):
    n_morton, n_sub = mesh_shape
    volume, panel, gather = (jnp.asarray(t) for t in operator_tables())
    vmem = pl.BlockSpec(memory_space=pltpu.VMEM)
    hbm = pl.BlockSpec(memory_space=pltpu.HBM)
    shape = jax.ShapeDtypeStruct(flow_state.shape, f32)
    block = jax.ShapeDtypeStruct((5, 128, 128), f32)
    operands = (
        flow_state,
        element_level.reshape(1, -1),
        neighbour,
        send_next,
        send_prev,
        jnp.transpose(coarse_face, (0, 2, 1)),
        jnp.transpose(fine_face, (0, 2, 3, 1)),
        send_count,
        volume,
        panel,
        gather,
    )
    spaces = [pltpu.VMEM] * 3 + [pltpu.SMEM] * 5 + [pltpu.VMEM] * 3
    pieces = pl.pallas_call(
        functools.partial(kernel, n_morton, n_sub),
        out_shape=(block, block, block),
        in_specs=[hbm] * len(operands),
        out_specs=(vmem, vmem, vmem),
        scratch_shapes=[space(x.shape, x.dtype) for space, x in zip(spaces, operands)]
        + [
            pltpu.SemaphoreType.DMA((len(operands),)),
            pltpu.VMEM((6, 128, 128), f32),
            pltpu.VMEM((256, 768), bf16),
            pltpu.VMEM((896, 768), bf16),
            pltpu.VMEM((128, 768), bf16),
            pltpu.VMEM((192, 768), bf16),
            pltpu.VMEM((6, 128, 128), f32),
            pltpu.VMEM((6, 128, 128), f32),
            pltpu.VMEM((512, 640), bf16),
            pltpu.VMEM((512, 640), bf16),
            pltpu.VMEM((128, 128), f32),
            pltpu.VMEM((128, 128), f32),
            pltpu.VMEM((128, 128), f32),
            pltpu.VMEM((128, 128), f32),
            pltpu.VMEM((128, 128), f32),
            pltpu.VMEM((2, 2, 32, 128), f32),
            pltpu.VMEM((2, 2, 32, 128), f32),
            pltpu.VMEM((2, n_sub, 10, 128), f32),
            pltpu.VMEM((2, n_sub, 10, 128), f32),
            pltpu.SemaphoreType.DMA((2, n_sub + 2)),
            pltpu.SemaphoreType.DMA((2, n_sub + 2)),
        ],
        compiler_params=pltpu.CompilerParams(
            collective_id=0, has_side_effects=True, vmem_limit_bytes=40 * 1024 * 1024
        ),
    )(*[pltpu.with_memory_space_constraint(x, pltpu.HBM) for x in operands])
    return pl.pallas_call(
        finish,
        out_shape=(shape, shape),
        in_specs=[vmem, vmem, vmem],
        out_specs=(hbm, hbm),
        scratch_shapes=[
            pltpu.VMEM(flow_state.shape, f32),
            pltpu.VMEM(flow_state.shape, f32),
            pltpu.SemaphoreType.DMA((2, 5)),
        ],
        compiler_params=pltpu.CompilerParams(vmem_limit_bytes=16 * 1024 * 1024),
    )(*pieces)


def solution(mesh):
    whole = ("morton", "sub")
    placed = (
        P(None, None, whole),
        P(whole),
        P(None, whole),
        P(whole, None),
        P(whole, None),
        P(whole, None, None),
        P(whole, None, None, None),
        P(whole, None),
    )
    mesh_shape = (mesh.shape["morton"], mesh.shape["sub"])
    return jax.shard_map(
        functools.partial(per_device, mesh_shape),
        mesh=mesh,
        in_specs=placed,
        out_specs=(P(None, None, whole), P(None, None, whole)),
        check_vma=False,
    )
```

```python
import functools

import jax
import jax.numpy as jnp
import numpy as np
from jax import lax
from jax.experimental import pallas as pl
from jax.experimental.pallas import tpu as pltpu
from jax.sharding import PartitionSpec as P

gamma_gas = 1.4
viscosity = 0.01
penalty = 0.1
lift_gain = 10.0
step_size = 0.05
section_a2 = -0.4178904745
section_b1 = 0.1496590219993
section_b2 = 0.3792103129999
MESH = pl.DeviceIdType.MESH
f32 = jnp.float32
bf16 = jnp.bfloat16


def basis_tables():
    points = np.array([-1.0, -np.sqrt(3.0 / 7.0), 0.0, np.sqrt(3.0 / 7.0), 1.0])
    weights = np.array([0.1, 49.0 / 90.0, 32.0 / 45.0, 49.0 / 90.0, 0.1])
    products = np.array(
        [np.prod([points[i] - points[m] for m in range(5) if m != i]) for i in range(5)]
    )
    derivative = np.zeros((5, 5))
    for i in range(5):
        for j in range(5):
            if i != j:
                derivative[i, j] = products[i] / (products[j] * (points[i] - points[j]))
        derivative[i, i] = -np.sum(derivative[i])
    halves = []
    projections = []
    for h in range(2):
        shifted = (points + 2.0 * h - 1.0) / 2.0
        interp = np.zeros((5, 5))
        for i in range(5):
            for j in range(5):
                interp[i, j] = np.prod(
                    [(shifted[i] - points[m]) / (points[j] - points[m]) for m in range(5) if m != j]
                )
        halves.append(interp)
        projections.append(weights[None, :] * interp.T / (2.0 * weights[:, None]))
    interpolation = np.stack([np.kron(halves[q // 2], halves[q % 2]) for q in range(4)])
    projection = np.stack([np.kron(projections[q // 2], projections[q % 2]) for q in range(4)])
    ident_five = np.eye(5)
    ident_quad = np.eye(25)
    gradients = np.stack(
        [
            np.kron(derivative, ident_quad),
            np.kron(ident_five, np.kron(derivative, ident_five)),
            np.kron(ident_quad, derivative),
        ]
    )
    laplace = (
        gradients[0] @ gradients[0] + gradients[1] @ gradients[1] + gradients[2] @ gradients[2]
    )
    return interpolation, projection, gradients, laplace


def two_parts(table):
    table = table.astype(np.float32)
    high = table.astype(jnp.bfloat16)
    low = (table - high.astype(np.float32)).astype(jnp.bfloat16)
    return np.stack([high, low])


def operator_tables():
    interpolation, projection, gradients, laplace = basis_tables()
    volume = np.zeros((128, 512))
    for d in range(3):
        volume[:125, 128 * d : 128 * d + 125] = -gradients[d]
    volume[:125, 384:509] = laplace
    panel = np.zeros((128, 512))
    gather = np.zeros((512, 128))
    for q in range(4):
        for f in range(5):
            rows = slice(25 * f, 25 * f + 25)
            columns = slice(128 * q + 25 * f, 128 * q + 25 * f + 25)
            panel[rows, columns] = interpolation[q].T
            gather[columns, rows] = projection[q]
    return two_parts(volume).reshape(256, 512), two_parts(panel), two_parts(gather)


def split(x):
    high = x.astype(bf16)
    low = (x - high.astype(f32)).astype(bf16)
    return high, low


def dot(a, b):
    return jnp.dot(a, b, preferred_element_type=f32)


def gas_state(fields):
    inverse = 1.0 / fields[0]
    kinetic = fields[1] * fields[1] + fields[2] * fields[2] + fields[3] * fields[3]
    pressure = (gamma_gas - 1.0) * (fields[4] - 0.5 * kinetic * inverse)
    return inverse, pressure


def flux_along(fields, d, inverse, pressure):
    velocity = fields[1 + d] * inverse
    components = [
        fields[1 + d],
        fields[1] * velocity,
        fields[2] * velocity,
        fields[3] * velocity,
        (fields[4] + pressure) * velocity,
    ]
    components[1 + d] = components[1 + d] + pressure
    return components, velocity


def sound_speed(inverse, pressure):
    return jnp.sqrt(gamma_gas * pressure * inverse)


def mortar_part(fields):
    inverse, pressure = gas_state(fields)
    return inverse, pressure, sound_speed(inverse, pressure)


def flux_by_lane(fields, parts, along):
    inverse, pressure, sound = parts
    normal = jnp.where(along < 0.5, fields[1], jnp.where(along < 1.5, fields[2], fields[3]))
    velocity = normal * inverse
    components = [
        normal,
        fields[1] * velocity + jnp.where(along < 0.5, pressure, 0.0),
        fields[2] * velocity + jnp.where((along > 0.5) & (along < 1.5), pressure, 0.0),
        fields[3] * velocity + jnp.where(along > 1.5, pressure, 0.0),
        (fields[4] + pressure) * velocity,
    ]
    return components, jnp.abs(velocity) + sound


def face_fields(ref):
    return [ref[25 * f : 25 * f + 25, :] for f in range(5)]


def both_halves(x):
    return x[0:128] + x[128:256]


def kernel(
    n_morton,
    n_sub,
    state_hbm,
    level_hbm,
    near_hbm,
    next_hbm,
    prev_hbm,
    coarse_hbm,
    fine_hbm,
    count_hbm,
    volume_hbm,
    panel_hbm,
    gather_hbm,
    x_ref,
    first_ref,
    rate_ref,
    state_ref,
    level_ref,
    near_ref,
    next_ref,
    prev_ref,
    coarse_ref,
    fine_ref,
    count_ref,
    volume_ref,
    panel_ref,
    gather_ref,
    load_sem,
    face_ref,
    face_bf_ref,
    pick_ref,
    spread_ref,
    send_pick_ref,
    outside_ref,
    added_ref,
    flux_high_ref,
    flux_low_ref,
    inner_ref,
    ring_ref,
    known_ref,
    arrived_ref,
    numeric_ref,
    passed_ref,
    ring_send,
    ring_recv,
    message_send,
    message_recv,
    send_sem,
    recv_sem,
):
    m = lax.axis_index("morton")
    s = lax.axis_index("sub")
    devices = n_morton * n_sub
    place = m * n_sub + s
    after = lax.rem(place + 1, devices)
    before = lax.rem(place + devices - 1, devices)
    after_id = (after // n_sub, lax.rem(after, n_sub))
    before_id = (before // n_sub, lax.rem(before, n_sub))
    peers = [lax.rem(s + o, n_sub) for o in range(n_sub)]

    barrier = pltpu.get_barrier_semaphore()
    for o in (4, 3, 5, 2, 6, 1, 7):
        pl.semaphore_signal(barrier, inc=1, device_id=(m, peers[o]), device_id_type=MESH)
    for target in (after_id, before_id):
        pl.semaphore_signal(barrier, inc=1, device_id=target, device_id_type=MESH)

    loads = [
        pltpu.make_async_copy(source, target, load_sem.at[i])
        for i, (source, target) in enumerate(
            (
                (state_hbm, state_ref),
                (level_hbm, level_ref),
                (fine_hbm, fine_ref),
                (coarse_hbm, coarse_ref),
                (next_hbm, next_ref),
                (prev_hbm, prev_ref),
                (near_hbm, near_ref),
                (count_hbm, count_ref),
                (volume_hbm, volume_ref),
                (panel_hbm, panel_ref),
                (gather_hbm, gather_ref),
            )
        )
    ]
    for load in loads:
        load.start()
    for load in loads[0:8]:
        load.wait()

    level = level_ref[...]
    metric = 0.25 * jnp.left_shift(jnp.ones_like(level), level).astype(f32)
    near = near_ref[...]
    extra = near - 832
    panel_lane = 768 + (extra & 3) * 16 + ((extra >> 2) & 1) * 8 + (extra >> 3)
    entry = jnp.where(near >= 832, panel_lane, jnp.where(near >= 768, near + 64, near))
    lane = lax.broadcasted_iota(jnp.int32, (1, 128), 1)
    low_lanes = lane < 64
    counts = jnp.zeros((1, 128), jnp.int32)
    for p in range(n_sub):
        counts = jnp.where((lane & 7) == p, count_ref[0, p], counts)
    used = ((lane >> 3) & 1) < counts

    for f in range(5):
        x_ref[f, 0:125, :] = state_ref[f]
        x_ref[f, 125:128, :] = jnp.ones((3, 128), f32)
    for face in range(6):
        face_ref[face, 125:126, :] = jnp.full((1, 128), float(face // 2), f32)
        face_ref[face, 126:127, :] = metric
        face_ref[face, 127:128, :] = jnp.full((1, 128), 1.0 if face % 2 else -1.0, f32)
    numeric_ref[125:128, :] = jnp.zeros((3, 128), f32)
    passed_ref[125:128, :] = jnp.zeros((3, 128), f32)

    rows = lax.broadcasted_iota(jnp.int32, (16, 128), 0)
    lanes = lax.broadcasted_iota(jnp.int32, (16, 128), 1)

    def marks(slots, target_ref, at):
        column = jnp.full((16, 128), -1, jnp.int32)
        for r, slot in enumerate(slots):
            column = jnp.where(rows == r, slot, column)
        for face in range(6):
            hit = jnp.where(column == lanes + 128 * face, 1.0, 0.0).astype(bf16)
            for row in at:
                target_ref[row : row + 16, 128 * face : 128 * face + 128] = hit

    for b in range(4):
        list_ref = (next_ref, prev_ref)[b // 2]
        marks([list_ref[0, 16 * (b % 2) + i] for i in range(16)], send_pick_ref, [16 * b])
    for p in range(n_sub):
        marks(
            [fine_ref[0, r // 4, r % 4, p] for r in range(8)] + [coarse_ref[0, j, p] for j in range(2)],
            send_pick_ref,
            [64 + 16 * p],
        )

    def onto_planes(target_ref, face, f, value):
        level_at = 4 * (face % 2)
        if face < 2:
            plane = slice(25 * level_at, 25 * level_at + 25)
            target_ref[f, plane, :] = target_ref[f, plane, :] + value
        elif face < 4:
            for a in range(5):
                start = 25 * a + 5 * level_at
                plane = slice(start, start + 5)
                target_ref[f, plane, :] = target_ref[f, plane, :] + value[5 * a : 5 * a + 5, :]
        else:
            plane = pl.ds(level_at, 25, stride=5)
            target_ref[f, plane, :] = target_ref[f, plane, :] + value

    def store_added(product):
        added = both_halves(product)
        for face in range(6):
            added_ref[face] = added[:, 128 * face : 128 * face + 128]

    def panels_of(source):
        coarse_rows = jnp.concatenate([source[:, 8 + j, :] for j in range(2)], axis=0)
        high, low = split(coarse_rows)
        wide = dot(high, panel_ref[0]) + dot(low, panel_ref[0]) + dot(high, panel_ref[1])
        return [wide[:, 128 * q : 128 * q + 128] for q in range(4)]

    gain = lift_gain * metric

    def section(step):
        for face in range(6):
            level_at = 4 * (face % 2)
            for f in range(5):
                base = 25 * f
                if face < 2:
                    face_ref[face, base : base + 25, :] = x_ref[f, 25 * level_at : 25 * level_at + 25, :]
                elif face < 4:
                    for a in range(5):
                        start = 25 * a + 5 * level_at
                        face_ref[face, base + 5 * a : base + 5 * a + 5, :] = x_ref[f, start : start + 5, :]
                else:
                    face_ref[face, base : base + 25, :] = x_ref[f, pl.ds(level_at, 25, stride=5), :]
        for face in range(6):
            high, low = split(face_ref[face])
            face_bf_ref[0:128, 128 * face : 128 * face + 128] = high
            face_bf_ref[128:256, 128 * face : 128 * face + 128] = low
        across = (((1,), (1,)), ((), ()))
        packed = lax.dot_general(
            send_pick_ref[...], face_bf_ref[...], across, preferred_element_type=f32
        )
        packed = packed[:, 0:128] + packed[:, 128:256]
        for p in range(n_sub):
            message_send[step, p] = packed[64 + 16 * p : 74 + 16 * p, :]
        for side in range(2):
            ring_send[step, side] = packed[32 * side : 32 * side + 32, :]
        if step == 0:
            pl.semaphore_wait(barrier, n_sub + 1)
        rings = []
        for side, target in enumerate((after_id, before_id)):
            copy = pltpu.make_async_remote_copy(
                src_ref=ring_send.at[step, side],
                dst_ref=ring_recv.at[step, side],
                send_sem=send_sem.at[step, n_sub + side],
                recv_sem=recv_sem.at[step, n_sub + side],
                device_id=target,
                device_id_type=MESH,
            )
            copy.start()
            rings.append(copy)
        messages = []
        for o in (4, 3, 5, 2, 6, 1, 7):
            copy = pltpu.make_async_remote_copy(
                src_ref=message_send.at[step, peers[o]],
                dst_ref=message_recv.at[step, s],
                send_sem=send_sem.at[step, o],
                recv_sem=recv_sem.at[step, o],
                device_id=(m, peers[o]),
                device_id_type=MESH,
            )
            copy.start()
            messages.append(copy)
        message_recv[step, s] = message_send[step, s]

        if step == 0:
            for load in loads[8:11]:
                load.wait()
        else:
            for face in range(6):
                for f in range(5):
                    onto_planes(rate_ref, face, f, gain * added_ref[face, 25 * f : 25 * f + 25, :])
            for f in range(5):
                first_ref[f] = (section_a2 * step_size) * rate_ref[f]
        fields = [x_ref[f] for f in range(5)]
        inverse, pressure = gas_state(fields)
        for d in range(3):
            components, unused = flux_along(fields, d, inverse, pressure)
            for f in range(5):
                high, low = split(components[f])
                flux_high_ref[128 * d : 128 * d + 128, 128 * f : 128 * f + 128] = high
                flux_low_ref[128 * d : 128 * d + 128, 128 * f : 128 * f + 128] = low
        for f in range(5):
            high, low = split(viscosity * metric * fields[f])
            flux_high_ref[384:512, 128 * f : 128 * f + 128] = high
            flux_low_ref[384:512, 128 * f : 128 * f + 128] = low
        total = both_halves(dot(volume_ref[...], flux_high_ref[...]))
        total = total + dot(volume_ref[0:128, :], flux_low_ref[...])
        for f in range(5):
            rate_ref[f] = metric * total[:, 128 * f : 128 * f + 128]

        if step == 0:
            for face in range(6):
                wanted = entry[face : face + 1, :]
                for block in range(56):
                    pick_ref[16 * block : 16 * block + 16, 128 * face : 128 * face + 128] = jnp.where(
                        rows + 16 * block == wanted, 1.0, 0.0
                    ).astype(bf16)
            spread_ref[0:64, :] = pick_ref[768:832, :]
            spread_ref[128:256, :] = pick_ref[768:896, :]
            owned = [
                jnp.where(j < count_ref[0, p], coarse_ref[0, j, p], -1) for j in range(2) for p in range(n_sub)
            ]
            marks(owned, spread_ref, [64, 80, 96, 112])
        local = both_halves(dot(face_bf_ref[...], pick_ref[0:768, :]))
        for face in range(6):
            outside_ref[face] = local[:, 128 * face : 128 * face + 128]
        inner_ref[...] = both_halves(
            lax.dot_general(face_bf_ref[...], pick_ref[768:896, :], across, preferred_element_type=f32)
        )
        own = jnp.concatenate([jnp.zeros((64, 128), f32)] + panels_of(message_send.at[step]), axis=0).T
        known_ref[...] = jnp.where(low_lanes, inner_ref[...], own)
        inner_facts = [inner_ref[125 + i : 126 + i, :] for i in range(3)]

        for face in range(6):
            d = face // 2
            orient_here = 1.0 if face % 2 else -1.0
            inside = face_fields(face_ref.at[face])
            beyond = face_fields(outside_ref.at[face])
            coupled = (near[face : face + 1, :] >= 0) & (near[face : face + 1, :] < 768)
            inverse, pressure = gas_state(inside)
            flux_in, velocity = flux_along(inside, d, inverse, pressure)
            speed_in = jnp.abs(velocity) + sound_speed(inverse, pressure)
            inverse, pressure = gas_state(beyond)
            flux_out, velocity = flux_along(beyond, d, inverse, pressure)
            speed_out = jnp.abs(velocity) + sound_speed(inverse, pressure)
            damping = 0.5 * jnp.maximum(speed_in, speed_out) + penalty * metric
            for f in range(5):
                value = 0.5 * orient_here * (flux_in[f] + flux_out[f]) + damping * (inside[f] - beyond[f])
                surface = orient_here * flux_in[f] - jnp.where(coupled, value, 0.0)
                onto_planes(rate_ref, face, f, gain * surface)
        if step == 0:
            for f in range(5):
                x_ref[f] = x_ref[f] + (section_b1 * step_size) * rate_ref[f]

        known = face_fields(known_ref)
        known_parts = mortar_part(known)
        inside = face_fields(inner_ref)
        flux_in, speed_in = flux_by_lane(inside, mortar_part(inside), inner_facts[0])
        for copy in rings + messages:
            copy.wait_recv()
        panels = panels_of(message_recv.at[step])
        ring_ref[...] = jnp.concatenate(
            [jnp.zeros((64, 128), f32), ring_recv[step, 0], ring_recv[step, 1]], axis=0
        ).T
        fine_rows = [message_recv[step, :, 4 * j + q, :] for q in range(4) for j in range(2)]
        arrived_ref[...] = jnp.concatenate(panels + fine_rows, axis=0).T
        facts = [
            jnp.where(low_lanes, x, arrived_ref[125 + i : 126 + i, :]) for i, x in enumerate(inner_facts)
        ]
        along, scale, orient = facts
        valid = jnp.where(low_lanes, orient, jnp.where(used, 1.0, 0.0)) != 0.0
        arrived = face_fields(arrived_ref)
        flux_new, speed_new = flux_by_lane(arrived, mortar_part(arrived), along)
        flux_old, speed_old = flux_by_lane(known, known_parts, along)
        damping = 0.5 * jnp.maximum(speed_new, speed_old) + penalty * scale
        damping = jnp.where(low_lanes, -damping, damping)
        for f in range(5):
            value = 0.5 * orient * (flux_new[f] + flux_old[f]) + damping * (arrived[f] - known[f])
            numeric_ref[25 * f : 25 * f + 25, :] = value
        numeric = numeric_ref[...]
        high, low = split(numeric)
        wide = dot(gather_ref[0], high) + dot(gather_ref[0], low) + dot(gather_ref[1], high)
        beyond = face_fields(ring_ref)
        along, scale, orient = inner_facts
        flux_out, speed_out = flux_by_lane(beyond, mortar_part(beyond), along)
        damping = 0.5 * jnp.maximum(speed_in, speed_out) + penalty * scale
        for f in range(5):
            value = 0.5 * orient * (flux_in[f] + flux_out[f]) + damping * (inside[f] - beyond[f])
            passed_ref[25 * f : 25 * f + 25, :] = jnp.where(low_lanes, 0.0, -value)
        ready = -numeric
        for q in range(4):
            block = (lane >= 64 + 16 * q) & (lane < 80 + 16 * q)
            ready = jnp.where(block, wide[128 * q : 128 * q + 128, :], ready)
        ready = jnp.where(valid, ready, 0.0)
        high, low = split(jnp.concatenate([ready, passed_ref[...]], axis=1))
        store_added(dot(jnp.concatenate([high, low], axis=0), spread_ref[...]))
        if step == 0:
            gain_now = (section_b1 * step_size * lift_gain) * metric
            for face in range(6):
                for f in range(5):
                    onto_planes(x_ref, face, f, gain_now * added_ref[face, 25 * f : 25 * f + 25, :])
        else:
            for face in range(6):
                for f in range(5):
                    onto_planes(rate_ref, face, f, gain * added_ref[face, 25 * f : 25 * f + 25, :])
        return rings + messages

    copies = section(0)
    copies = copies + section(1)
    for copy in copies:
        copy.wait_send()


def finish(x_ref, first_ref, rate_ref, out_hbm, register_hbm, out_ref, register_ref, sem):
    copies = []
    for f in range(5):
        register = first_ref[f, 0:125, :] + step_size * rate_ref[f, 0:125, :]
        register_ref[f] = register
        out_ref[f] = x_ref[f, 0:125, :] + section_b2 * register
        copies.append(pltpu.make_async_copy(register_ref.at[f], register_hbm.at[f], sem.at[0, f]))
        copies.append(pltpu.make_async_copy(out_ref.at[f], out_hbm.at[f], sem.at[1, f]))
        for copy in copies[-2:]:
            copy.start()
    for copy in copies:
        copy.wait()


def per_device(mesh_shape, flow_state, element_level, neighbour, send_next, send_prev, coarse_face, fine_face, send_count):
    n_morton, n_sub = mesh_shape
    volume, panel, gather = (jnp.asarray(t) for t in operator_tables())
    vmem = pl.BlockSpec(memory_space=pltpu.VMEM)
    hbm = pl.BlockSpec(memory_space=pltpu.HBM)
    shape = jax.ShapeDtypeStruct(flow_state.shape, f32)
    block = jax.ShapeDtypeStruct((5, 128, 128), f32)
    operands = (
        flow_state,
        element_level.reshape(1, -1),
        neighbour,
        send_next,
        send_prev,
        jnp.transpose(coarse_face, (0, 2, 1)),
        jnp.transpose(fine_face, (0, 2, 3, 1)),
        send_count,
        volume,
        panel,
        gather,
    )
    spaces = [pltpu.VMEM] * 3 + [pltpu.SMEM] * 5 + [pltpu.VMEM] * 3
    pieces = pl.pallas_call(
        functools.partial(kernel, n_morton, n_sub),
        out_shape=(block, block, block),
        in_specs=[hbm] * len(operands),
        out_specs=(vmem, vmem, vmem),
        scratch_shapes=[space(x.shape, x.dtype) for space, x in zip(spaces, operands)]
        + [
            pltpu.SemaphoreType.DMA((len(operands),)),
            pltpu.VMEM((6, 128, 128), f32),
            pltpu.VMEM((256, 768), bf16),
            pltpu.VMEM((896, 768), bf16),
            pltpu.VMEM((256, 768), bf16),
            pltpu.VMEM((192, 768), bf16),
            pltpu.VMEM((6, 128, 128), f32),
            pltpu.VMEM((6, 128, 128), f32),
            pltpu.VMEM((512, 640), bf16),
            pltpu.VMEM((512, 640), bf16),
            pltpu.VMEM((128, 128), f32),
            pltpu.VMEM((128, 128), f32),
            pltpu.VMEM((128, 128), f32),
            pltpu.VMEM((128, 128), f32),
            pltpu.VMEM((128, 128), f32),
            pltpu.VMEM((128, 128), f32),
            pltpu.VMEM((2, 2, 32, 128), f32),
            pltpu.VMEM((2, 2, 32, 128), f32),
            pltpu.VMEM((2, n_sub, 10, 128), f32),
            pltpu.VMEM((2, n_sub, 10, 128), f32),
            pltpu.SemaphoreType.DMA((2, n_sub + 2)),
            pltpu.SemaphoreType.DMA((2, n_sub + 2)),
        ],
        compiler_params=pltpu.CompilerParams(
            collective_id=0, has_side_effects=True, vmem_limit_bytes=40 * 1024 * 1024
        ),
    )(*[pltpu.with_memory_space_constraint(x, pltpu.HBM) for x in operands])
    return pl.pallas_call(
        finish,
        out_shape=(shape, shape),
        in_specs=[vmem, vmem, vmem],
        out_specs=(hbm, hbm),
        scratch_shapes=[
            pltpu.VMEM(flow_state.shape, f32),
            pltpu.VMEM(flow_state.shape, f32),
            pltpu.SemaphoreType.DMA((2, 5)),
        ],
        compiler_params=pltpu.CompilerParams(vmem_limit_bytes=16 * 1024 * 1024),
    )(*pieces)


def solution(mesh):
    whole = ("morton", "sub")
    placed = (
        P(None, None, whole),
        P(whole),
        P(None, whole),
        P(whole, None),
        P(whole, None),
        P(whole, None, None),
        P(whole, None, None, None),
        P(whole, None),
    )
    mesh_shape = (mesh.shape["morton"], mesh.shape["sub"])
    return jax.shard_map(
        functools.partial(per_device, mesh_shape),
        mesh=mesh,
        in_specs=placed,
        out_specs=(P(None, None, whole), P(None, None, whole)),
        check_vma=False,
    )
```

```python
import functools

import jax
import jax.numpy as jnp
import numpy as np
from jax import lax
from jax.experimental import pallas as pl
from jax.experimental.pallas import tpu as pltpu
from jax.sharding import PartitionSpec as P

gamma_gas = 1.4
viscosity = 0.01
penalty = 0.1
lift_gain = 10.0
step_size = 0.05
section_a2 = -0.4178904745
section_b1 = 0.1496590219993
section_b2 = 0.3792103129999
MESH = pl.DeviceIdType.MESH
f32 = jnp.float32
bf16 = jnp.bfloat16


def basis_tables():
    points = np.array([-1.0, -np.sqrt(3.0 / 7.0), 0.0, np.sqrt(3.0 / 7.0), 1.0])
    weights = np.array([0.1, 49.0 / 90.0, 32.0 / 45.0, 49.0 / 90.0, 0.1])
    products = np.array(
        [np.prod([points[i] - points[m] for m in range(5) if m != i]) for i in range(5)]
    )
    derivative = np.zeros((5, 5))
    for i in range(5):
        for j in range(5):
            if i != j:
                derivative[i, j] = products[i] / (products[j] * (points[i] - points[j]))
        derivative[i, i] = -np.sum(derivative[i])
    halves = []
    projections = []
    for h in range(2):
        shifted = (points + 2.0 * h - 1.0) / 2.0
        interp = np.zeros((5, 5))
        for i in range(5):
            for j in range(5):
                interp[i, j] = np.prod(
                    [(shifted[i] - points[m]) / (points[j] - points[m]) for m in range(5) if m != j]
                )
        halves.append(interp)
        projections.append(weights[None, :] * interp.T / (2.0 * weights[:, None]))
    interpolation = np.stack([np.kron(halves[q // 2], halves[q % 2]) for q in range(4)])
    projection = np.stack([np.kron(projections[q // 2], projections[q % 2]) for q in range(4)])
    ident_five = np.eye(5)
    ident_quad = np.eye(25)
    gradients = np.stack(
        [
            np.kron(derivative, ident_quad),
            np.kron(ident_five, np.kron(derivative, ident_five)),
            np.kron(ident_quad, derivative),
        ]
    )
    laplace = (
        gradients[0] @ gradients[0] + gradients[1] @ gradients[1] + gradients[2] @ gradients[2]
    )
    return interpolation, projection, gradients, laplace


def two_parts(table):
    table = table.astype(np.float32)
    high = table.astype(jnp.bfloat16)
    low = (table - high.astype(np.float32)).astype(jnp.bfloat16)
    return np.stack([high, low])


def operator_tables():
    interpolation, projection, gradients, laplace = basis_tables()
    volume = np.zeros((128, 512))
    for d in range(3):
        volume[:125, 128 * d : 128 * d + 125] = -gradients[d]
    volume[:125, 384:509] = laplace
    panel = np.zeros((128, 512))
    gather = np.zeros((512, 128))
    for q in range(4):
        for f in range(5):
            rows = slice(25 * f, 25 * f + 25)
            columns = slice(128 * q + 25 * f, 128 * q + 25 * f + 25)
            panel[rows, columns] = interpolation[q].T
            gather[columns, rows] = projection[q]
    beside = two_parts(gather).reshape(8, 128, 128).transpose(1, 0, 2).reshape(128, 1024)
    return two_parts(volume).reshape(256, 512), two_parts(panel).reshape(256, 512), beside


def split(x):
    high = x.astype(bf16)
    low = (x - high.astype(f32)).astype(bf16)
    return high, low


def dot(a, b):
    return jnp.dot(a, b, preferred_element_type=f32)


def gas_state(fields):
    inverse = 1.0 / fields[0]
    kinetic = fields[1] * fields[1] + fields[2] * fields[2] + fields[3] * fields[3]
    pressure = (gamma_gas - 1.0) * (fields[4] - 0.5 * kinetic * inverse)
    return inverse, pressure


def flux_along(fields, d, inverse, pressure):
    velocity = fields[1 + d] * inverse
    components = [
        fields[1 + d],
        fields[1] * velocity,
        fields[2] * velocity,
        fields[3] * velocity,
        (fields[4] + pressure) * velocity,
    ]
    components[1 + d] = components[1 + d] + pressure
    return components, velocity


def sound_speed(inverse, pressure):
    return jnp.sqrt(gamma_gas * pressure * inverse)


def mortar_part(fields):
    inverse, pressure = gas_state(fields)
    return inverse, pressure, sound_speed(inverse, pressure)


def flux_by_lane(fields, parts, along):
    inverse, pressure, sound = parts
    normal = jnp.where(along < 0.5, fields[1], jnp.where(along < 1.5, fields[2], fields[3]))
    velocity = normal * inverse
    components = [
        normal,
        fields[1] * velocity + jnp.where(along < 0.5, pressure, 0.0),
        fields[2] * velocity + jnp.where((along > 0.5) & (along < 1.5), pressure, 0.0),
        fields[3] * velocity + jnp.where(along > 1.5, pressure, 0.0),
        (fields[4] + pressure) * velocity,
    ]
    return components, jnp.abs(velocity) + sound


def face_fields(ref):
    return [ref[25 * f : 25 * f + 25, :] for f in range(5)]


def both_halves(x):
    return x[0:128] + x[128:256]


def kernel(
    n_morton,
    n_sub,
    state_hbm,
    level_hbm,
    near_hbm,
    next_hbm,
    prev_hbm,
    coarse_hbm,
    fine_hbm,
    count_hbm,
    volume_hbm,
    panel_hbm,
    gather_hbm,
    x_ref,
    first_ref,
    rate_ref,
    state_ref,
    level_ref,
    near_ref,
    next_ref,
    prev_ref,
    coarse_ref,
    fine_ref,
    count_ref,
    volume_ref,
    panel_ref,
    gather_ref,
    load_sem,
    face_ref,
    face_bf_ref,
    pick_ref,
    spread_ref,
    send_pick_ref,
    outside_ref,
    added_ref,
    flux_high_ref,
    flux_low_ref,
    inner_ref,
    ring_ref,
    known_ref,
    arrived_ref,
    numeric_ref,
    passed_ref,
    ring_send,
    ring_recv,
    message_send,
    message_recv,
    send_sem,
    recv_sem,
):
    m = lax.axis_index("morton")
    s = lax.axis_index("sub")
    devices = n_morton * n_sub
    place = m * n_sub + s
    after = lax.rem(place + 1, devices)
    before = lax.rem(place + devices - 1, devices)
    after_id = (after // n_sub, lax.rem(after, n_sub))
    before_id = (before // n_sub, lax.rem(before, n_sub))
    peers = [lax.rem(s + o, n_sub) for o in range(n_sub)]

    barrier = pltpu.get_barrier_semaphore()
    for o in (4, 3, 5, 2, 6, 1, 7):
        pl.semaphore_signal(barrier, inc=1, device_id=(m, peers[o]), device_id_type=MESH)
    for target in (after_id, before_id):
        pl.semaphore_signal(barrier, inc=1, device_id=target, device_id_type=MESH)

    loads = [
        pltpu.make_async_copy(source, target, load_sem.at[i])
        for i, (source, target) in enumerate(
            (
                (state_hbm, state_ref),
                (level_hbm, level_ref),
                (fine_hbm, fine_ref),
                (coarse_hbm, coarse_ref),
                (next_hbm, next_ref),
                (prev_hbm, prev_ref),
                (near_hbm, near_ref),
                (count_hbm, count_ref),
                (volume_hbm, volume_ref),
                (panel_hbm, panel_ref),
                (gather_hbm, gather_ref),
            )
        )
    ]
    for load in loads:
        load.start()
    for load in loads[0:8]:
        load.wait()

    level = level_ref[...]
    metric = 0.25 * jnp.left_shift(jnp.ones_like(level), level).astype(f32)
    near = near_ref[...]
    extra = near - 832
    panel_lane = 768 + (extra & 3) * 16 + ((extra >> 2) & 1) * 8 + (extra >> 3)
    entry = jnp.where(near >= 832, panel_lane, jnp.where(near >= 768, near + 64, near))
    lane = lax.broadcasted_iota(jnp.int32, (1, 128), 1)
    low_lanes = lane < 64
    counts = jnp.zeros((1, 128), jnp.int32)
    for p in range(n_sub):
        counts = jnp.where((lane & 7) == p, count_ref[0, p], counts)
    used = ((lane >> 3) & 1) < counts

    for f in range(5):
        x_ref[f, 0:125, :] = state_ref[f]
        x_ref[f, 125:128, :] = jnp.ones((3, 128), f32)
    for face in range(6):
        face_ref[face, 125:126, :] = jnp.full((1, 128), float(face // 2), f32)
        face_ref[face, 126:127, :] = metric
        face_ref[face, 127:128, :] = jnp.full((1, 128), 1.0 if face % 2 else -1.0, f32)
    numeric_ref[125:128, :] = jnp.zeros((3, 128), f32)
    passed_ref[125:128, :] = jnp.zeros((3, 128), f32)

    rows = lax.broadcasted_iota(jnp.int32, (16, 128), 0)
    lanes = lax.broadcasted_iota(jnp.int32, (16, 128), 1)

    def marks(slots, target_ref, at):
        column = jnp.full((16, 128), -1, jnp.int32)
        for r, slot in enumerate(slots):
            column = jnp.where(rows == r, slot, column)
        for face in range(6):
            hit = jnp.where(column == lanes + 128 * face, 1.0, 0.0).astype(bf16)
            for row in at:
                target_ref[row : row + 16, 128 * face : 128 * face + 128] = hit

    for b in range(4):
        list_ref = (next_ref, prev_ref)[b // 2]
        marks([list_ref[0, 16 * (b % 2) + i] for i in range(16)], send_pick_ref, [16 * b])
    for p in range(n_sub):
        marks(
            [fine_ref[0, r // 4, r % 4, p] for r in range(8)] + [coarse_ref[0, j, p] for j in range(2)],
            send_pick_ref,
            [64 + 16 * p],
        )

    def onto_planes(target_ref, face, f, value):
        level_at = 4 * (face % 2)
        if face < 2:
            plane = slice(25 * level_at, 25 * level_at + 25)
            target_ref[f, plane, :] = target_ref[f, plane, :] + value
        elif face < 4:
            for a in range(5):
                start = 25 * a + 5 * level_at
                plane = slice(start, start + 5)
                target_ref[f, plane, :] = target_ref[f, plane, :] + value[5 * a : 5 * a + 5, :]
        else:
            plane = pl.ds(level_at, 25, stride=5)
            target_ref[f, plane, :] = target_ref[f, plane, :] + value

    def store_added(product):
        added = both_halves(product)
        for face in range(6):
            added_ref[face] = added[:, 128 * face : 128 * face + 128]

    def panels_of(source):
        coarse_rows = jnp.concatenate([source[:, 8 + j, :] for j in range(2)], axis=0)
        high, low = split(coarse_rows)
        upper = jnp.concatenate([high, high], axis=1)
        lower = jnp.concatenate([low, jnp.zeros_like(low)], axis=1)
        wide = dot(jnp.concatenate([upper, lower], axis=0), panel_ref[...])
        wide = wide[0:16] + wide[16:32]
        return [wide[:, 128 * q : 128 * q + 128] for q in range(4)]

    gain = lift_gain * metric

    def section(step):
        for face in range(6):
            level_at = 4 * (face % 2)
            for f in range(5):
                base = 25 * f
                if face < 2:
                    face_ref[face, base : base + 25, :] = x_ref[f, 25 * level_at : 25 * level_at + 25, :]
                elif face < 4:
                    for a in range(5):
                        start = 25 * a + 5 * level_at
                        face_ref[face, base + 5 * a : base + 5 * a + 5, :] = x_ref[f, start : start + 5, :]
                else:
                    face_ref[face, base : base + 25, :] = x_ref[f, pl.ds(level_at, 25, stride=5), :]
        for face in range(6):
            high, low = split(face_ref[face])
            face_bf_ref[0:128, 128 * face : 128 * face + 128] = high
            face_bf_ref[128:256, 128 * face : 128 * face + 128] = low
        across = (((1,), (1,)), ((), ()))
        packed = lax.dot_general(
            send_pick_ref[...], face_bf_ref[...], across, preferred_element_type=f32
        )
        packed = packed[:, 0:128] + packed[:, 128:256]
        for p in range(n_sub):
            message_send[step, p] = packed[64 + 16 * p : 74 + 16 * p, :]
        for side in range(2):
            ring_send[step, side] = packed[32 * side : 32 * side + 32, :]
        if step == 0:
            pl.semaphore_wait(barrier, n_sub + 1)
        messages = []
        for o in (4,):
            copy = pltpu.make_async_remote_copy(
                src_ref=message_send.at[step, peers[o]],
                dst_ref=message_recv.at[step, s],
                send_sem=send_sem.at[step, o],
                recv_sem=recv_sem.at[step, o],
                device_id=(m, peers[o]),
                device_id_type=MESH,
            )
            copy.start()
            messages.append(copy)
        rings = []
        for side, target in enumerate((after_id, before_id)):
            copy = pltpu.make_async_remote_copy(
                src_ref=ring_send.at[step, side],
                dst_ref=ring_recv.at[step, side],
                send_sem=send_sem.at[step, n_sub + side],
                recv_sem=recv_sem.at[step, n_sub + side],
                device_id=target,
                device_id_type=MESH,
            )
            copy.start()
            rings.append(copy)
        for o in (3, 5, 2, 6, 1, 7):
            copy = pltpu.make_async_remote_copy(
                src_ref=message_send.at[step, peers[o]],
                dst_ref=message_recv.at[step, s],
                send_sem=send_sem.at[step, o],
                recv_sem=recv_sem.at[step, o],
                device_id=(m, peers[o]),
                device_id_type=MESH,
            )
            copy.start()
            messages.append(copy)
        message_recv[step, s] = message_send[step, s]

        if step == 0:
            for load in loads[8:11]:
                load.wait()
        else:
            for face in range(6):
                for f in range(5):
                    onto_planes(rate_ref, face, f, gain * added_ref[face, 25 * f : 25 * f + 25, :])
            for f in range(5):
                first_ref[f] = (section_a2 * step_size) * rate_ref[f]
        fields = [x_ref[f] for f in range(5)]
        inverse, pressure = gas_state(fields)
        for d in range(3):
            components, unused = flux_along(fields, d, inverse, pressure)
            for f in range(5):
                high, low = split(components[f])
                flux_high_ref[128 * d : 128 * d + 128, 128 * f : 128 * f + 128] = high
                flux_low_ref[128 * d : 128 * d + 128, 128 * f : 128 * f + 128] = low
        for f in range(5):
            high, low = split(viscosity * metric * fields[f])
            flux_high_ref[384:512, 128 * f : 128 * f + 128] = high
            flux_low_ref[384:512, 128 * f : 128 * f + 128] = low
        total = both_halves(dot(volume_ref[...], flux_high_ref[...]))
        total = total + dot(volume_ref[0:128, :], flux_low_ref[...])
        for f in range(5):
            rate_ref[f] = metric * total[:, 128 * f : 128 * f + 128]

        if step == 0:
            for face in range(6):
                wanted = entry[face : face + 1, :]
                for block in range(56):
                    pick_ref[16 * block : 16 * block + 16, 128 * face : 128 * face + 128] = jnp.where(
                        rows + 16 * block == wanted, 1.0, 0.0
                    ).astype(bf16)
            spread_ref[0:64, :] = pick_ref[768:832, :]
            spread_ref[128:256, :] = pick_ref[768:896, :]
            owned = [
                jnp.where(j < count_ref[0, p], coarse_ref[0, j, p], -1) for j in range(2) for p in range(n_sub)
            ]
            marks(owned, spread_ref, [64, 80, 96, 112])
        local = both_halves(dot(face_bf_ref[...], pick_ref[0:768, :]))
        for face in range(6):
            outside_ref[face] = local[:, 128 * face : 128 * face + 128]
        inner_ref[...] = both_halves(
            lax.dot_general(face_bf_ref[...], pick_ref[768:896, :], across, preferred_element_type=f32)
        )
        own = jnp.concatenate([jnp.zeros((64, 128), f32)] + panels_of(message_send.at[step]), axis=0).T
        known_ref[...] = jnp.where(low_lanes, inner_ref[...], own)
        inner_facts = [inner_ref[125 + i : 126 + i, :] for i in range(3)]

        for face in range(6):
            d = face // 2
            orient_here = 1.0 if face % 2 else -1.0
            inside = face_fields(face_ref.at[face])
            beyond = face_fields(outside_ref.at[face])
            coupled = (near[face : face + 1, :] >= 0) & (near[face : face + 1, :] < 768)
            inverse, pressure = gas_state(inside)
            flux_in, velocity = flux_along(inside, d, inverse, pressure)
            speed_in = jnp.abs(velocity) + sound_speed(inverse, pressure)
            inverse, pressure = gas_state(beyond)
            flux_out, velocity = flux_along(beyond, d, inverse, pressure)
            speed_out = jnp.abs(velocity) + sound_speed(inverse, pressure)
            damping = 0.5 * jnp.maximum(speed_in, speed_out) + penalty * metric
            for f in range(5):
                value = 0.5 * orient_here * (flux_in[f] + flux_out[f]) + damping * (inside[f] - beyond[f])
                surface = orient_here * flux_in[f] - jnp.where(coupled, value, 0.0)
                onto_planes(rate_ref, face, f, gain * surface)
        if step == 0:
            for f in range(5):
                x_ref[f] = x_ref[f] + (section_b1 * step_size) * rate_ref[f]

        known = face_fields(known_ref)
        known_parts = mortar_part(known)
        inside = face_fields(inner_ref)
        flux_in, speed_in = flux_by_lane(inside, mortar_part(inside), inner_facts[0])
        for copy in rings + messages:
            copy.wait_recv()
        panels = panels_of(message_recv.at[step])
        ring_ref[...] = jnp.concatenate(
            [jnp.zeros((64, 128), f32), ring_recv[step, 0], ring_recv[step, 1]], axis=0
        ).T
        fine_rows = [message_recv[step, :, 4 * j + q, :] for q in range(4) for j in range(2)]
        arrived_ref[...] = jnp.concatenate(panels + fine_rows, axis=0).T
        facts = [
            jnp.where(low_lanes, x, arrived_ref[125 + i : 126 + i, :]) for i, x in enumerate(inner_facts)
        ]
        along, scale, orient = facts
        valid = jnp.where(low_lanes, orient, jnp.where(used, 1.0, 0.0)) != 0.0
        arrived = face_fields(arrived_ref)
        flux_new, speed_new = flux_by_lane(arrived, mortar_part(arrived), along)
        flux_old, speed_old = flux_by_lane(known, known_parts, along)
        damping = 0.5 * jnp.maximum(speed_new, speed_old) + penalty * scale
        damping = jnp.where(low_lanes, -damping, damping)
        for f in range(5):
            value = 0.5 * orient * (flux_new[f] + flux_old[f]) + damping * (arrived[f] - known[f])
            numeric_ref[25 * f : 25 * f + 25, :] = value
        numeric = numeric_ref[...]
        high = numeric.astype(bf16).astype(f32)
        mixed = jnp.where(low_lanes, pltpu.roll(numeric - high, 64, 1), high)
        panel_of = jnp.where(low_lanes, lane, lane - 64) >> 4
        parts = [jnp.where(panel_of == q, mixed, 0.0) for q in range(4)]
        parts = parts + [jnp.where((panel_of == q) & ~low_lanes, high, 0.0) for q in range(4)]
        chosen = dot(gather_ref[...], jnp.concatenate(parts, axis=0).astype(bf16))
        beyond = face_fields(ring_ref)
        along, scale, orient = inner_facts
        flux_out, speed_out = flux_by_lane(beyond, mortar_part(beyond), along)
        damping = 0.5 * jnp.maximum(speed_in, speed_out) + penalty * scale
        for f in range(5):
            value = 0.5 * orient * (flux_in[f] + flux_out[f]) + damping * (inside[f] - beyond[f])
            passed_ref[25 * f : 25 * f + 25, :] = jnp.where(low_lanes, 0.0, -value)
        ready = jnp.where(low_lanes, -numeric, chosen + pltpu.roll(chosen, 64, 1))
        ready = jnp.where(valid, ready, 0.0)
        high, low = split(jnp.concatenate([ready, passed_ref[...]], axis=1))
        store_added(dot(jnp.concatenate([high, low], axis=0), spread_ref[...]))
        if step == 0:
            gain_now = (section_b1 * step_size * lift_gain) * metric
            for face in range(6):
                for f in range(5):
                    onto_planes(x_ref, face, f, gain_now * added_ref[face, 25 * f : 25 * f + 25, :])
        else:
            for face in range(6):
                for f in range(5):
                    onto_planes(rate_ref, face, f, gain * added_ref[face, 25 * f : 25 * f + 25, :])
        return rings + messages

    copies = section(0)
    copies = copies + section(1)
    for copy in copies:
        copy.wait_send()


def finish(x_ref, first_ref, rate_ref, out_hbm, register_hbm, out_ref, register_ref, sem):
    copies = []
    for f in range(5):
        register = first_ref[f, 0:125, :] + step_size * rate_ref[f, 0:125, :]
        register_ref[f] = register
        out_ref[f] = x_ref[f, 0:125, :] + section_b2 * register
        copies.append(pltpu.make_async_copy(register_ref.at[f], register_hbm.at[f], sem.at[0, f]))
        copies.append(pltpu.make_async_copy(out_ref.at[f], out_hbm.at[f], sem.at[1, f]))
        for copy in copies[-2:]:
            copy.start()
    for copy in copies:
        copy.wait()


def per_device(mesh_shape, flow_state, element_level, neighbour, send_next, send_prev, coarse_face, fine_face, send_count):
    n_morton, n_sub = mesh_shape
    volume, panel, gather = (jnp.asarray(t) for t in operator_tables())
    vmem = pl.BlockSpec(memory_space=pltpu.VMEM)
    hbm = pl.BlockSpec(memory_space=pltpu.HBM)
    shape = jax.ShapeDtypeStruct(flow_state.shape, f32)
    block = jax.ShapeDtypeStruct((5, 128, 128), f32)
    operands = (
        flow_state,
        element_level.reshape(1, -1),
        neighbour,
        send_next,
        send_prev,
        jnp.transpose(coarse_face, (0, 2, 1)),
        jnp.transpose(fine_face, (0, 2, 3, 1)),
        send_count,
        volume,
        panel,
        gather,
    )
    spaces = [pltpu.VMEM] * 3 + [pltpu.SMEM] * 5 + [pltpu.VMEM] * 3
    pieces = pl.pallas_call(
        functools.partial(kernel, n_morton, n_sub),
        out_shape=(block, block, block),
        in_specs=[hbm] * len(operands),
        out_specs=(vmem, vmem, vmem),
        scratch_shapes=[space(x.shape, x.dtype) for space, x in zip(spaces, operands)]
        + [
            pltpu.SemaphoreType.DMA((len(operands),)),
            pltpu.VMEM((6, 128, 128), f32),
            pltpu.VMEM((256, 768), bf16),
            pltpu.VMEM((896, 768), bf16),
            pltpu.VMEM((256, 768), bf16),
            pltpu.VMEM((192, 768), bf16),
            pltpu.VMEM((6, 128, 128), f32),
            pltpu.VMEM((6, 128, 128), f32),
            pltpu.VMEM((512, 640), bf16),
            pltpu.VMEM((512, 640), bf16),
            pltpu.VMEM((128, 128), f32),
            pltpu.VMEM((128, 128), f32),
            pltpu.VMEM((128, 128), f32),
            pltpu.VMEM((128, 128), f32),
            pltpu.VMEM((128, 128), f32),
            pltpu.VMEM((128, 128), f32),
            pltpu.VMEM((2, 2, 32, 128), f32),
            pltpu.VMEM((2, 2, 32, 128), f32),
            pltpu.VMEM((2, n_sub, 10, 128), f32),
            pltpu.VMEM((2, n_sub, 10, 128), f32),
            pltpu.SemaphoreType.DMA((2, n_sub + 2)),
            pltpu.SemaphoreType.DMA((2, n_sub + 2)),
        ],
        compiler_params=pltpu.CompilerParams(
            collective_id=0, has_side_effects=True, vmem_limit_bytes=40 * 1024 * 1024
        ),
    )(*[pltpu.with_memory_space_constraint(x, pltpu.HBM) for x in operands])
    return pl.pallas_call(
        finish,
        out_shape=(shape, shape),
        in_specs=[vmem, vmem, vmem],
        out_specs=(hbm, hbm),
        scratch_shapes=[
            pltpu.VMEM(flow_state.shape, f32),
            pltpu.VMEM(flow_state.shape, f32),
            pltpu.SemaphoreType.DMA((2, 5)),
        ],
        compiler_params=pltpu.CompilerParams(vmem_limit_bytes=16 * 1024 * 1024),
    )(*pieces)


def solution(mesh):
    whole = ("morton", "sub")
    placed = (
        P(None, None, whole),
        P(whole),
        P(None, whole),
        P(whole, None),
        P(whole, None),
        P(whole, None, None),
        P(whole, None, None, None),
        P(whole, None),
    )
    mesh_shape = (mesh.shape["morton"], mesh.shape["sub"])
    return jax.shard_map(
        functools.partial(per_device, mesh_shape),
        mesh=mesh,
        in_specs=placed,
        out_specs=(P(None, None, whole), P(None, None, whole)),
        check_vma=False,
    )
```

```python
import functools

import jax
import jax.numpy as jnp
import numpy as np
from jax import lax
from jax.experimental import pallas as pl
from jax.experimental.pallas import tpu as pltpu
from jax.sharding import PartitionSpec as P

gamma_gas = 1.4
viscosity = 0.01
penalty = 0.1
lift_gain = 10.0
step_size = 0.05
section_a2 = -0.4178904745
section_b1 = 0.1496590219993
section_b2 = 0.3792103129999
MESH = pl.DeviceIdType.MESH
f32 = jnp.float32
bf16 = jnp.bfloat16


def basis_tables():
    points = np.array([-1.0, -np.sqrt(3.0 / 7.0), 0.0, np.sqrt(3.0 / 7.0), 1.0])
    weights = np.array([0.1, 49.0 / 90.0, 32.0 / 45.0, 49.0 / 90.0, 0.1])
    products = np.array(
        [np.prod([points[i] - points[m] for m in range(5) if m != i]) for i in range(5)]
    )
    derivative = np.zeros((5, 5))
    for i in range(5):
        for j in range(5):
            if i != j:
                derivative[i, j] = products[i] / (products[j] * (points[i] - points[j]))
        derivative[i, i] = -np.sum(derivative[i])
    halves = []
    projections = []
    for h in range(2):
        shifted = (points + 2.0 * h - 1.0) / 2.0
        interp = np.zeros((5, 5))
        for i in range(5):
            for j in range(5):
                interp[i, j] = np.prod(
                    [(shifted[i] - points[m]) / (points[j] - points[m]) for m in range(5) if m != j]
                )
        halves.append(interp)
        projections.append(weights[None, :] * interp.T / (2.0 * weights[:, None]))
    interpolation = np.stack([np.kron(halves[q // 2], halves[q % 2]) for q in range(4)])
    projection = np.stack([np.kron(projections[q // 2], projections[q % 2]) for q in range(4)])
    ident_five = np.eye(5)
    ident_quad = np.eye(25)
    gradients = np.stack(
        [
            np.kron(derivative, ident_quad),
            np.kron(ident_five, np.kron(derivative, ident_five)),
            np.kron(ident_quad, derivative),
        ]
    )
    laplace = (
        gradients[0] @ gradients[0] + gradients[1] @ gradients[1] + gradients[2] @ gradients[2]
    )
    return interpolation, projection, gradients, laplace


def two_parts(table):
    table = table.astype(np.float32)
    high = table.astype(jnp.bfloat16)
    low = (table - high.astype(np.float32)).astype(jnp.bfloat16)
    return np.stack([high, low])


def operator_tables():
    interpolation, projection, gradients, laplace = basis_tables()
    volume = np.zeros((128, 512))
    for d in range(3):
        volume[:125, 128 * d : 128 * d + 125] = -gradients[d]
    volume[:125, 384:509] = laplace
    panel = np.zeros((128, 512))
    gather = np.zeros((512, 128))
    for q in range(4):
        for f in range(5):
            rows = slice(25 * f, 25 * f + 25)
            columns = slice(128 * q + 25 * f, 128 * q + 25 * f + 25)
            panel[rows, columns] = interpolation[q].T
            gather[columns, rows] = projection[q]
    beside = two_parts(gather).reshape(8, 128, 128).transpose(1, 0, 2).reshape(128, 1024)
    return two_parts(volume).reshape(256, 512), two_parts(panel).reshape(256, 512), beside


def split(x):
    high = x.astype(bf16)
    low = (x - high.astype(f32)).astype(bf16)
    return high, low


def dot(a, b):
    return jnp.dot(a, b, preferred_element_type=f32)


def gas_state(fields):
    inverse = 1.0 / fields[0]
    kinetic = fields[1] * fields[1] + fields[2] * fields[2] + fields[3] * fields[3]
    pressure = (gamma_gas - 1.0) * (fields[4] - 0.5 * kinetic * inverse)
    return inverse, pressure


def flux_along(fields, d, inverse, pressure):
    velocity = fields[1 + d] * inverse
    components = [
        fields[1 + d],
        fields[1] * velocity,
        fields[2] * velocity,
        fields[3] * velocity,
        (fields[4] + pressure) * velocity,
    ]
    components[1 + d] = components[1 + d] + pressure
    return components, velocity


def sound_speed(inverse, pressure):
    return jnp.sqrt(gamma_gas * pressure * inverse)


def mortar_part(fields):
    inverse, pressure = gas_state(fields)
    return inverse, pressure, sound_speed(inverse, pressure)


def flux_by_lane(fields, parts, along):
    inverse, pressure, sound = parts
    normal = jnp.where(along < 0.5, fields[1], jnp.where(along < 1.5, fields[2], fields[3]))
    velocity = normal * inverse
    components = [
        normal,
        fields[1] * velocity + jnp.where(along < 0.5, pressure, 0.0),
        fields[2] * velocity + jnp.where((along > 0.5) & (along < 1.5), pressure, 0.0),
        fields[3] * velocity + jnp.where(along > 1.5, pressure, 0.0),
        (fields[4] + pressure) * velocity,
    ]
    return components, jnp.abs(velocity) + sound


def face_fields(ref):
    return [ref[25 * f : 25 * f + 25, :] for f in range(5)]


def both_halves(x):
    return x[0:128] + x[128:256]


def kernel(
    n_morton,
    n_sub,
    state_hbm,
    level_hbm,
    near_hbm,
    next_hbm,
    prev_hbm,
    coarse_hbm,
    fine_hbm,
    count_hbm,
    volume_hbm,
    panel_hbm,
    gather_hbm,
    x_ref,
    first_ref,
    rate_ref,
    state_ref,
    level_ref,
    near_ref,
    next_ref,
    prev_ref,
    coarse_ref,
    fine_ref,
    count_ref,
    volume_ref,
    panel_ref,
    gather_ref,
    load_sem,
    face_ref,
    face_bf_ref,
    pick_ref,
    spread_ref,
    send_pick_ref,
    outside_ref,
    added_ref,
    flux_high_ref,
    flux_low_ref,
    inner_ref,
    ring_ref,
    known_ref,
    arrived_ref,
    numeric_ref,
    passed_ref,
    ring_send,
    ring_recv,
    message_send,
    message_recv,
    relay_ref,
    relay_sem,
    send_sem,
    recv_sem,
):
    m = lax.axis_index("morton")
    s = lax.axis_index("sub")
    devices = n_morton * n_sub
    place = m * n_sub + s
    after = lax.rem(place + 1, devices)
    before = lax.rem(place + devices - 1, devices)
    after_id = (after // n_sub, lax.rem(after, n_sub))
    before_id = (before // n_sub, lax.rem(before, n_sub))
    peers = [lax.rem(s + o, n_sub) for o in range(n_sub)]

    barrier = pltpu.get_barrier_semaphore()
    for o in (4, 3, 5, 2, 6, 1, 7):
        pl.semaphore_signal(barrier, inc=1, device_id=(m, peers[o]), device_id_type=MESH)
    group_before = (lax.rem(m + n_morton - 1, n_morton), 0)
    group_after = (lax.rem(m + 1, n_morton), 0)

    @pl.when(s == 0)
    def greet_groups():
        for target in (before_id, group_after):
            pl.semaphore_signal(barrier, inc=1, device_id=target, device_id_type=MESH)


    loads = [
        pltpu.make_async_copy(source, target, load_sem.at[i])
        for i, (source, target) in enumerate(
            (
                (state_hbm, state_ref),
                (level_hbm, level_ref),
                (fine_hbm, fine_ref),
                (coarse_hbm, coarse_ref),
                (next_hbm, next_ref),
                (prev_hbm, prev_ref),
                (near_hbm, near_ref),
                (count_hbm, count_ref),
                (volume_hbm, volume_ref),
                (panel_hbm, panel_ref),
                (gather_hbm, gather_ref),
            )
        )
    ]
    for load in loads:
        load.start()
    for load in loads[0:8]:
        load.wait()

    level = level_ref[...]
    metric = 0.25 * jnp.left_shift(jnp.ones_like(level), level).astype(f32)
    near = near_ref[...]
    extra = near - 832
    panel_lane = 768 + (extra & 3) * 16 + ((extra >> 2) & 1) * 8 + (extra >> 3)
    entry = jnp.where(near >= 832, panel_lane, jnp.where(near >= 768, near + 64, near))
    lane = lax.broadcasted_iota(jnp.int32, (1, 128), 1)
    low_lanes = lane < 64
    counts = jnp.zeros((1, 128), jnp.int32)
    for p in range(n_sub):
        counts = jnp.where((lane & 7) == p, count_ref[0, p], counts)
    used = ((lane >> 3) & 1) < counts

    for f in range(5):
        x_ref[f, 0:125, :] = state_ref[f]
        x_ref[f, 125:128, :] = jnp.ones((3, 128), f32)
    for face in range(6):
        face_ref[face, 125:126, :] = jnp.full((1, 128), float(face // 2), f32)
        face_ref[face, 126:127, :] = metric
        face_ref[face, 127:128, :] = jnp.full((1, 128), 1.0 if face % 2 else -1.0, f32)
    numeric_ref[125:128, :] = jnp.zeros((3, 128), f32)
    passed_ref[125:128, :] = jnp.zeros((3, 128), f32)

    rows = lax.broadcasted_iota(jnp.int32, (16, 128), 0)
    lanes = lax.broadcasted_iota(jnp.int32, (16, 128), 1)

    def marks(slots, target_ref, at):
        column = jnp.full((16, 128), -1, jnp.int32)
        for r, slot in enumerate(slots):
            column = jnp.where(rows == r, slot, column)
        for face in range(6):
            hit = jnp.where(column == lanes + 128 * face, 1.0, 0.0).astype(bf16)
            for row in at:
                target_ref[row : row + 16, 128 * face : 128 * face + 128] = hit

    for b in range(4):
        list_ref = (next_ref, prev_ref)[b // 2]
        marks([list_ref[0, 16 * (b % 2) + i] for i in range(16)], send_pick_ref, [16 * b])
    for p in range(n_sub):
        marks(
            [fine_ref[0, r // 4, r % 4, p] for r in range(8)] + [coarse_ref[0, j, p] for j in range(2)],
            send_pick_ref,
            [64 + 16 * p],
        )

    def onto_planes(target_ref, face, f, value):
        level_at = 4 * (face % 2)
        if face < 2:
            plane = slice(25 * level_at, 25 * level_at + 25)
            target_ref[f, plane, :] = target_ref[f, plane, :] + value
        elif face < 4:
            for a in range(5):
                start = 25 * a + 5 * level_at
                plane = slice(start, start + 5)
                target_ref[f, plane, :] = target_ref[f, plane, :] + value[5 * a : 5 * a + 5, :]
        else:
            plane = pl.ds(level_at, 25, stride=5)
            target_ref[f, plane, :] = target_ref[f, plane, :] + value

    def store_added(product):
        added = both_halves(product)
        for face in range(6):
            added_ref[face] = added[:, 128 * face : 128 * face + 128]

    def panels_of(source):
        coarse_rows = jnp.concatenate([source[:, 8 + j, :] for j in range(2)], axis=0)
        high, low = split(coarse_rows)
        upper = jnp.concatenate([high, high], axis=1)
        lower = jnp.concatenate([low, jnp.zeros_like(low)], axis=1)
        wide = dot(jnp.concatenate([upper, lower], axis=0), panel_ref[...])
        wide = wide[0:16] + wide[16:32]
        return [wide[:, 128 * q : 128 * q + 128] for q in range(4)]

    gain = lift_gain * metric

    def section(step):
        for face in range(6):
            level_at = 4 * (face % 2)
            for f in range(5):
                base = 25 * f
                if face < 2:
                    face_ref[face, base : base + 25, :] = x_ref[f, 25 * level_at : 25 * level_at + 25, :]
                elif face < 4:
                    for a in range(5):
                        start = 25 * a + 5 * level_at
                        face_ref[face, base + 5 * a : base + 5 * a + 5, :] = x_ref[f, start : start + 5, :]
                else:
                    face_ref[face, base : base + 25, :] = x_ref[f, pl.ds(level_at, 25, stride=5), :]
        for face in range(6):
            high, low = split(face_ref[face])
            face_bf_ref[0:128, 128 * face : 128 * face + 128] = high
            face_bf_ref[128:256, 128 * face : 128 * face + 128] = low
        across = (((1,), (1,)), ((), ()))
        packed = lax.dot_general(
            send_pick_ref[...], face_bf_ref[...], across, preferred_element_type=f32
        )
        packed = packed[:, 0:128] + packed[:, 128:256]
        for p in range(n_sub):
            message_send[step, p] = packed[64 + 16 * p : 74 + 16 * p, :]
        for side in range(2):
            ring_send[step, side] = packed[32 * side : 32 * side + 32, :]
        if step == 0:
            pl.semaphore_wait(barrier, n_sub - 1 + (1 - (s + n_sub - 1) // n_sub) + (s + 1) // n_sub)
        messages = []
        for o in (4,):
            copy = pltpu.make_async_remote_copy(
                src_ref=message_send.at[step, peers[o]],
                dst_ref=message_recv.at[step, s],
                send_sem=send_sem.at[step, o],
                recv_sem=recv_sem.at[step, o],
                device_id=(m, peers[o]),
                device_id_type=MESH,
            )
            copy.start()
            messages.append(copy)
        rings = []
        for side, target in enumerate((after_id, before_id)):
            copy = pltpu.make_async_remote_copy(
                src_ref=ring_send.at[step, side],
                dst_ref=ring_recv.at[step, side],
                send_sem=send_sem.at[step, n_sub + side],
                recv_sem=recv_sem.at[step, n_sub + side],
                device_id=target,
                device_id_type=MESH,
            )
            rings.append(copy)
            if step == 0 and side == 1:
                relay = pltpu.make_async_remote_copy(
                    src_ref=ring_send.at[0, 1],
                    dst_ref=relay_ref,
                    send_sem=send_sem.at[0, n_sub + 1],
                    recv_sem=relay_sem.at[0],
                    device_id=group_before,
                    device_id_type=MESH,
                )
                pl.when(s == 0)(relay.start)
                pl.when(s > 0)(copy.start)
            else:
                copy.start()
        for o in (3, 5, 2, 6, 1, 7):
            copy = pltpu.make_async_remote_copy(
                src_ref=message_send.at[step, peers[o]],
                dst_ref=message_recv.at[step, s],
                send_sem=send_sem.at[step, o],
                recv_sem=recv_sem.at[step, o],
                device_id=(m, peers[o]),
                device_id_type=MESH,
            )
            copy.start()
            messages.append(copy)
        message_recv[step, s] = message_send[step, s]

        if step == 0:
            for load in loads[8:11]:
                load.wait()
        else:
            for face in range(6):
                for f in range(5):
                    onto_planes(rate_ref, face, f, gain * added_ref[face, 25 * f : 25 * f + 25, :])
            for f in range(5):
                first_ref[f] = (section_a2 * step_size) * rate_ref[f]
        fields = [x_ref[f] for f in range(5)]
        inverse, pressure = gas_state(fields)
        for d in range(3):
            components, unused = flux_along(fields, d, inverse, pressure)
            for f in range(5):
                high, low = split(components[f])
                flux_high_ref[128 * d : 128 * d + 128, 128 * f : 128 * f + 128] = high
                flux_low_ref[128 * d : 128 * d + 128, 128 * f : 128 * f + 128] = low
        for f in range(5):
            high, low = split(viscosity * metric * fields[f])
            flux_high_ref[384:512, 128 * f : 128 * f + 128] = high
            flux_low_ref[384:512, 128 * f : 128 * f + 128] = low
        total = both_halves(dot(volume_ref[...], flux_high_ref[...]))
        total = total + dot(volume_ref[0:128, :], flux_low_ref[...])
        for f in range(5):
            rate_ref[f] = metric * total[:, 128 * f : 128 * f + 128]

        if step == 0:
            for face in range(6):
                wanted = entry[face : face + 1, :]
                for block in range(56):
                    pick_ref[16 * block : 16 * block + 16, 128 * face : 128 * face + 128] = jnp.where(
                        rows + 16 * block == wanted, 1.0, 0.0
                    ).astype(bf16)
            spread_ref[0:64, :] = pick_ref[768:832, :]
            spread_ref[128:256, :] = pick_ref[768:896, :]
            owned = [
                jnp.where(j < count_ref[0, p], coarse_ref[0, j, p], -1) for j in range(2) for p in range(n_sub)
            ]
            marks(owned, spread_ref, [64, 80, 96, 112])
        local = both_halves(dot(face_bf_ref[...], pick_ref[0:768, :]))
        for face in range(6):
            outside_ref[face] = local[:, 128 * face : 128 * face + 128]
        inner_ref[...] = both_halves(
            lax.dot_general(face_bf_ref[...], pick_ref[768:896, :], across, preferred_element_type=f32)
        )
        own = jnp.concatenate([jnp.zeros((64, 128), f32)] + panels_of(message_send.at[step]), axis=0).T
        known_ref[...] = jnp.where(low_lanes, inner_ref[...], own)
        inner_facts = [inner_ref[125 + i : 126 + i, :] for i in range(3)]

        for face in range(6):
            d = face // 2
            orient_here = 1.0 if face % 2 else -1.0
            inside = face_fields(face_ref.at[face])
            beyond = face_fields(outside_ref.at[face])
            coupled = (near[face : face + 1, :] >= 0) & (near[face : face + 1, :] < 768)
            inverse, pressure = gas_state(inside)
            flux_in, velocity = flux_along(inside, d, inverse, pressure)
            speed_in = jnp.abs(velocity) + sound_speed(inverse, pressure)
            inverse, pressure = gas_state(beyond)
            flux_out, velocity = flux_along(beyond, d, inverse, pressure)
            speed_out = jnp.abs(velocity) + sound_speed(inverse, pressure)
            damping = 0.5 * jnp.maximum(speed_in, speed_out) + penalty * metric
            for f in range(5):
                value = 0.5 * orient_here * (flux_in[f] + flux_out[f]) + damping * (inside[f] - beyond[f])
                surface = orient_here * flux_in[f] - jnp.where(coupled, value, 0.0)
                onto_planes(rate_ref, face, f, gain * surface)
        if step == 0:
            for f in range(5):
                x_ref[f] = x_ref[f] + (section_b1 * step_size) * rate_ref[f]

        known = face_fields(known_ref)
        known_parts = mortar_part(known)
        inside = face_fields(inner_ref)
        flux_in, speed_in = flux_by_lane(inside, mortar_part(inside), inner_facts[0])
        if step == 0:
            passed_on = pltpu.make_async_remote_copy(
                src_ref=relay_ref,
                dst_ref=ring_recv.at[0, 1],
                send_sem=relay_sem.at[1],
                recv_sem=recv_sem.at[0, n_sub + 1],
                device_id=(m, n_sub - 1),
                device_id_type=MESH,
            )

            @pl.when(s == 0)
            def pass_on():
                relay.wait_recv()
                passed_on.start()

        for copy in rings + messages:
            copy.wait_recv()
        panels = panels_of(message_recv.at[step])
        ring_ref[...] = jnp.concatenate(
            [jnp.zeros((64, 128), f32), ring_recv[step, 0], ring_recv[step, 1]], axis=0
        ).T
        fine_rows = [message_recv[step, :, 4 * j + q, :] for q in range(4) for j in range(2)]
        arrived_ref[...] = jnp.concatenate(panels + fine_rows, axis=0).T
        facts = [
            jnp.where(low_lanes, x, arrived_ref[125 + i : 126 + i, :]) for i, x in enumerate(inner_facts)
        ]
        along, scale, orient = facts
        valid = jnp.where(low_lanes, orient, jnp.where(used, 1.0, 0.0)) != 0.0
        arrived = face_fields(arrived_ref)
        flux_new, speed_new = flux_by_lane(arrived, mortar_part(arrived), along)
        flux_old, speed_old = flux_by_lane(known, known_parts, along)
        damping = 0.5 * jnp.maximum(speed_new, speed_old) + penalty * scale
        damping = jnp.where(low_lanes, -damping, damping)
        for f in range(5):
            value = 0.5 * orient * (flux_new[f] + flux_old[f]) + damping * (arrived[f] - known[f])
            numeric_ref[25 * f : 25 * f + 25, :] = value
        numeric = numeric_ref[...]
        high = numeric.astype(bf16).astype(f32)
        mixed = jnp.where(low_lanes, pltpu.roll(numeric - high, 64, 1), high)
        panel_of = jnp.where(low_lanes, lane, lane - 64) >> 4
        parts = [jnp.where(panel_of == q, mixed, 0.0) for q in range(4)]
        parts = parts + [jnp.where((panel_of == q) & ~low_lanes, high, 0.0) for q in range(4)]
        chosen = dot(gather_ref[...], jnp.concatenate(parts, axis=0).astype(bf16))
        beyond = face_fields(ring_ref)
        along, scale, orient = inner_facts
        flux_out, speed_out = flux_by_lane(beyond, mortar_part(beyond), along)
        damping = 0.5 * jnp.maximum(speed_in, speed_out) + penalty * scale
        for f in range(5):
            value = 0.5 * orient * (flux_in[f] + flux_out[f]) + damping * (inside[f] - beyond[f])
            passed_ref[25 * f : 25 * f + 25, :] = jnp.where(low_lanes, 0.0, -value)
        ready = jnp.where(low_lanes, -numeric, chosen + pltpu.roll(chosen, 64, 1))
        ready = jnp.where(valid, ready, 0.0)
        high, low = split(jnp.concatenate([ready, passed_ref[...]], axis=1))
        store_added(dot(jnp.concatenate([high, low], axis=0), spread_ref[...]))
        if step == 0:
            gain_now = (section_b1 * step_size * lift_gain) * metric
            for face in range(6):
                for f in range(5):
                    onto_planes(x_ref, face, f, gain_now * added_ref[face, 25 * f : 25 * f + 25, :])
        else:
            for face in range(6):
                for f in range(5):
                    onto_planes(rate_ref, face, f, gain * added_ref[face, 25 * f : 25 * f + 25, :])
        if step == 0:
            pl.when(s == 0)(passed_on.wait_send)
        return rings + messages

    copies = section(0)
    copies = copies + section(1)
    for copy in copies:
        copy.wait_send()


def finish(x_ref, first_ref, rate_ref, out_hbm, register_hbm, out_ref, register_ref, sem):
    copies = []
    for f in range(5):
        register = first_ref[f, 0:125, :] + step_size * rate_ref[f, 0:125, :]
        register_ref[f] = register
        out_ref[f] = x_ref[f, 0:125, :] + section_b2 * register
        copies.append(pltpu.make_async_copy(register_ref.at[f], register_hbm.at[f], sem.at[0, f]))
        copies.append(pltpu.make_async_copy(out_ref.at[f], out_hbm.at[f], sem.at[1, f]))
        for copy in copies[-2:]:
            copy.start()
    for copy in copies:
        copy.wait()


def per_device(mesh_shape, flow_state, element_level, neighbour, send_next, send_prev, coarse_face, fine_face, send_count):
    n_morton, n_sub = mesh_shape
    volume, panel, gather = (jnp.asarray(t) for t in operator_tables())
    vmem = pl.BlockSpec(memory_space=pltpu.VMEM)
    hbm = pl.BlockSpec(memory_space=pltpu.HBM)
    shape = jax.ShapeDtypeStruct(flow_state.shape, f32)
    block = jax.ShapeDtypeStruct((5, 128, 128), f32)
    operands = (
        flow_state,
        element_level.reshape(1, -1),
        neighbour,
        send_next,
        send_prev,
        jnp.transpose(coarse_face, (0, 2, 1)),
        jnp.transpose(fine_face, (0, 2, 3, 1)),
        send_count,
        volume,
        panel,
        gather,
    )
    spaces = [pltpu.VMEM] * 3 + [pltpu.SMEM] * 5 + [pltpu.VMEM] * 3
    pieces = pl.pallas_call(
        functools.partial(kernel, n_morton, n_sub),
        out_shape=(block, block, block),
        in_specs=[hbm] * len(operands),
        out_specs=(vmem, vmem, vmem),
        scratch_shapes=[space(x.shape, x.dtype) for space, x in zip(spaces, operands)]
        + [
            pltpu.SemaphoreType.DMA((len(operands),)),
            pltpu.VMEM((6, 128, 128), f32),
            pltpu.VMEM((256, 768), bf16),
            pltpu.VMEM((896, 768), bf16),
            pltpu.VMEM((256, 768), bf16),
            pltpu.VMEM((192, 768), bf16),
            pltpu.VMEM((6, 128, 128), f32),
            pltpu.VMEM((6, 128, 128), f32),
            pltpu.VMEM((512, 640), bf16),
            pltpu.VMEM((512, 640), bf16),
            pltpu.VMEM((128, 128), f32),
            pltpu.VMEM((128, 128), f32),
            pltpu.VMEM((128, 128), f32),
            pltpu.VMEM((128, 128), f32),
            pltpu.VMEM((128, 128), f32),
            pltpu.VMEM((128, 128), f32),
            pltpu.VMEM((2, 2, 32, 128), f32),
            pltpu.VMEM((2, 2, 32, 128), f32),
            pltpu.VMEM((2, n_sub, 10, 128), f32),
            pltpu.VMEM((2, n_sub, 10, 128), f32),
            pltpu.VMEM((32, 128), f32),
            pltpu.SemaphoreType.DMA((2,)),
            pltpu.SemaphoreType.DMA((2, n_sub + 2)),
            pltpu.SemaphoreType.DMA((2, n_sub + 2)),
        ],
        compiler_params=pltpu.CompilerParams(
            collective_id=0, has_side_effects=True, vmem_limit_bytes=40 * 1024 * 1024
        ),
    )(*[pltpu.with_memory_space_constraint(x, pltpu.HBM) for x in operands])
    return pl.pallas_call(
        finish,
        out_shape=(shape, shape),
        in_specs=[vmem, vmem, vmem],
        out_specs=(hbm, hbm),
        scratch_shapes=[
            pltpu.VMEM(flow_state.shape, f32),
            pltpu.VMEM(flow_state.shape, f32),
            pltpu.SemaphoreType.DMA((2, 5)),
        ],
        compiler_params=pltpu.CompilerParams(vmem_limit_bytes=16 * 1024 * 1024),
    )(*pieces)


def solution(mesh):
    whole = ("morton", "sub")
    placed = (
        P(None, None, whole),
        P(whole),
        P(None, whole),
        P(whole, None),
        P(whole, None),
        P(whole, None, None),
        P(whole, None, None, None),
        P(whole, None),
    )
    mesh_shape = (mesh.shape["morton"], mesh.shape["sub"])
    return jax.shard_map(
        functools.partial(per_device, mesh_shape),
        mesh=mesh,
        in_specs=placed,
        out_specs=(P(None, None, whole), P(None, None, whole)),
        check_vma=False,
    )
```

```python
import functools

import jax
import jax.numpy as jnp
import numpy as np
from jax import lax
from jax.experimental import pallas as pl
from jax.experimental.pallas import tpu as pltpu
from jax.sharding import PartitionSpec as P

gamma_gas = 1.4
viscosity = 0.01
penalty = 0.1
lift_gain = 10.0
step_size = 0.05
section_a2 = -0.4178904745
section_b1 = 0.1496590219993
section_b2 = 0.3792103129999
MESH = pl.DeviceIdType.MESH
f32 = jnp.float32
bf16 = jnp.bfloat16


def basis_tables():
    points = np.array([-1.0, -np.sqrt(3.0 / 7.0), 0.0, np.sqrt(3.0 / 7.0), 1.0])
    weights = np.array([0.1, 49.0 / 90.0, 32.0 / 45.0, 49.0 / 90.0, 0.1])
    products = np.array(
        [np.prod([points[i] - points[m] for m in range(5) if m != i]) for i in range(5)]
    )
    derivative = np.zeros((5, 5))
    for i in range(5):
        for j in range(5):
            if i != j:
                derivative[i, j] = products[i] / (products[j] * (points[i] - points[j]))
        derivative[i, i] = -np.sum(derivative[i])
    halves = []
    projections = []
    for h in range(2):
        shifted = (points + 2.0 * h - 1.0) / 2.0
        interp = np.zeros((5, 5))
        for i in range(5):
            for j in range(5):
                interp[i, j] = np.prod(
                    [(shifted[i] - points[m]) / (points[j] - points[m]) for m in range(5) if m != j]
                )
        halves.append(interp)
        projections.append(weights[None, :] * interp.T / (2.0 * weights[:, None]))
    interpolation = np.stack([np.kron(halves[q // 2], halves[q % 2]) for q in range(4)])
    projection = np.stack([np.kron(projections[q // 2], projections[q % 2]) for q in range(4)])
    ident_five = np.eye(5)
    ident_quad = np.eye(25)
    gradients = np.stack(
        [
            np.kron(derivative, ident_quad),
            np.kron(ident_five, np.kron(derivative, ident_five)),
            np.kron(ident_quad, derivative),
        ]
    )
    laplace = (
        gradients[0] @ gradients[0] + gradients[1] @ gradients[1] + gradients[2] @ gradients[2]
    )
    return interpolation, projection, gradients, laplace


def two_parts(table):
    table = table.astype(np.float32)
    high = table.astype(jnp.bfloat16)
    low = (table - high.astype(np.float32)).astype(jnp.bfloat16)
    return np.stack([high, low])


def operator_tables():
    interpolation, projection, gradients, laplace = basis_tables()
    volume = np.zeros((128, 512))
    for d in range(3):
        volume[:125, 128 * d : 128 * d + 125] = -gradients[d]
    volume[:125, 384:509] = laplace
    panel = np.zeros((128, 512))
    gather = np.zeros((512, 128))
    for q in range(4):
        for f in range(5):
            rows = slice(25 * f, 25 * f + 25)
            columns = slice(128 * q + 25 * f, 128 * q + 25 * f + 25)
            panel[rows, columns] = interpolation[q].T
            gather[columns, rows] = projection[q]
    beside = two_parts(gather).reshape(8, 128, 128).transpose(1, 0, 2).reshape(128, 1024)
    return two_parts(volume).reshape(256, 512), two_parts(panel).reshape(256, 512), beside


def split(x):
    high = x.astype(bf16)
    low = (x - high.astype(f32)).astype(bf16)
    return high, low


def dot(a, b):
    return jnp.dot(a, b, preferred_element_type=f32)


def gas_state(fields):
    inverse = 1.0 / fields[0]
    kinetic = fields[1] * fields[1] + fields[2] * fields[2] + fields[3] * fields[3]
    pressure = (gamma_gas - 1.0) * (fields[4] - 0.5 * kinetic * inverse)
    return inverse, pressure


def flux_along(fields, d, inverse, pressure):
    velocity = fields[1 + d] * inverse
    components = [
        fields[1 + d],
        fields[1] * velocity,
        fields[2] * velocity,
        fields[3] * velocity,
        (fields[4] + pressure) * velocity,
    ]
    components[1 + d] = components[1 + d] + pressure
    return components, velocity


def sound_speed(inverse, pressure):
    return jnp.sqrt(gamma_gas * pressure * inverse)


def mortar_part(fields):
    inverse, pressure = gas_state(fields)
    return inverse, pressure, sound_speed(inverse, pressure)


def flux_by_lane(fields, parts, along):
    inverse, pressure, sound = parts
    normal = jnp.where(along < 0.5, fields[1], jnp.where(along < 1.5, fields[2], fields[3]))
    velocity = normal * inverse
    components = [
        normal,
        fields[1] * velocity + jnp.where(along < 0.5, pressure, 0.0),
        fields[2] * velocity + jnp.where((along > 0.5) & (along < 1.5), pressure, 0.0),
        fields[3] * velocity + jnp.where(along > 1.5, pressure, 0.0),
        (fields[4] + pressure) * velocity,
    ]
    return components, jnp.abs(velocity) + sound


def face_fields(ref):
    return [ref[25 * f : 25 * f + 25, :] for f in range(5)]


def both_halves(x):
    return x[0:128] + x[128:256]


def kernel(
    n_morton,
    n_sub,
    state_hbm,
    level_hbm,
    near_hbm,
    next_hbm,
    prev_hbm,
    coarse_hbm,
    fine_hbm,
    count_hbm,
    volume_hbm,
    panel_hbm,
    gather_hbm,
    x_ref,
    first_ref,
    rate_ref,
    state_ref,
    level_ref,
    near_ref,
    next_ref,
    prev_ref,
    coarse_ref,
    fine_ref,
    count_ref,
    volume_ref,
    panel_ref,
    gather_ref,
    load_sem,
    face_ref,
    face_bf_ref,
    pick_ref,
    spread_ref,
    send_pick_ref,
    outside_ref,
    added_ref,
    flux_high_ref,
    flux_low_ref,
    inner_ref,
    ring_ref,
    known_ref,
    arrived_ref,
    numeric_ref,
    passed_ref,
    ring_send,
    ring_recv,
    message_send,
    message_recv,
    relay_ref,
    relay_sem,
    send_sem,
    recv_sem,
):
    m = lax.axis_index("morton")
    s = lax.axis_index("sub")
    devices = n_morton * n_sub
    place = m * n_sub + s
    after = lax.rem(place + 1, devices)
    before = lax.rem(place + devices - 1, devices)
    after_id = (after // n_sub, lax.rem(after, n_sub))
    before_id = (before // n_sub, lax.rem(before, n_sub))
    peers = [lax.rem(s + o, n_sub) for o in range(n_sub)]

    barrier = pltpu.get_barrier_semaphore()
    for o in (4, 3, 5, 2, 6, 1, 7):
        pl.semaphore_signal(barrier, inc=1, device_id=(m, peers[o]), device_id_type=MESH)
    first_place = place == 0
    relay_place = place == devices - n_sub

    @pl.when(s == 0)
    def greet_before():
        pl.semaphore_signal(barrier, inc=1, device_id=before_id, device_id_type=MESH)

    @pl.when((s == n_sub - 1) & (place < devices - 1))
    def greet_after():
        pl.semaphore_signal(barrier, inc=1, device_id=after_id, device_id_type=MESH)

    @pl.when(relay_place)
    def greet_first():
        pl.semaphore_signal(barrier, inc=1, device_id=(0, 0), device_id_type=MESH)

    loads = [
        pltpu.make_async_copy(source, target, load_sem.at[i])
        for i, (source, target) in enumerate(
            (
                (state_hbm, state_ref),
                (level_hbm, level_ref),
                (fine_hbm, fine_ref),
                (coarse_hbm, coarse_ref),
                (next_hbm, next_ref),
                (prev_hbm, prev_ref),
                (near_hbm, near_ref),
                (count_hbm, count_ref),
                (volume_hbm, volume_ref),
                (panel_hbm, panel_ref),
                (gather_hbm, gather_ref),
            )
        )
    ]
    for load in loads:
        load.start()
    for load in loads[0:8]:
        load.wait()

    level = level_ref[...]
    metric = 0.25 * jnp.left_shift(jnp.ones_like(level), level).astype(f32)
    near = near_ref[...]
    extra = near - 832
    panel_lane = 768 + (extra & 3) * 16 + ((extra >> 2) & 1) * 8 + (extra >> 3)
    entry = jnp.where(near >= 832, panel_lane, jnp.where(near >= 768, near + 64, near))
    lane = lax.broadcasted_iota(jnp.int32, (1, 128), 1)
    low_lanes = lane < 64
    counts = jnp.zeros((1, 128), jnp.int32)
    for p in range(n_sub):
        counts = jnp.where((lane & 7) == p, count_ref[0, p], counts)
    used = ((lane >> 3) & 1) < counts

    for f in range(5):
        x_ref[f, 0:125, :] = state_ref[f]
        x_ref[f, 125:128, :] = jnp.ones((3, 128), f32)
    for face in range(6):
        face_ref[face, 125:126, :] = jnp.full((1, 128), float(face // 2), f32)
        face_ref[face, 126:127, :] = metric
        face_ref[face, 127:128, :] = jnp.full((1, 128), 1.0 if face % 2 else -1.0, f32)
    numeric_ref[125:128, :] = jnp.zeros((3, 128), f32)
    passed_ref[125:128, :] = jnp.zeros((3, 128), f32)

    rows = lax.broadcasted_iota(jnp.int32, (16, 128), 0)
    lanes = lax.broadcasted_iota(jnp.int32, (16, 128), 1)

    def marks(slots, target_ref, at):
        column = jnp.full((16, 128), -1, jnp.int32)
        for r, slot in enumerate(slots):
            column = jnp.where(rows == r, slot, column)
        for face in range(6):
            hit = jnp.where(column == lanes + 128 * face, 1.0, 0.0).astype(bf16)
            for row in at:
                target_ref[row : row + 16, 128 * face : 128 * face + 128] = hit

    for b in range(4):
        list_ref = (next_ref, prev_ref)[b // 2]
        marks([list_ref[0, 16 * (b % 2) + i] for i in range(16)], send_pick_ref, [16 * b])
    for p in range(n_sub):
        marks(
            [fine_ref[0, r // 4, r % 4, p] for r in range(8)] + [coarse_ref[0, j, p] for j in range(2)],
            send_pick_ref,
            [64 + 16 * p],
        )

    def onto_planes(target_ref, face, f, value):
        level_at = 4 * (face % 2)
        if face < 2:
            plane = slice(25 * level_at, 25 * level_at + 25)
            target_ref[f, plane, :] = target_ref[f, plane, :] + value
        elif face < 4:
            for a in range(5):
                start = 25 * a + 5 * level_at
                plane = slice(start, start + 5)
                target_ref[f, plane, :] = target_ref[f, plane, :] + value[5 * a : 5 * a + 5, :]
        else:
            plane = pl.ds(level_at, 25, stride=5)
            target_ref[f, plane, :] = target_ref[f, plane, :] + value

    def store_added(product):
        added = both_halves(product)
        for face in range(6):
            added_ref[face] = added[:, 128 * face : 128 * face + 128]

    def panels_of(source):
        coarse_rows = jnp.concatenate([source[:, 8 + j, :] for j in range(2)], axis=0)
        high, low = split(coarse_rows)
        upper = jnp.concatenate([high, high], axis=1)
        lower = jnp.concatenate([low, jnp.zeros_like(low)], axis=1)
        wide = dot(jnp.concatenate([upper, lower], axis=0), panel_ref[...])
        wide = wide[0:16] + wide[16:32]
        return [wide[:, 128 * q : 128 * q + 128] for q in range(4)]

    gain = lift_gain * metric

    def section(step):
        for face in range(6):
            level_at = 4 * (face % 2)
            for f in range(5):
                base = 25 * f
                if face < 2:
                    face_ref[face, base : base + 25, :] = x_ref[f, 25 * level_at : 25 * level_at + 25, :]
                elif face < 4:
                    for a in range(5):
                        start = 25 * a + 5 * level_at
                        face_ref[face, base + 5 * a : base + 5 * a + 5, :] = x_ref[f, start : start + 5, :]
                else:
                    face_ref[face, base : base + 25, :] = x_ref[f, pl.ds(level_at, 25, stride=5), :]
        for face in range(6):
            high, low = split(face_ref[face])
            face_bf_ref[0:128, 128 * face : 128 * face + 128] = high
            face_bf_ref[128:256, 128 * face : 128 * face + 128] = low
        across = (((1,), (1,)), ((), ()))
        packed = lax.dot_general(
            send_pick_ref[...], face_bf_ref[...], across, preferred_element_type=f32
        )
        packed = packed[:, 0:128] + packed[:, 128:256]
        for p in range(n_sub):
            message_send[step, p] = packed[64 + 16 * p : 74 + 16 * p, :]
        for side in range(2):
            ring_send[step, side] = packed[32 * side : 32 * side + 32, :]
        if step == 0:
            pl.semaphore_wait(barrier, n_sub - 1 + (1 - (s + n_sub - 1) // n_sub) + (s + 1) // n_sub)
        messages = []
        for o in (4,):
            copy = pltpu.make_async_remote_copy(
                src_ref=message_send.at[step, peers[o]],
                dst_ref=message_recv.at[step, s],
                send_sem=send_sem.at[step, o],
                recv_sem=recv_sem.at[step, o],
                device_id=(m, peers[o]),
                device_id_type=MESH,
            )
            copy.start()
            messages.append(copy)
        rings = []
        for side, target in enumerate((after_id, before_id)):
            copy = pltpu.make_async_remote_copy(
                src_ref=ring_send.at[step, side],
                dst_ref=ring_recv.at[step, side],
                send_sem=send_sem.at[step, n_sub + side],
                recv_sem=recv_sem.at[step, n_sub + side],
                device_id=target,
                device_id_type=MESH,
            )
            rings.append(copy)
            if step == 0 and side == 1:
                relay = pltpu.make_async_remote_copy(
                    src_ref=ring_send.at[0, 1],
                    dst_ref=relay_ref,
                    send_sem=send_sem.at[0, n_sub + 1],
                    recv_sem=relay_sem.at[0],
                    device_id=(n_morton - 1, 0),
                    device_id_type=MESH,
                )
                pl.when(first_place)(relay.start)
                pl.when(place > 0)(copy.start)
            else:
                copy.start()
        for o in (3, 5, 2, 6, 1, 7):
            copy = pltpu.make_async_remote_copy(
                src_ref=message_send.at[step, peers[o]],
                dst_ref=message_recv.at[step, s],
                send_sem=send_sem.at[step, o],
                recv_sem=recv_sem.at[step, o],
                device_id=(m, peers[o]),
                device_id_type=MESH,
            )
            copy.start()
            messages.append(copy)
        message_recv[step, s] = message_send[step, s]

        if step == 0:
            for load in loads[8:11]:
                load.wait()
        else:
            for face in range(6):
                for f in range(5):
                    onto_planes(rate_ref, face, f, gain * added_ref[face, 25 * f : 25 * f + 25, :])
            for f in range(5):
                first_ref[f] = (section_a2 * step_size) * rate_ref[f]
        fields = [x_ref[f] for f in range(5)]
        inverse, pressure = gas_state(fields)
        for d in range(3):
            components, unused = flux_along(fields, d, inverse, pressure)
            for f in range(5):
                high, low = split(components[f])
                flux_high_ref[128 * d : 128 * d + 128, 128 * f : 128 * f + 128] = high
                flux_low_ref[128 * d : 128 * d + 128, 128 * f : 128 * f + 128] = low
        for f in range(5):
            high, low = split(viscosity * metric * fields[f])
            flux_high_ref[384:512, 128 * f : 128 * f + 128] = high
            flux_low_ref[384:512, 128 * f : 128 * f + 128] = low
        total = both_halves(dot(volume_ref[...], flux_high_ref[...]))
        total = total + dot(volume_ref[0:128, :], flux_low_ref[...])
        for f in range(5):
            rate_ref[f] = metric * total[:, 128 * f : 128 * f + 128]

        if step == 0:
            for face in range(6):
                wanted = entry[face : face + 1, :]
                for block in range(56):
                    pick_ref[16 * block : 16 * block + 16, 128 * face : 128 * face + 128] = jnp.where(
                        rows + 16 * block == wanted, 1.0, 0.0
                    ).astype(bf16)
            spread_ref[0:64, :] = pick_ref[768:832, :]
            spread_ref[128:256, :] = pick_ref[768:896, :]
            owned = [
                jnp.where(j < count_ref[0, p], coarse_ref[0, j, p], -1) for j in range(2) for p in range(n_sub)
            ]
            marks(owned, spread_ref, [64, 80, 96, 112])
        local = both_halves(dot(face_bf_ref[...], pick_ref[0:768, :]))
        for face in range(6):
            outside_ref[face] = local[:, 128 * face : 128 * face + 128]
        inner_ref[...] = both_halves(
            lax.dot_general(face_bf_ref[...], pick_ref[768:896, :], across, preferred_element_type=f32)
        )
        own = jnp.concatenate([jnp.zeros((64, 128), f32)] + panels_of(message_send.at[step]), axis=0).T
        known_ref[...] = jnp.where(low_lanes, inner_ref[...], own)
        inner_facts = [inner_ref[125 + i : 126 + i, :] for i in range(3)]

        for face in range(6):
            d = face // 2
            orient_here = 1.0 if face % 2 else -1.0
            inside = face_fields(face_ref.at[face])
            beyond = face_fields(outside_ref.at[face])
            coupled = (near[face : face + 1, :] >= 0) & (near[face : face + 1, :] < 768)
            inverse, pressure = gas_state(inside)
            flux_in, velocity = flux_along(inside, d, inverse, pressure)
            speed_in = jnp.abs(velocity) + sound_speed(inverse, pressure)
            inverse, pressure = gas_state(beyond)
            flux_out, velocity = flux_along(beyond, d, inverse, pressure)
            speed_out = jnp.abs(velocity) + sound_speed(inverse, pressure)
            damping = 0.5 * jnp.maximum(speed_in, speed_out) + penalty * metric
            for f in range(5):
                value = 0.5 * orient_here * (flux_in[f] + flux_out[f]) + damping * (inside[f] - beyond[f])
                surface = orient_here * flux_in[f] - jnp.where(coupled, value, 0.0)
                onto_planes(rate_ref, face, f, gain * surface)
        if step == 0:
            for f in range(5):
                x_ref[f] = x_ref[f] + (section_b1 * step_size) * rate_ref[f]

        known = face_fields(known_ref)
        known_parts = mortar_part(known)
        inside = face_fields(inner_ref)
        flux_in, speed_in = flux_by_lane(inside, mortar_part(inside), inner_facts[0])
        if step == 0:
            passed_on = pltpu.make_async_remote_copy(
                src_ref=relay_ref,
                dst_ref=ring_recv.at[0, 1],
                send_sem=relay_sem.at[1],
                recv_sem=recv_sem.at[0, n_sub + 1],
                device_id=(m, n_sub - 1),
                device_id_type=MESH,
            )

            @pl.when(relay_place)
            def pass_on():
                relay.wait_recv()
                passed_on.start()

        for copy in rings + messages:
            copy.wait_recv()
        panels = panels_of(message_recv.at[step])
        ring_ref[...] = jnp.concatenate(
            [jnp.zeros((64, 128), f32), ring_recv[step, 0], ring_recv[step, 1]], axis=0
        ).T
        fine_rows = [message_recv[step, :, 4 * j + q, :] for q in range(4) for j in range(2)]
        arrived_ref[...] = jnp.concatenate(panels + fine_rows, axis=0).T
        facts = [
            jnp.where(low_lanes, x, arrived_ref[125 + i : 126 + i, :]) for i, x in enumerate(inner_facts)
        ]
        along, scale, orient = facts
        valid = jnp.where(low_lanes, orient, jnp.where(used, 1.0, 0.0)) != 0.0
        arrived = face_fields(arrived_ref)
        flux_new, speed_new = flux_by_lane(arrived, mortar_part(arrived), along)
        flux_old, speed_old = flux_by_lane(known, known_parts, along)
        damping = 0.5 * jnp.maximum(speed_new, speed_old) + penalty * scale
        damping = jnp.where(low_lanes, -damping, damping)
        for f in range(5):
            value = 0.5 * orient * (flux_new[f] + flux_old[f]) + damping * (arrived[f] - known[f])
            numeric_ref[25 * f : 25 * f + 25, :] = value
        numeric = numeric_ref[...]
        high = numeric.astype(bf16).astype(f32)
        mixed = jnp.where(low_lanes, pltpu.roll(numeric - high, 64, 1), high)
        panel_of = jnp.where(low_lanes, lane, lane - 64) >> 4
        parts = [jnp.where(panel_of == q, mixed, 0.0) for q in range(4)]
        parts = parts + [jnp.where((panel_of == q) & ~low_lanes, high, 0.0) for q in range(4)]
        chosen = dot(gather_ref[...], jnp.concatenate(parts, axis=0).astype(bf16))
        beyond = face_fields(ring_ref)
        along, scale, orient = inner_facts
        flux_out, speed_out = flux_by_lane(beyond, mortar_part(beyond), along)
        damping = 0.5 * jnp.maximum(speed_in, speed_out) + penalty * scale
        for f in range(5):
            value = 0.5 * orient * (flux_in[f] + flux_out[f]) + damping * (inside[f] - beyond[f])
            passed_ref[25 * f : 25 * f + 25, :] = jnp.where(low_lanes, 0.0, -value)
        ready = jnp.where(low_lanes, -numeric, chosen + pltpu.roll(chosen, 64, 1))
        ready = jnp.where(valid, ready, 0.0)
        high, low = split(jnp.concatenate([ready, passed_ref[...]], axis=1))
        store_added(dot(jnp.concatenate([high, low], axis=0), spread_ref[...]))
        if step == 0:
            gain_now = (section_b1 * step_size * lift_gain) * metric
            for face in range(6):
                for f in range(5):
                    onto_planes(x_ref, face, f, gain_now * added_ref[face, 25 * f : 25 * f + 25, :])
        else:
            for face in range(6):
                for f in range(5):
                    onto_planes(rate_ref, face, f, gain * added_ref[face, 25 * f : 25 * f + 25, :])
        if step == 0:
            pl.when(relay_place)(passed_on.wait_send)
        return rings + messages

    copies = section(0)
    copies = copies + section(1)
    for copy in copies:
        copy.wait_send()


def finish(x_ref, first_ref, rate_ref, out_hbm, register_hbm, out_ref, register_ref, sem):
    copies = []
    for f in range(5):
        register = first_ref[f, 0:125, :] + step_size * rate_ref[f, 0:125, :]
        register_ref[f] = register
        out_ref[f] = x_ref[f, 0:125, :] + section_b2 * register
        copies.append(pltpu.make_async_copy(register_ref.at[f], register_hbm.at[f], sem.at[0, f]))
        copies.append(pltpu.make_async_copy(out_ref.at[f], out_hbm.at[f], sem.at[1, f]))
        for copy in copies[-2:]:
            copy.start()
    for copy in copies:
        copy.wait()


def per_device(mesh_shape, flow_state, element_level, neighbour, send_next, send_prev, coarse_face, fine_face, send_count):
    n_morton, n_sub = mesh_shape
    volume, panel, gather = (jnp.asarray(t) for t in operator_tables())
    vmem = pl.BlockSpec(memory_space=pltpu.VMEM)
    hbm = pl.BlockSpec(memory_space=pltpu.HBM)
    shape = jax.ShapeDtypeStruct(flow_state.shape, f32)
    block = jax.ShapeDtypeStruct((5, 128, 128), f32)
    operands = (
        flow_state,
        element_level.reshape(1, -1),
        neighbour,
        send_next,
        send_prev,
        jnp.transpose(coarse_face, (0, 2, 1)),
        jnp.transpose(fine_face, (0, 2, 3, 1)),
        send_count,
        volume,
        panel,
        gather,
    )
    spaces = [pltpu.VMEM] * 3 + [pltpu.SMEM] * 5 + [pltpu.VMEM] * 3
    pieces = pl.pallas_call(
        functools.partial(kernel, n_morton, n_sub),
        out_shape=(block, block, block),
        in_specs=[hbm] * len(operands),
        out_specs=(vmem, vmem, vmem),
        scratch_shapes=[space(x.shape, x.dtype) for space, x in zip(spaces, operands)]
        + [
            pltpu.SemaphoreType.DMA((len(operands),)),
            pltpu.VMEM((6, 128, 128), f32),
            pltpu.VMEM((256, 768), bf16),
            pltpu.VMEM((896, 768), bf16),
            pltpu.VMEM((256, 768), bf16),
            pltpu.VMEM((192, 768), bf16),
            pltpu.VMEM((6, 128, 128), f32),
            pltpu.VMEM((6, 128, 128), f32),
            pltpu.VMEM((512, 640), bf16),
            pltpu.VMEM((512, 640), bf16),
            pltpu.VMEM((128, 128), f32),
            pltpu.VMEM((128, 128), f32),
            pltpu.VMEM((128, 128), f32),
            pltpu.VMEM((128, 128), f32),
            pltpu.VMEM((128, 128), f32),
            pltpu.VMEM((128, 128), f32),
            pltpu.VMEM((2, 2, 32, 128), f32),
            pltpu.VMEM((2, 2, 32, 128), f32),
            pltpu.VMEM((2, n_sub, 10, 128), f32),
            pltpu.VMEM((2, n_sub, 10, 128), f32),
            pltpu.VMEM((32, 128), f32),
            pltpu.SemaphoreType.DMA((2,)),
            pltpu.SemaphoreType.DMA((2, n_sub + 2)),
            pltpu.SemaphoreType.DMA((2, n_sub + 2)),
        ],
        compiler_params=pltpu.CompilerParams(
            collective_id=0, has_side_effects=True, vmem_limit_bytes=40 * 1024 * 1024
        ),
    )(*[pltpu.with_memory_space_constraint(x, pltpu.HBM) for x in operands])
    return pl.pallas_call(
        finish,
        out_shape=(shape, shape),
        in_specs=[vmem, vmem, vmem],
        out_specs=(hbm, hbm),
        scratch_shapes=[
            pltpu.VMEM(flow_state.shape, f32),
            pltpu.VMEM(flow_state.shape, f32),
            pltpu.SemaphoreType.DMA((2, 5)),
        ],
        compiler_params=pltpu.CompilerParams(vmem_limit_bytes=16 * 1024 * 1024),
    )(*pieces)


def solution(mesh):
    whole = ("morton", "sub")
    placed = (
        P(None, None, whole),
        P(whole),
        P(None, whole),
        P(whole, None),
        P(whole, None),
        P(whole, None, None),
        P(whole, None, None, None),
        P(whole, None),
    )
    mesh_shape = (mesh.shape["morton"], mesh.shape["sub"])
    return jax.shard_map(
        functools.partial(per_device, mesh_shape),
        mesh=mesh,
        in_specs=placed,
        out_specs=(P(None, None, whole), P(None, None, whole)),
        check_vma=False,
    )
```

```python
import functools

import jax
import jax.numpy as jnp
import numpy as np
from jax import lax
from jax.experimental import pallas as pl
from jax.experimental.pallas import tpu as pltpu
from jax.sharding import PartitionSpec as P

gamma_gas = 1.4
viscosity = 0.01
penalty = 0.1
lift_gain = 10.0
step_size = 0.05
section_a2 = -0.4178904745
section_b1 = 0.1496590219993
section_b2 = 0.3792103129999
MESH = pl.DeviceIdType.MESH
f32 = jnp.float32
bf16 = jnp.bfloat16


def basis_tables():
    points = np.array([-1.0, -np.sqrt(3.0 / 7.0), 0.0, np.sqrt(3.0 / 7.0), 1.0])
    weights = np.array([0.1, 49.0 / 90.0, 32.0 / 45.0, 49.0 / 90.0, 0.1])
    products = np.array(
        [np.prod([points[i] - points[m] for m in range(5) if m != i]) for i in range(5)]
    )
    derivative = np.zeros((5, 5))
    for i in range(5):
        for j in range(5):
            if i != j:
                derivative[i, j] = products[i] / (products[j] * (points[i] - points[j]))
        derivative[i, i] = -np.sum(derivative[i])
    halves = []
    projections = []
    for h in range(2):
        shifted = (points + 2.0 * h - 1.0) / 2.0
        interp = np.zeros((5, 5))
        for i in range(5):
            for j in range(5):
                interp[i, j] = np.prod(
                    [(shifted[i] - points[m]) / (points[j] - points[m]) for m in range(5) if m != j]
                )
        halves.append(interp)
        projections.append(weights[None, :] * interp.T / (2.0 * weights[:, None]))
    interpolation = np.stack([np.kron(halves[q // 2], halves[q % 2]) for q in range(4)])
    projection = np.stack([np.kron(projections[q // 2], projections[q % 2]) for q in range(4)])
    ident_five = np.eye(5)
    ident_quad = np.eye(25)
    gradients = np.stack(
        [
            np.kron(derivative, ident_quad),
            np.kron(ident_five, np.kron(derivative, ident_five)),
            np.kron(ident_quad, derivative),
        ]
    )
    laplace = (
        gradients[0] @ gradients[0] + gradients[1] @ gradients[1] + gradients[2] @ gradients[2]
    )
    return interpolation, projection, gradients, laplace


def two_parts(table):
    table = table.astype(np.float32)
    high = table.astype(jnp.bfloat16)
    low = (table - high.astype(np.float32)).astype(jnp.bfloat16)
    return np.stack([high, low])


def operator_tables():
    interpolation, projection, gradients, laplace = basis_tables()
    volume = np.zeros((128, 512))
    for d in range(3):
        volume[:125, 128 * d : 128 * d + 125] = -gradients[d]
    volume[:125, 384:509] = laplace
    panel = np.zeros((128, 512))
    gather = np.zeros((512, 128))
    for q in range(4):
        for f in range(5):
            rows = slice(25 * f, 25 * f + 25)
            columns = slice(128 * q + 25 * f, 128 * q + 25 * f + 25)
            panel[rows, columns] = interpolation[q].T
            gather[columns, rows] = projection[q]
    beside = two_parts(gather).reshape(8, 128, 128).transpose(1, 0, 2).reshape(128, 1024)
    return two_parts(volume).reshape(256, 512), two_parts(panel).reshape(256, 512), beside


def split(x):
    high = x.astype(bf16)
    low = (x - high.astype(f32)).astype(bf16)
    return high, low


def dot(a, b):
    return jnp.dot(a, b, preferred_element_type=f32)


def gas_state(fields):
    inverse = 1.0 / fields[0]
    kinetic = fields[1] * fields[1] + fields[2] * fields[2] + fields[3] * fields[3]
    pressure = (gamma_gas - 1.0) * (fields[4] - 0.5 * kinetic * inverse)
    return inverse, pressure


def flux_along(fields, d, inverse, pressure):
    velocity = fields[1 + d] * inverse
    components = [
        fields[1 + d],
        fields[1] * velocity,
        fields[2] * velocity,
        fields[3] * velocity,
        (fields[4] + pressure) * velocity,
    ]
    components[1 + d] = components[1 + d] + pressure
    return components, velocity


def sound_speed(inverse, pressure):
    return jnp.sqrt(gamma_gas * pressure * inverse)


def mortar_part(fields):
    inverse, pressure = gas_state(fields)
    return inverse, pressure, sound_speed(inverse, pressure)


def flux_by_lane(fields, parts, along):
    inverse, pressure, sound = parts
    normal = jnp.where(along < 0.5, fields[1], jnp.where(along < 1.5, fields[2], fields[3]))
    velocity = normal * inverse
    components = [
        normal,
        fields[1] * velocity + jnp.where(along < 0.5, pressure, 0.0),
        fields[2] * velocity + jnp.where((along > 0.5) & (along < 1.5), pressure, 0.0),
        fields[3] * velocity + jnp.where(along > 1.5, pressure, 0.0),
        (fields[4] + pressure) * velocity,
    ]
    return components, jnp.abs(velocity) + sound


def face_fields(ref):
    return [ref[25 * f : 25 * f + 25, :] for f in range(5)]


def both_halves(x):
    return x[0:128] + x[128:256]


def kernel(
    n_morton,
    n_sub,
    state_hbm,
    level_hbm,
    near_hbm,
    next_hbm,
    prev_hbm,
    coarse_hbm,
    fine_hbm,
    count_hbm,
    volume_hbm,
    panel_hbm,
    gather_hbm,
    x_ref,
    first_ref,
    rate_ref,
    state_ref,
    level_ref,
    near_ref,
    next_ref,
    prev_ref,
    coarse_ref,
    fine_ref,
    count_ref,
    volume_ref,
    panel_ref,
    gather_ref,
    load_sem,
    face_ref,
    face_bf_ref,
    pick_ref,
    spread_ref,
    send_pick_ref,
    outside_ref,
    added_ref,
    flux_high_ref,
    flux_low_ref,
    inner_ref,
    ring_ref,
    known_ref,
    arrived_ref,
    numeric_ref,
    passed_ref,
    ring_send,
    ring_recv,
    message_send,
    message_recv,
    relay_ref,
    relay_sem,
    send_sem,
    recv_sem,
):
    m = lax.axis_index("morton")
    s = lax.axis_index("sub")
    devices = n_morton * n_sub
    place = m * n_sub + s
    after = lax.rem(place + 1, devices)
    before = lax.rem(place + devices - 1, devices)
    after_id = (after // n_sub, lax.rem(after, n_sub))
    before_id = (before // n_sub, lax.rem(before, n_sub))
    peers = [lax.rem(s + o, n_sub) for o in range(n_sub)]

    barrier = pltpu.get_barrier_semaphore()
    for o in (4, 3, 5, 2, 6, 1, 7):
        pl.semaphore_signal(barrier, inc=1, device_id=(m, peers[o]), device_id_type=MESH)
    first_place = place == 0
    relay_place = place == devices - n_sub

    @pl.when(s == 0)
    def greet_before():
        pl.semaphore_signal(barrier, inc=1, device_id=before_id, device_id_type=MESH)

    @pl.when((s == n_sub - 1) & (place < devices - 1))
    def greet_after():
        pl.semaphore_signal(barrier, inc=1, device_id=after_id, device_id_type=MESH)

    @pl.when(relay_place)
    def greet_first():
        pl.semaphore_signal(barrier, inc=1, device_id=(0, 0), device_id_type=MESH)

    loads = [
        pltpu.make_async_copy(source, target, load_sem.at[i])
        for i, (source, target) in enumerate(
            (
                (state_hbm, state_ref),
                (level_hbm, level_ref),
                (fine_hbm, fine_ref),
                (coarse_hbm, coarse_ref),
                (next_hbm, next_ref),
                (prev_hbm, prev_ref),
                (near_hbm, near_ref),
                (count_hbm, count_ref),
                (volume_hbm, volume_ref),
                (panel_hbm, panel_ref),
                (gather_hbm, gather_ref),
            )
        )
    ]
    for load in loads:
        load.start()
    for load in loads[0:8]:
        load.wait()

    level = level_ref[...]
    metric = 0.25 * jnp.left_shift(jnp.ones_like(level), level).astype(f32)
    near = near_ref[...]
    extra = near - 832
    panel_lane = 768 + (extra & 3) * 16 + ((extra >> 2) & 1) * 8 + (extra >> 3)
    entry = jnp.where(near >= 832, panel_lane, jnp.where(near >= 768, near + 64, near))
    lane = lax.broadcasted_iota(jnp.int32, (1, 128), 1)
    low_lanes = lane < 64
    counts = jnp.zeros((1, 128), jnp.int32)
    for p in range(n_sub):
        counts = jnp.where((lane & 7) == p, count_ref[0, p], counts)
    used = ((lane >> 3) & 1) < counts

    for f in range(5):
        x_ref[f, 0:125, :] = state_ref[f]
        x_ref[f, 125:128, :] = jnp.ones((3, 128), f32)
    for face in range(6):
        face_ref[face, 125:126, :] = jnp.full((1, 128), float(face // 2), f32)
        face_ref[face, 126:127, :] = metric
        face_ref[face, 127:128, :] = jnp.full((1, 128), 1.0 if face % 2 else -1.0, f32)
    numeric_ref[125:128, :] = jnp.zeros((3, 128), f32)
    passed_ref[125:128, :] = jnp.zeros((3, 128), f32)

    rows = lax.broadcasted_iota(jnp.int32, (16, 128), 0)
    lanes = lax.broadcasted_iota(jnp.int32, (16, 128), 1)

    def marks(slots, target_ref, at):
        column = jnp.full((16, 128), -1, jnp.int32)
        for r, slot in enumerate(slots):
            column = jnp.where(rows == r, slot, column)
        for face in range(6):
            hit = jnp.where(column == lanes + 128 * face, 1.0, 0.0).astype(bf16)
            for row in at:
                target_ref[row : row + 16, 128 * face : 128 * face + 128] = hit

    for b in range(4):
        list_ref = (next_ref, prev_ref)[b // 2]
        marks([list_ref[0, 16 * (b % 2) + i] for i in range(16)], send_pick_ref, [16 * b])
    for p in range(n_sub):
        marks(
            [fine_ref[0, r // 4, r % 4, p] for r in range(8)] + [coarse_ref[0, j, p] for j in range(2)],
            send_pick_ref,
            [64 + 16 * p],
        )

    def onto_planes(target_ref, face, f, value):
        level_at = 4 * (face % 2)
        if face < 2:
            plane = slice(25 * level_at, 25 * level_at + 25)
            target_ref[f, plane, :] = target_ref[f, plane, :] + value
        elif face < 4:
            for a in range(5):
                start = 25 * a + 5 * level_at
                plane = slice(start, start + 5)
                target_ref[f, plane, :] = target_ref[f, plane, :] + value[5 * a : 5 * a + 5, :]
        else:
            plane = pl.ds(level_at, 25, stride=5)
            target_ref[f, plane, :] = target_ref[f, plane, :] + value

    def store_added(product):
        added = both_halves(product)
        for face in range(6):
            added_ref[face] = added[:, 128 * face : 128 * face + 128]

    def panels_of(source):
        coarse_rows = jnp.concatenate([source[:, 8 + j, :] for j in range(2)], axis=0)
        high, low = split(coarse_rows)
        upper = jnp.concatenate([high, high], axis=1)
        lower = jnp.concatenate([low, jnp.zeros_like(low)], axis=1)
        wide = dot(jnp.concatenate([upper, lower], axis=0), panel_ref[...])
        wide = wide[0:16] + wide[16:32]
        return [wide[:, 128 * q : 128 * q + 128] for q in range(4)]

    gain = lift_gain * metric

    def section(step):
        for face in range(6):
            level_at = 4 * (face % 2)
            for f in range(5):
                base = 25 * f
                if face < 2:
                    face_ref[face, base : base + 25, :] = x_ref[f, 25 * level_at : 25 * level_at + 25, :]
                elif face < 4:
                    for a in range(5):
                        start = 25 * a + 5 * level_at
                        face_ref[face, base + 5 * a : base + 5 * a + 5, :] = x_ref[f, start : start + 5, :]
                else:
                    face_ref[face, base : base + 25, :] = x_ref[f, pl.ds(level_at, 25, stride=5), :]
        for face in range(6):
            high, low = split(face_ref[face])
            face_bf_ref[0:128, 128 * face : 128 * face + 128] = high
            face_bf_ref[128:256, 128 * face : 128 * face + 128] = low
        across = (((1,), (1,)), ((), ()))
        packed = lax.dot_general(
            send_pick_ref[...], face_bf_ref[...], across, preferred_element_type=f32
        )
        packed = packed[:, 0:128] + packed[:, 128:256]
        for side in range(2):
            ring_send[step, side] = packed[32 * side : 32 * side + 32, :]
        if step == 0:
            pl.semaphore_wait(barrier, n_sub - 1 + (1 - (s + n_sub - 1) // n_sub) + (s + 1) // n_sub)
        rings = []
        for side, target in enumerate((after_id, before_id)):
            copy = pltpu.make_async_remote_copy(
                src_ref=ring_send.at[step, side],
                dst_ref=ring_recv.at[step, side],
                send_sem=send_sem.at[step, n_sub + side],
                recv_sem=recv_sem.at[step, n_sub + side],
                device_id=target,
                device_id_type=MESH,
            )
            rings.append(copy)
            if step == 0 and side == 1:
                relay = pltpu.make_async_remote_copy(
                    src_ref=ring_send.at[0, 1],
                    dst_ref=relay_ref,
                    send_sem=send_sem.at[0, n_sub + 1],
                    recv_sem=relay_sem.at[0],
                    device_id=(n_morton - 1, 0),
                    device_id_type=MESH,
                )
                pl.when(first_place)(relay.start)
                pl.when(place > 0)(copy.start)
            else:
                copy.start()
        for p in range(n_sub):
            message_send[step, p] = packed[64 + 16 * p : 74 + 16 * p, :]
        messages = []
        for o in (4,):
            copy = pltpu.make_async_remote_copy(
                src_ref=message_send.at[step, peers[o]],
                dst_ref=message_recv.at[step, s],
                send_sem=send_sem.at[step, o],
                recv_sem=recv_sem.at[step, o],
                device_id=(m, peers[o]),
                device_id_type=MESH,
            )
            copy.start()
            messages.append(copy)
        for o in (3, 5, 2, 6, 1, 7):
            copy = pltpu.make_async_remote_copy(
                src_ref=message_send.at[step, peers[o]],
                dst_ref=message_recv.at[step, s],
                send_sem=send_sem.at[step, o],
                recv_sem=recv_sem.at[step, o],
                device_id=(m, peers[o]),
                device_id_type=MESH,
            )
            copy.start()
            messages.append(copy)
        message_recv[step, s] = message_send[step, s]

        if step == 0:
            for load in loads[8:11]:
                load.wait()
        else:
            for face in range(6):
                for f in range(5):
                    onto_planes(rate_ref, face, f, gain * added_ref[face, 25 * f : 25 * f + 25, :])
            for f in range(5):
                first_ref[f] = (section_a2 * step_size) * rate_ref[f]
        fields = [x_ref[f] for f in range(5)]
        inverse, pressure = gas_state(fields)
        for d in range(3):
            components, unused = flux_along(fields, d, inverse, pressure)
            for f in range(5):
                high, low = split(components[f])
                flux_high_ref[128 * d : 128 * d + 128, 128 * f : 128 * f + 128] = high
                flux_low_ref[128 * d : 128 * d + 128, 128 * f : 128 * f + 128] = low
        for f in range(5):
            high, low = split(viscosity * metric * fields[f])
            flux_high_ref[384:512, 128 * f : 128 * f + 128] = high
            flux_low_ref[384:512, 128 * f : 128 * f + 128] = low
        total = both_halves(dot(volume_ref[...], flux_high_ref[...]))
        total = total + dot(volume_ref[0:128, :], flux_low_ref[...])
        for f in range(5):
            rate_ref[f] = metric * total[:, 128 * f : 128 * f + 128]

        if step == 0:
            for face in range(6):
                wanted = entry[face : face + 1, :]
                for block in range(56):
                    pick_ref[16 * block : 16 * block + 16, 128 * face : 128 * face + 128] = jnp.where(
                        rows + 16 * block == wanted, 1.0, 0.0
                    ).astype(bf16)
            spread_ref[0:64, :] = pick_ref[768:832, :]
            spread_ref[128:256, :] = pick_ref[768:896, :]
            owned = [
                jnp.where(j < count_ref[0, p], coarse_ref[0, j, p], -1) for j in range(2) for p in range(n_sub)
            ]
            marks(owned, spread_ref, [64, 80, 96, 112])
        local = both_halves(dot(face_bf_ref[...], pick_ref[0:768, :]))
        for face in range(6):
            outside_ref[face] = local[:, 128 * face : 128 * face + 128]
        inner_ref[...] = both_halves(
            lax.dot_general(face_bf_ref[...], pick_ref[768:896, :], across, preferred_element_type=f32)
        )
        own = jnp.concatenate([jnp.zeros((64, 128), f32)] + panels_of(message_send.at[step]), axis=0).T
        known_ref[...] = jnp.where(low_lanes, inner_ref[...], own)
        inner_facts = [inner_ref[125 + i : 126 + i, :] for i in range(3)]

        for face in range(6):
            d = face // 2
            orient_here = 1.0 if face % 2 else -1.0
            inside = face_fields(face_ref.at[face])
            beyond = face_fields(outside_ref.at[face])
            coupled = (near[face : face + 1, :] >= 0) & (near[face : face + 1, :] < 768)
            inverse, pressure = gas_state(inside)
            flux_in, velocity = flux_along(inside, d, inverse, pressure)
            speed_in = jnp.abs(velocity) + sound_speed(inverse, pressure)
            inverse, pressure = gas_state(beyond)
            flux_out, velocity = flux_along(beyond, d, inverse, pressure)
            speed_out = jnp.abs(velocity) + sound_speed(inverse, pressure)
            damping = 0.5 * jnp.maximum(speed_in, speed_out) + penalty * metric
            for f in range(5):
                value = 0.5 * orient_here * (flux_in[f] + flux_out[f]) + damping * (inside[f] - beyond[f])
                surface = orient_here * flux_in[f] - jnp.where(coupled, value, 0.0)
                onto_planes(rate_ref, face, f, gain * surface)
        if step == 0:
            for f in range(5):
                x_ref[f] = x_ref[f] + (section_b1 * step_size) * rate_ref[f]

        known = face_fields(known_ref)
        known_parts = mortar_part(known)
        inside = face_fields(inner_ref)
        flux_in, speed_in = flux_by_lane(inside, mortar_part(inside), inner_facts[0])
        if step == 0:
            passed_on = pltpu.make_async_remote_copy(
                src_ref=relay_ref,
                dst_ref=ring_recv.at[0, 1],
                send_sem=relay_sem.at[1],
                recv_sem=recv_sem.at[0, n_sub + 1],
                device_id=(m, n_sub - 1),
                device_id_type=MESH,
            )

            @pl.when(relay_place)
            def pass_on():
                relay.wait_recv()
                passed_on.start()

        for copy in rings + messages:
            copy.wait_recv()
        panels = panels_of(message_recv.at[step])
        ring_ref[...] = jnp.concatenate(
            [jnp.zeros((64, 128), f32), ring_recv[step, 0], ring_recv[step, 1]], axis=0
        ).T
        fine_rows = [message_recv[step, :, 4 * j + q, :] for q in range(4) for j in range(2)]
        arrived_ref[...] = jnp.concatenate(panels + fine_rows, axis=0).T
        facts = [
            jnp.where(low_lanes, x, arrived_ref[125 + i : 126 + i, :]) for i, x in enumerate(inner_facts)
        ]
        along, scale, orient = facts
        valid = jnp.where(low_lanes, orient, jnp.where(used, 1.0, 0.0)) != 0.0
        arrived = face_fields(arrived_ref)
        flux_new, speed_new = flux_by_lane(arrived, mortar_part(arrived), along)
        flux_old, speed_old = flux_by_lane(known, known_parts, along)
        damping = 0.5 * jnp.maximum(speed_new, speed_old) + penalty * scale
        damping = jnp.where(low_lanes, -damping, damping)
        for f in range(5):
            value = 0.5 * orient * (flux_new[f] + flux_old[f]) + damping * (arrived[f] - known[f])
            numeric_ref[25 * f : 25 * f + 25, :] = value
        numeric = numeric_ref[...]
        high = numeric.astype(bf16).astype(f32)
        mixed = jnp.where(low_lanes, pltpu.roll(numeric - high, 64, 1), high)
        panel_of = jnp.where(low_lanes, lane, lane - 64) >> 4
        parts = [jnp.where(panel_of == q, mixed, 0.0) for q in range(4)]
        parts = parts + [jnp.where((panel_of == q) & ~low_lanes, high, 0.0) for q in range(4)]
        chosen = dot(gather_ref[...], jnp.concatenate(parts, axis=0).astype(bf16))
        beyond = face_fields(ring_ref)
        along, scale, orient = inner_facts
        flux_out, speed_out = flux_by_lane(beyond, mortar_part(beyond), along)
        damping = 0.5 * jnp.maximum(speed_in, speed_out) + penalty * scale
        for f in range(5):
            value = 0.5 * orient * (flux_in[f] + flux_out[f]) + damping * (inside[f] - beyond[f])
            passed_ref[25 * f : 25 * f + 25, :] = jnp.where(low_lanes, 0.0, -value)
        ready = jnp.where(low_lanes, -numeric, chosen + pltpu.roll(chosen, 64, 1))
        ready = jnp.where(valid, ready, 0.0)
        high, low = split(jnp.concatenate([ready, passed_ref[...]], axis=1))
        store_added(dot(jnp.concatenate([high, low], axis=0), spread_ref[...]))
        if step == 0:
            gain_now = (section_b1 * step_size * lift_gain) * metric
            for face in range(6):
                for f in range(5):
                    onto_planes(x_ref, face, f, gain_now * added_ref[face, 25 * f : 25 * f + 25, :])
        else:
            for face in range(6):
                for f in range(5):
                    onto_planes(rate_ref, face, f, gain * added_ref[face, 25 * f : 25 * f + 25, :])
        if step == 0:
            pl.when(relay_place)(passed_on.wait_send)
        return rings + messages

    copies = section(0)
    copies = copies + section(1)
    for copy in copies:
        copy.wait_send()


def finish(x_ref, first_ref, rate_ref, out_hbm, register_hbm, out_ref, register_ref, sem):
    copies = []
    for f in range(5):
        register = first_ref[f, 0:125, :] + step_size * rate_ref[f, 0:125, :]
        register_ref[f] = register
        out_ref[f] = x_ref[f, 0:125, :] + section_b2 * register
        copies.append(pltpu.make_async_copy(register_ref.at[f], register_hbm.at[f], sem.at[0, f]))
        copies.append(pltpu.make_async_copy(out_ref.at[f], out_hbm.at[f], sem.at[1, f]))
        for copy in copies[-2:]:
            copy.start()
    for copy in copies:
        copy.wait()


def per_device(mesh_shape, flow_state, element_level, neighbour, send_next, send_prev, coarse_face, fine_face, send_count):
    n_morton, n_sub = mesh_shape
    volume, panel, gather = (jnp.asarray(t) for t in operator_tables())
    vmem = pl.BlockSpec(memory_space=pltpu.VMEM)
    hbm = pl.BlockSpec(memory_space=pltpu.HBM)
    shape = jax.ShapeDtypeStruct(flow_state.shape, f32)
    block = jax.ShapeDtypeStruct((5, 128, 128), f32)
    operands = (
        flow_state,
        element_level.reshape(1, -1),
        neighbour,
        send_next,
        send_prev,
        jnp.transpose(coarse_face, (0, 2, 1)),
        jnp.transpose(fine_face, (0, 2, 3, 1)),
        send_count,
        volume,
        panel,
        gather,
    )
    spaces = [pltpu.VMEM] * 3 + [pltpu.SMEM] * 5 + [pltpu.VMEM] * 3
    pieces = pl.pallas_call(
        functools.partial(kernel, n_morton, n_sub),
        out_shape=(block, block, block),
        in_specs=[hbm] * len(operands),
        out_specs=(vmem, vmem, vmem),
        scratch_shapes=[space(x.shape, x.dtype) for space, x in zip(spaces, operands)]
        + [
            pltpu.SemaphoreType.DMA((len(operands),)),
            pltpu.VMEM((6, 128, 128), f32),
            pltpu.VMEM((256, 768), bf16),
            pltpu.VMEM((896, 768), bf16),
            pltpu.VMEM((256, 768), bf16),
            pltpu.VMEM((192, 768), bf16),
            pltpu.VMEM((6, 128, 128), f32),
            pltpu.VMEM((6, 128, 128), f32),
            pltpu.VMEM((512, 640), bf16),
            pltpu.VMEM((512, 640), bf16),
            pltpu.VMEM((128, 128), f32),
            pltpu.VMEM((128, 128), f32),
            pltpu.VMEM((128, 128), f32),
            pltpu.VMEM((128, 128), f32),
            pltpu.VMEM((128, 128), f32),
            pltpu.VMEM((128, 128), f32),
            pltpu.VMEM((2, 2, 32, 128), f32),
            pltpu.VMEM((2, 2, 32, 128), f32),
            pltpu.VMEM((2, n_sub, 10, 128), f32),
            pltpu.VMEM((2, n_sub, 10, 128), f32),
            pltpu.VMEM((32, 128), f32),
            pltpu.SemaphoreType.DMA((2,)),
            pltpu.SemaphoreType.DMA((2, n_sub + 2)),
            pltpu.SemaphoreType.DMA((2, n_sub + 2)),
        ],
        compiler_params=pltpu.CompilerParams(
            collective_id=0, has_side_effects=True, vmem_limit_bytes=40 * 1024 * 1024
        ),
    )(*[pltpu.with_memory_space_constraint(x, pltpu.HBM) for x in operands])
    return pl.pallas_call(
        finish,
        out_shape=(shape, shape),
        in_specs=[vmem, vmem, vmem],
        out_specs=(hbm, hbm),
        scratch_shapes=[
            pltpu.VMEM(flow_state.shape, f32),
            pltpu.VMEM(flow_state.shape, f32),
            pltpu.SemaphoreType.DMA((2, 5)),
        ],
        compiler_params=pltpu.CompilerParams(vmem_limit_bytes=16 * 1024 * 1024),
    )(*pieces)


def solution(mesh):
    whole = ("morton", "sub")
    placed = (
        P(None, None, whole),
        P(whole),
        P(None, whole),
        P(whole, None),
        P(whole, None),
        P(whole, None, None),
        P(whole, None, None, None),
        P(whole, None),
    )
    mesh_shape = (mesh.shape["morton"], mesh.shape["sub"])
    return jax.shard_map(
        functools.partial(per_device, mesh_shape),
        mesh=mesh,
        in_specs=placed,
        out_specs=(P(None, None, whole), P(None, None, whole)),
        check_vma=False,
    )
```
